32 devices in a mesh: strike: 8 (over z, y), depth: 4 (over x, core).
Axes of the slice: x: 2, y: 2, z: 4, core: 2. Of those that a mesh axis runs over, the one named last changes fastest.
Arguments:
- velocity: float32 [3, 128, 64, 256], P(None, 'strike', 'depth'), may hold values from -6 to 6
- stress: float32 [6, 128, 64, 256], P(None, 'strike', 'depth'), may hold values from -6 to 6
- material: int32 [128, 64, 256], P('strike', 'depth'), may hold values from 0 to 3
- patch_order: int32 [48], replicated, may hold values from 0 to 47, each once
- fault_params: float32 [4, 64, 48], P(None, 'depth', 'strike'), may hold values from -5 to 5, as said below
Outputs:
- velocity_out: float32 [3, 128, 64, 256], P(None, 'strike', 'depth')
- slip_rate: float32 [64, 48], P('depth', 'strike')
The draws below stay inside these ranges and needn't reach their ends.
Inputs may be any that keep to these rules, and one draw needn't show every extreme that they name: `fault_params`: row 0 in 0.3 to 1.2, row 1 in -0.5 to 1.5, row 2 in 1 to 3, row 3 in -5 to 5. `patch_order`: each fault column exactly once.
All inputs are finite; a program needn't handle non-finite values.
Results may differ from the reference program's by a relative error of at most 0.0003.
Values sent between devices are 32-bit elements; how exact they have to be, the bound alone decides.
A program may use at most 64 MiB of HBM per device.

```python
import jax
import jax.numpy as jnp
from jax import lax

NY = 256
NEWTON = 8
NX = 128
NZ = 64
FAULT_ROW = 128
FAULT_START = 32
FAULT_COLS = 48


def draw_fault_params(key, part):
    keys = jax.random.split(jax.random.fold_in(key, 17), 4)
    shape = (NZ, FAULT_COLS)
    coef = jnp.exp(jax.random.uniform(keys[0], shape, jnp.float32, jnp.log(0.3), jnp.log(1.2)))
    psi = jax.random.uniform(keys[1], shape, jnp.float32, -0.5, 1.5)
    normal_stress = jax.random.uniform(keys[2], shape, jnp.float32, 1.0, 3.0)
    background = jnp.clip(1.5 * jax.random.normal(keys[3], shape, jnp.float32), -5.0, 5.0)
    return jnp.stack([coef, psi, normal_stress, background]).astype(jnp.float32)


def touch_ends(drawn, own_key, low, top_value):
    dims = drawn.shape
    index_at = [jax.random.randint(jax.random.fold_in(own_key, axis), (), 0, dims[axis]) for axis in range(len(dims))]
    drawn = drawn.at[tuple(index_at)].set(low)
    longest = dims.index(max(dims))
    index_at[longest] = (index_at[longest] + 1) % dims[longest]
    return drawn.at[tuple(index_at)].set(top_value)


def steps_of(rng, dims, cuts, least, top_value):
    gain = 1.0
    for dim, blocks in cuts:
        heights = jax.random.uniform(jax.random.fold_in(jax.random.fold_in(rng, 6), dim), (blocks,), jnp.float32, least / len(cuts), top_value / len(cuts))
        gain = gain * jnp.repeat(jnp.exp(heights), dims[dim] // blocks).reshape((-1,) + (1,) * (len(dims) - 1 - dim))
    return gain


def normal_values(own_key, extent, deviation, bound, cuts=(), held_as=jnp.bfloat16):
    gain = steps_of(own_key, extent, cuts, -0.22, 0.18) if cuts else 1.0
    array = jax.random.normal(own_key, extent, jnp.float32) * deviation * gain
    return jnp.minimum(jnp.maximum(array, -bound), bound).astype(held_as)


def setup_inputs(seed: int = 0) -> dict:
    key_list = jax.random.split(jax.random.key(seed), 6)
    return {
        "velocity": normal_values(key_list[0], (3, NX, NZ, NY), 1.0, 6.0, ((1, 8), (2, 4)), jnp.float32),
        "stress": normal_values(key_list[1], (6, NX, NZ, NY), 1.0, 6.0, ((1, 8), (2, 4)), jnp.float32),
        "material": touch_ends(jax.random.randint(key_list[2], (NX, NZ, NY), 0, 4), jax.random.fold_in(key_list[2], 1), 0, 3).astype(jnp.int32),
        "patch_order": jax.random.permutation(key_list[3], FAULT_COLS).astype(jnp.int32),
        "fault_params": draw_fault_params(jax.random.fold_in(key_list[5], 71), 0),
    }


BUOY = (1.0, 0.8, 0.6, 1.25)
C_ONE = 9.0 / 8.0
C_TWO = -1.0 / 24.0

def inverse_sinh(value):
    magnitude = jnp.log(jnp.abs(value) + jnp.sqrt(1.0 + value * value))
    return jnp.where(value < 0, -magnitude, magnitude)

def shifted(field, axis, width):
    pads = [(0, 0)] * field.ndim
    pads[axis] = (2, 2)
    padded = jnp.pad(field, pads)

    def part(offset):
        return lax.slice_in_dim(padded, 2 + offset, 2 + offset + width, axis=axis)
    return part

def minus_diff(field, axis):
    part = shifted(field, axis, field.shape[axis])
    return C_ONE * (part(0) - part(-1)) + C_TWO * (part(1) - part(-2))

def plus_diff(field, axis):
    part = shifted(field, axis, field.shape[axis])
    return C_ONE * (part(1) - part(0)) + C_TWO * (part(2) - part(-1))

def friction(tau_trial, params):
    coef, psi, normal_stress, background = (params[0], params[1], params[2], params[3])
    tau_total = tau_trial + background
    half_q = 0.5 * jnp.exp(psi / coef)
    scale = normal_stress * coef
    rate = jnp.zeros_like(tau_total)
    for step in range(NEWTON):
        arg_val = rate * half_q
        resid = tau_total - rate - scale * inverse_sinh(arg_val)
        slope = -1.0 - scale * half_q / jnp.sqrt(1.0 + arg_val * arg_val)
        rate = rate - 0.35 * resid / slope
    return rate

def reference(velocity, stress, material, patch_order, fault_params):
    buoyancy = jnp.zeros(material.shape, jnp.float32)
    for index in range(4):
        buoyancy = buoyancy + (material == index).astype(jnp.float32) * BUOY[index]
    dxx = minus_diff(stress[0], 0)
    vx = velocity[0] + 0.25 * buoyancy * (dxx + minus_diff(stress[3], 2) + minus_diff(stress[4], 1))
    vy = velocity[1] + 0.25 * buoyancy * (plus_diff(stress[3], 0) + plus_diff(stress[1], 2) + minus_diff(stress[5], 1))
    vz = velocity[2] + 0.25 * buoyancy * (plus_diff(stress[4], 0) + plus_diff(stress[5], 2) + plus_diff(stress[2], 1))
    cols = slice(FAULT_START, FAULT_START + FAULT_COLS)
    traction = (stress[3, cols, :, FAULT_ROW] + 0.5 * dxx[cols, :, FAULT_ROW]).T
    owned = traction[:, patch_order]
    slip_rate = friction(owned, fault_params)
    slip_cols = jnp.zeros_like(slip_rate).at[:, patch_order].set(slip_rate).T
    plus_side = vx[cols, :, FAULT_ROW]
    minus_side = vx[cols, :, FAULT_ROW - 1]
    middle = 0.5 * (plus_side + minus_side)
    vx = vx.at[cols, :, FAULT_ROW].set(middle + 0.5 * slip_cols)
    vx = vx.at[cols, :, FAULT_ROW - 1].set(middle - 0.5 * slip_cols)
    return (jnp.stack([vx, vy, vz]), slip_rate)
```

```python
import functools

import jax
import jax.numpy as jnp
from jax import lax
from jax.experimental import pallas as pl
from jax.experimental.pallas import tpu as pltpu
from jax.sharding import PartitionSpec as P

NEWTON = 8
BUOY = (1.0, 0.8, 0.6, 1.25)
C_ONE = 9.0 / 8.0
C_TWO = -1.0 / 24.0
MESH = pl.DeviceIdType.MESH


def friction(tau_total, coef, psi, normal_stress):
    half_q = 0.5 * jnp.exp(psi / coef)
    scale = normal_stress * coef
    stiff = scale * half_q
    rate = jnp.zeros_like(tau_total)
    for _ in range(NEWTON):
        arg_val = rate * half_q
        root = jnp.sqrt(1.0 + arg_val * arg_val)
        magnitude = jnp.log(jnp.abs(arg_val) + root)
        resid = tau_total - rate - scale * jnp.where(arg_val < 0, -magnitude, magnitude)
        rate = rate + 0.35 * resid * (root / (root + stiff))
    return rate


def kernel(
    dims, vel, st, mat, order, fp, out, slip,
    po, sx, so, vb, mb, bb, pb, ownp, zup, zdn, zlo, zhi, packs, recv,
    lsem, zload, psend, precv, xsend, xrecv, zsend, zrecv, strike_in, depth_in,
):
    n, nd, cx, cz, ny, fc, wide = dims
    row = ny // 2
    per = fc // n
    first_tile = n // 4
    tiles = fc // cx
    me = lax.axis_index("strike")
    dep = lax.axis_index("depth")
    has_left, has_right = me > 0, me < n - 1
    has_below, has_above = dep > 0, dep < nd - 1
    is_tile = jnp.logical_and(me >= first_tile, me < first_tile + tiles)
    near = jnp.logical_and(me >= first_tile - 1, me <= first_tile + tiles)

    def tile_at(j):
        return first_tile <= j < first_tile + tiles

    def near_at(j):
        return first_tile - 1 <= j <= first_tile + tiles

    def sends_to(j):
        return jnp.logical_and(me != j, jnp.logical_or(near, tile_at(j)))

    def hears_from(j):
        return jnp.logical_and(me != j, jnp.logical_or(is_tile, near_at(j)))

    def partner(j):
        beside = jnp.logical_or(me == j - 1, me == j + 1)
        return jnp.logical_or(beside, jnp.logical_or(sends_to(j), hears_from(j)))

    barrier = pltpu.get_barrier_semaphore()
    for j in range(n):

        @pl.when(jnp.logical_and(j > me, partner(j)))
        def _():
            pl.semaphore_signal(barrier, inc=1, device_id=(j, dep), device_id_type=MESH)

    @pl.when(has_above)
    def _():
        pl.semaphore_signal(barrier, inc=1, device_id=(me, dep + 1), device_id_type=MESH)

    loads = [
        pltpu.make_async_copy(st.at[0], sx.at[0, pl.ds(2, cx)], lsem.at[0]),
        pltpu.make_async_copy(st.at[3], sx.at[1, pl.ds(2, cx)], lsem.at[1]),
        pltpu.make_async_copy(fp, pb, lsem.at[2]),
        pltpu.make_async_copy(st.at[4], sx.at[2, pl.ds(2, cx)], lsem.at[3]),
        pltpu.make_async_copy(st.at[2], so.at[1], lsem.at[4]),
        pltpu.make_async_copy(st.at[5], so.at[2], lsem.at[5]),
        pltpu.make_async_copy(st.at[1], so.at[0], lsem.at[6]),
        pltpu.make_async_copy(mat, mb, lsem.at[7]),
        pltpu.make_async_copy(vel, vb, lsem.at[8]),
        pltpu.make_async_copy(order, po, lsem.at[9]),
    ]
    up_rows = ((4, cz - 2), (4, cz - 1), (5, cz - 2), (5, cz - 1), (2, cz - 1))
    down_rows = ((4, 0), (5, 0), (2, 0), (2, 1))
    zloads = [
        pltpu.make_async_copy(st.at[f, :, r], held.at[k], zload.at[at + k])
        for rows, held, at in ((up_rows, zup, 0), (down_rows, zdn, 5))
        for k, (f, r) in enumerate(rows)
    ]
    for load in loads[9:] + loads[:3] + zloads + loads[3:9]:
        load.start()

    zero_row = jnp.zeros((2, cz, ny), jnp.float32)

    @pl.when(jnp.logical_not(has_left))
    def _():
        for f in range(3):
            sx[f, 0:2] = zero_row

    @pl.when(jnp.logical_not(has_right))
    def _():
        for f in range(3):
            sx[f, cx + 2 : cx + 4] = zero_row

    @pl.when(jnp.logical_not(has_below))
    def _():
        zlo[...] = jnp.zeros(zlo.shape, jnp.float32)

    @pl.when(jnp.logical_not(has_above))
    def _():
        zhi[...] = jnp.zeros(zhi.shape, jnp.float32)

    for j in range(n):
        if not near_at(j):

            @pl.when(jnp.logical_not(is_tile))
            def _():
                recv[j] = jnp.zeros(recv.shape[1:], jnp.float32)

    earlier = has_below.astype(jnp.int32)
    for j in range(n):
        earlier = earlier + jnp.logical_and(j < me, partner(j)).astype(jnp.int32)
    with jax.named_scope("entry"):

        @pl.when(earlier > 0)
        def _():
            pl.semaphore_wait(barrier, earlier)

    for j in range(n):
        told = jnp.logical_or(hears_from(j), me == j + 1)

        @pl.when(jnp.logical_and(j < me, told))
        def _():
            pl.semaphore_signal(
                strike_in.at[me], inc=1, device_id=(j, dep), device_id_type=MESH
            )

    @pl.when(has_below)
    def _():
        pl.semaphore_signal(depth_in, inc=1, device_id=(me, dep - 1), device_id_type=MESH)

    def x_copies(up):
        pairs = []
        for g, (f, fields) in enumerate(((0, 1), (1, 2))):
            if up:
                rows = 2 if f == 0 else 1
                src, dst, to = cx - rows, 2 - rows, me + 1
            else:
                rows = 1 if f == 0 else 2
                src, dst, to = 0, cx + 2, me - 1
            slot = g if up else 2 + g
            pairs.append(
                pltpu.make_async_remote_copy(
                    src_ref=st.at[pl.ds(3 * f, fields), pl.ds(src, rows)],
                    dst_ref=sx.at[pl.ds(f, fields), pl.ds(dst, rows)],
                    send_sem=xsend.at[slot],
                    recv_sem=xrecv.at[slot],
                    device_id=(to, dep),
                    device_id_type=MESH,
                )
            )
        return pairs

    def z_copy(up):
        return pltpu.make_async_remote_copy(
            src_ref=zup if up else zdn,
            dst_ref=zlo if up else zhi,
            send_sem=zsend.at[0 if up else 1],
            recv_sem=zrecv.at[0 if up else 1],
            device_id=(me, dep + 1 if up else dep - 1),
            device_id_type=MESH,
        )

    def pack_copy(j):
        return pltpu.make_async_remote_copy(
            src_ref=packs.at[min(max(j - first_tile, 0), tiles - 1)],
            dst_ref=recv.at[me],
            send_sem=psend.at[j],
            recv_sem=precv.at[me],
            device_id=(j, dep),
            device_id_type=MESH,
        )

    def pack_arrival(j):
        return pltpu.make_async_remote_copy(
            src_ref=packs.at[0],
            dst_ref=recv.at[j],
            send_sem=psend.at[j],
            recv_sem=precv.at[j],
            device_id=(j, dep),
            device_id_type=MESH,
        )

    @pl.when(has_left)
    def _():
        for copy in x_copies(False):
            copy.start()

    lane = lax.broadcasted_iota(jnp.int32, (cz, wide), 1)
    lane_one = lax.broadcasted_iota(jnp.int32, (cz, 128), 1)
    with jax.named_scope("first_loads"):
        loads[0].wait()
        loads[1].wait()
        loads[2].wait()
        loads[9].wait()
    with jax.named_scope("pack"):
        base = jnp.where(near, 4 * cx + (me - first_tile) * cx, -4 * wide)
        normal = jnp.zeros((cz, wide), jnp.float32)
        shear = jnp.zeros((cz, wide), jnp.float32)
        for i in range(cx):
            here = lane == base + i
            normal = jnp.where(here, sx[0, 2 + i, :, row : row + 1], normal)
            shear = jnp.where(here, sx[1, 2 + i, :, row : row + 1], shear)
        dxx = C_ONE * (normal - pltpu.roll(normal, 1, 1)) + C_TWO * (
            pltpu.roll(normal, wide - 1, 1) - pltpu.roll(normal, 2, 1)
        )
        share = shear + 0.5 * dxx
        share = jnp.where(jnp.logical_and(lane >= 4 * cx, lane < 4 * cx + fc), share, 0.0)
        blocks = [share for _ in range(tiles)]
        params = [pb[j].T for j in range(per)]
        for f in range(4):
            mine = jnp.full((cz, 128), 1.0, jnp.float32)
            for j in range(per):
                column = po[me * per + j]
                value = params[j][:, f : f + 1]
                mine = jnp.where(lane_one == cx + j, value, mine)
                for t in range(tiles):
                    local = column - t * cx
                    held = jnp.logical_and(local >= 0, local < cx)
                    place = jnp.where(held, f * cx + local, -1)
                    blocks[t] = jnp.where(lane == place, value, blocks[t])
            ownp[f] = mine
        for t in range(tiles):
            packs[t] = blocks[t]
        my_tile = jnp.clip(me - first_tile, 0, tiles - 1)

        @pl.when(near)
        def _():
            recv[me] = packs[my_tile]

    for j in range(n):

        @pl.when(jnp.logical_and(j < me, sends_to(j)))
        def _():
            pack_copy(j).start()

    with jax.named_scope("z_loads"):
        for load in zloads:
            load.wait()

    @pl.when(has_below)
    def _():
        z_copy(False).start()

    with jax.named_scope("loads"):
        for load in loads[3:9]:
            load.wait()

    yi = lax.broadcasted_iota(jnp.int32, (cz, ny), 1)
    zi = lax.broadcasted_iota(jnp.int32, (cz, ny), 0)

    def y_at(field, offset):
        moved = pltpu.roll(field, (-offset) % ny, 1)
        keep = yi < ny - offset if offset > 0 else yi >= -offset
        return jnp.where(keep, moved, 0.0)

    def z_at(field):
        def at(offset):
            if offset == 0:
                return field
            moved = pltpu.roll(field, (-offset) % cz, 0)
            keep = zi < cz - offset if offset > 0 else zi >= -offset
            return jnp.where(keep, moved, 0.0)

        return at

    def minus(at):
        return C_ONE * (at(0) - at(-1)) + C_TWO * (at(1) - at(-2))

    def plus(at):
        return C_ONE * (at(1) - at(0)) + C_TWO * (at(2) - at(-1))

    def along_x(f, x):
        return lambda offset: sx[f, x + 2 + offset]

    def along_y(field):
        return lambda offset: field if offset == 0 else y_at(field, offset)

    def buoyancy(x):
        material = mb[x]
        b = jnp.full((cz, ny), 0.25 * BUOY[0], jnp.float32)
        for index in range(1, 4):
            b = jnp.where(material == index, 0.25 * BUOY[index], b)
        bb[x] = b
        return b

    def across(x):
        return minus(along_x(0, x)), plus(along_x(1, x)), plus(along_x(2, x))

    def local(x):
        sxz, szz, syz = sx[2, x + 2], so[1, x], so[2, x]
        return (
            minus(along_y(sx[1, x + 2])) + minus(z_at(sxz)),
            plus(along_y(so[0, x])) + minus(z_at(syz)),
            plus(along_y(syz)) + plus(z_at(szz)),
        )

    def inner(x, carry):
        b, along, rest = buoyancy(x), across(x), local(x)
        for c in range(3):
            out[c, x] = vb[c, x] + b * (along[c] + rest[c])
        return carry

    def outer(x):
        b, rest = buoyancy(x), local(x)
        for c in range(3):
            out[c, x] = vb[c, x] + b * rest[c]

    edges = (0, 1, cx - 2, cx - 1)
    with jax.named_scope("outer"):
        for x in edges:
            outer(x)

    with jax.named_scope("wait_next"):

        @pl.when(has_right)
        def _():
            pl.semaphore_wait(strike_in.at[me + 1], 1)
            for copy in x_copies(True):
                copy.start()

        @pl.when(has_above)
        def _():
            pl.semaphore_wait(depth_in, 1)
            z_copy(True).start()

    with jax.named_scope("inner"):
        lax.fori_loop(2, cx - 2, inner, 0)

    with jax.named_scope("wait_far"):
        for j in range(n):

            @pl.when(jnp.logical_and(j > me, sends_to(j)))
            def _():
                @pl.when(me != j - 1)
                def _():
                    pl.semaphore_wait(strike_in.at[j], 1)

                pack_copy(j).start()

    with jax.named_scope("z_wait"):

        @pl.when(has_below)
        def _():
            z_copy(True).wait_recv()

        @pl.when(has_above)
        def _():
            z_copy(False).wait_recv()

    first = lax.broadcasted_iota(jnp.int32, (8, ny), 0)

    def face(x, carry):
        def low(k):
            return zlo[k, pl.ds(x, 1), :]

        def high(k):
            return zhi[k, pl.ds(x, 1), :]

        def put(at, one, two):
            return jnp.where(first == at, one, jnp.where(first == two[0], two[1], 0.0))

        b = bb[x, 0:8]
        out[0, x, 0:8] -= b * put(0, C_ONE * low(1) + C_TWO * low(0), (1, C_TWO * low(1)))
        out[1, x, 0:8] -= b * put(0, C_ONE * low(3) + C_TWO * low(2), (1, C_TWO * low(3)))
        out[2, x, 0:8] -= b * jnp.where(first == 0, C_TWO * low(4), 0.0)
        b = bb[x, cz - 8 : cz]
        out[0, x, cz - 8 : cz] += b * jnp.where(first == 7, C_TWO * high(0), 0.0)
        out[1, x, cz - 8 : cz] += b * jnp.where(first == 7, C_TWO * high(1), 0.0)
        out[2, x, cz - 8 : cz] += b * put(
            7, C_ONE * high(2) + C_TWO * high(3), (6, C_TWO * high(2))
        )
        return carry

    with jax.named_scope("face"):
        lax.fori_loop(0, cx, face, 0)

    with jax.named_scope("x_wait"):

        @pl.when(has_left)
        def _():
            for copy in x_copies(True):
                copy.wait_recv()

        @pl.when(has_right)
        def _():
            for copy in x_copies(False):
                copy.wait_recv()

    with jax.named_scope("edges"):
        for x in edges:
            along = across(x)
            for c in range(3):
                out[c, x] += bb[x] * along[c]

    with jax.named_scope("pack_wait"):
        for j in range(n):

            @pl.when(hears_from(j))
            def _():
                pack_arrival(j).wait_recv()

    with jax.named_scope("friction"):
        total = recv[first_tile - 1]
        for j in range(n):
            if j != first_tile - 1:
                total = total + recv[j]
        used = lane_one < cx
        fields = []
        for f in range(4):
            moved = total if f == 0 else pltpu.roll(total, wide - f * cx, 1)
            fields.append(jnp.where(used, moved[:, :128], ownp[f]))
        tau = jnp.zeros((cz, 128), jnp.float32)
        for t in range(tiles):
            moved = pltpu.roll(total, wide - (4 + t) * cx, 1)[:, :128]
            tau = jnp.where(jnp.logical_and(used, my_tile == t), moved, tau)
        for j in range(per):
            picked = jnp.where(lane == 4 * cx + po[me * per + j], total, 0.0)
            tau = jnp.where(
                lane_one == cx + j, jnp.sum(picked, axis=1, keepdims=True), tau
            )
        rate = friction(tau + fields[3], fields[0], fields[1], fields[2])
        slip[...] = rate.T[cx : cx + per]

    with jax.named_scope("fix"):

        @pl.when(is_tile)
        def _():
            for i in range(cx):
                s = 0.5 * rate[:, i : i + 1]
                low = out[0, i, :, row - 128 : row]
                high = out[0, i, :, row : row + 128]
                middle = 0.5 * (high + pltpu.roll(low, 1, 1))
                out[0, i, :, row : row + 128] = jnp.where(lane_one == 0, middle + s, high)
                out[0, i, :, row - 128 : row] = jnp.where(
                    lane_one == 127, pltpu.roll(middle, 127, 1) - s, low
                )

    with jax.named_scope("sends_done"):
        for j in range(n):

            @pl.when(sends_to(j))
            def _():
                pack_copy(j).wait_send()

        @pl.when(has_above)
        def _():
            z_copy(True).wait_send()

        @pl.when(has_below)
        def _():
            z_copy(False).wait_send()

        @pl.when(has_right)
        def _():
            for copy in x_copies(True):
                copy.wait_send()

        @pl.when(has_left)
        def _():
            for copy in x_copies(False):
                copy.wait_send()


def write_out(held, slip, out, slip_out, sem):
    copies = [pltpu.make_async_copy(slip, slip_out, sem.at[3])]
    copies += [pltpu.make_async_copy(held.at[c], out.at[c], sem.at[c]) for c in range(3)]
    for copy in copies:
        copy.start()
    for copy in copies:
        copy.wait()


def per_device(n, nd, velocity, stress, material, patch_order, fault_params):
    _, cx, cz, ny = stress.shape
    fc = patch_order.shape[0]
    per = fc // n
    wide = -(-(4 * cx + fc + 2) // 128) * 128
    dims = (n, nd, cx, cz, ny, fc, wide)
    tiles = fc // cx
    f32 = jnp.float32
    anywhere = pl.BlockSpec(memory_space=pltpu.HBM)
    dma = pltpu.SemaphoreType.DMA
    params = jnp.transpose(fault_params, (2, 0, 1))
    big = (velocity, stress, material, patch_order, params)
    held = pl.pallas_call(
        functools.partial(kernel, dims),
        out_shape=(
            jax.ShapeDtypeStruct(velocity.shape, f32),
            jax.ShapeDtypeStruct((per, cz), f32),
        ),
        in_specs=[anywhere] * 5,
        out_specs=(pl.BlockSpec(memory_space=pltpu.VMEM), pl.BlockSpec(memory_space=pltpu.VMEM)),
        scratch_shapes=[
            pltpu.SMEM((fc,), jnp.int32),
            pltpu.VMEM((3, cx + 4, cz, ny), f32),
            pltpu.VMEM((3, cx, cz, ny), f32),
            pltpu.VMEM((3, cx, cz, ny), f32),
            pltpu.VMEM((cx, cz, ny), jnp.int32),
            pltpu.VMEM((cx, cz, ny), f32),
            pltpu.VMEM((per, 4, cz), f32),
            pltpu.VMEM((4, cz, 128), f32),
            pltpu.VMEM((5, cx, ny), f32),
            pltpu.VMEM((4, cx, ny), f32),
            pltpu.VMEM((5, cx, ny), f32),
            pltpu.VMEM((4, cx, ny), f32),
            pltpu.VMEM((tiles, cz, wide), f32),
            pltpu.VMEM((n, cz, wide), f32),
            dma((10,)),
            dma((9,)),
            dma((n,)),
            dma((n,)),
            dma((4,)),
            dma((4,)),
            dma((2,)),
            dma((2,)),
            pltpu.SemaphoreType.REGULAR((n,)),
            pltpu.SemaphoreType.REGULAR,
        ],
        compiler_params=pltpu.CompilerParams(collective_id=0, has_side_effects=True, vmem_limit_bytes=12 << 20),
    )(*[pltpu.with_memory_space_constraint(v, pltpu.HBM) for v in big])
    resident = pl.BlockSpec(memory_space=pltpu.VMEM)
    moved, slip = pl.pallas_call(
        write_out,
        out_shape=(
            jax.ShapeDtypeStruct(velocity.shape, f32),
            jax.ShapeDtypeStruct((per, cz), f32),
        ),
        in_specs=[resident, resident],
        out_specs=(anywhere, anywhere),
        scratch_shapes=[dma((4,))],
        compiler_params=pltpu.CompilerParams(vmem_limit_bytes=4 << 20),
    )(*held)
    return moved, slip.T


def solution(mesh):
    n, nd = mesh.shape["strike"], mesh.shape["depth"]
    return jax.shard_map(
        functools.partial(per_device, n, nd),
        mesh=mesh,
        in_specs=(
            P(None, "strike", "depth", None),
            P(None, "strike", "depth", None),
            P("strike", "depth", None),
            P(),
            P(None, "depth", "strike"),
        ),
        out_specs=(P(None, "strike", "depth", None), P("depth", "strike")),
        check_vma=False,
    )
```

```python
import functools

import jax
import jax.numpy as jnp
from jax import lax
from jax.experimental import pallas as pl
from jax.experimental.pallas import tpu as pltpu
from jax.sharding import PartitionSpec as P

NEWTON = 8
BUOY = (1.0, 0.8, 0.6, 1.25)
C_ONE = 9.0 / 8.0
C_TWO = -1.0 / 24.0
MESH = pl.DeviceIdType.MESH


def friction(tau_total, coef, psi, normal_stress):
    half_q = 0.5 * jnp.exp(psi / coef)
    scale = normal_stress * coef
    stiff = scale * half_q
    rate = jnp.zeros_like(tau_total)
    for _ in range(NEWTON):
        arg_val = rate * half_q
        root = jnp.sqrt(1.0 + arg_val * arg_val)
        magnitude = jnp.log(jnp.abs(arg_val) + root)
        resid = tau_total - rate - scale * jnp.where(arg_val < 0, -magnitude, magnitude)
        rate = rate + 0.35 * resid * (root / (root + stiff))
    return rate


def kernel(
    dims, vel, st, mat, order, fp, out, slip,
    po, col, sx, so, vb, mb, bb, pb, ownp, zout, zin, packs, recv, halo,
    lsem, psend, precv, hsend, hrecv, xsend, xrecv, zsend, zrecv, next_in, far_in, depth_in,
):
    n, nd, cx, cz, ny, fc, wide = dims
    row = ny // 2
    per = fc // n
    first_tile = n // 4
    tiles = fc // cx
    me = lax.axis_index("strike")
    dep = lax.axis_index("depth")
    has_left, has_right = me > 0, me < n - 1
    has_below, has_above = dep > 0, dep < nd - 1
    is_tile = jnp.logical_and(me >= first_tile, me < first_tile + tiles)
    near = jnp.logical_and(me >= first_tile - 1, me < first_tile + tiles)

    def tile_at(j):
        return first_tile <= j < first_tile + tiles

    def near_at(j):
        return first_tile - 1 <= j < first_tile + tiles

    last = first_tile + tiles
    is_last = me == last

    def sends_to(j):
        return jnp.logical_and(me != j, jnp.logical_or(near, tile_at(j)))

    def halo_to(j):
        return jnp.logical_and(is_last, me != j)

    def reaches(j):
        return jnp.logical_or(sends_to(j), halo_to(j))

    def reached_by(j):
        return jnp.logical_and(me != j, jnp.logical_or(is_tile, near_at(j) or j == last))

    def partner(j):
        beside = jnp.logical_or(me == j - 1, me == j + 1)
        return jnp.logical_or(beside, jnp.logical_or(reaches(j), reached_by(j)))

    barrier = pltpu.get_barrier_semaphore()
    for j in range(n):

        @pl.when(jnp.logical_and(j > me, partner(j)))
        def _():
            pl.semaphore_signal(barrier, inc=1, device_id=(j, dep), device_id_type=MESH)

    @pl.when(has_above)
    def _():
        pl.semaphore_signal(barrier, inc=1, device_id=(me, dep + 1), device_id_type=MESH)

    step = cx // 4
    columns = [
        pltpu.make_async_copy(
            st.at[3 * f, pl.ds(k * step, step), :, pl.ds(row, 128)],
            col.at[f, pl.ds(k * step, step)],
            lsem.at[2],
        )
        for k in range(4)
        for f in range(2)
    ]
    small = [
        pltpu.make_async_copy(order, po, lsem.at[0]),
        pltpu.make_async_copy(fp, pb, lsem.at[1]),
    ]
    z_rows = (
        (4, cz - 2), (4, cz - 1), (5, cz - 2), (5, cz - 1), (2, cz - 1),
        (4, 0), (5, 0), (2, 0), (2, 1),
    )
    zloads = [
        pltpu.make_async_copy(st.at[f, :, r], zout.at[k], lsem.at[3])
        for k, (f, r) in enumerate(z_rows)
    ]
    loads = [
        pltpu.make_async_copy(st.at[0], sx.at[0, pl.ds(2, cx)], lsem.at[4]),
        pltpu.make_async_copy(
            st.at[pl.ds(3, 2)], sx.at[pl.ds(1, 2), pl.ds(2, cx)], lsem.at[4]
        ),
        pltpu.make_async_copy(st.at[pl.ds(1, 2)], so.at[pl.ds(0, 2)], lsem.at[5]),
        pltpu.make_async_copy(st.at[5], so.at[2], lsem.at[5]),
        pltpu.make_async_copy(mat, mb, lsem.at[6]),
        pltpu.make_async_copy(vel, vb, lsem.at[7]),
    ]
    for load in small + columns + zloads + loads:
        load.start()

    def arrived(ref, sem):
        pltpu.make_async_copy(ref, ref, sem).wait()

    zlo, zhi = zin.at[pl.ds(0, 5)], zin.at[pl.ds(5, 4)]
    zero_row = jnp.zeros((2, cz, ny), jnp.float32)

    @pl.when(jnp.logical_not(has_left))
    def _():
        for f in range(3):
            sx[f, 0:2] = zero_row

    @pl.when(jnp.logical_not(has_right))
    def _():
        for f in range(3):
            sx[f, cx + 2 : cx + 4] = zero_row

    @pl.when(jnp.logical_not(has_below))
    def _():
        zin[0:5] = jnp.zeros((5, cx, ny), jnp.float32)

    @pl.when(jnp.logical_not(has_above))
    def _():
        zin[5:9] = jnp.zeros((4, cx, ny), jnp.float32)

    for j in range(n):
        if not near_at(j):

            @pl.when(jnp.logical_not(is_tile))
            def _():
                recv[j] = jnp.zeros(recv.shape[1:], jnp.float32)

    def x_copies(up):
        pairs = []
        for f, fields in ((0, 1), (1, 2)):
            if up:
                rows = 2 if f == 0 else 1
                src, dst, to = cx - rows, 2 - rows, me + 1
            else:
                rows = 1 if f == 0 else 2
                src, dst, to = 0, cx + 2, me - 1
            slot = 0 if up else 1
            pairs.append(
                pltpu.make_async_remote_copy(
                    src_ref=st.at[pl.ds(3 * f, fields), pl.ds(src, rows)],
                    dst_ref=sx.at[pl.ds(f, fields), pl.ds(dst, rows)],
                    send_sem=xsend.at[slot],
                    recv_sem=xrecv.at[slot],
                    device_id=(to, dep),
                    device_id_type=MESH,
                )
            )
        return pairs

    def z_copy(up):
        return pltpu.make_async_remote_copy(
            src_ref=zout.at[pl.ds(0, 5)] if up else zout.at[pl.ds(5, 4)],
            dst_ref=zlo if up else zhi,
            send_sem=zsend.at[0 if up else 1],
            recv_sem=zrecv.at[0 if up else 1],
            device_id=(me, dep + 1 if up else dep - 1),
            device_id_type=MESH,
        )

    def pack_copy(j):
        return pltpu.make_async_remote_copy(
            src_ref=packs.at[min(max(j - first_tile, 0), tiles - 1)],
            dst_ref=recv.at[me],
            send_sem=psend,
            recv_sem=precv,
            device_id=(j, dep),
            device_id_type=MESH,
        )

    def halo_copy(j):
        return pltpu.make_async_remote_copy(
            src_ref=st.at[0, 0, :, pl.ds(row, 128)],
            dst_ref=halo,
            send_sem=hsend,
            recv_sem=hrecv,
            device_id=(j, dep),
            device_id_type=MESH,
        )

    earlier = has_below.astype(jnp.int32)
    for j in range(n):
        earlier = earlier + jnp.logical_and(j < me, partner(j)).astype(jnp.int32)
    late = me > last

    def enter():
        @pl.when(earlier > 0)
        def _():
            pl.semaphore_wait(barrier, earlier)

        @pl.when(is_last)
        def _():
            for j in range(last):
                halo_copy(j).start()

        for j in range(n):
            told = jnp.logical_and(j < me - 1, reached_by(j))

            @pl.when(told)
            def _():
                pl.semaphore_signal(
                    far_in.at[late.astype(jnp.int32)],
                    inc=1,
                    device_id=(j, dep),
                    device_id_type=MESH,
                )

        @pl.when(has_left)
        def _():
            pl.semaphore_signal(next_in, inc=1, device_id=(me - 1, dep), device_id_type=MESH)

        @pl.when(has_below)
        def _():
            pl.semaphore_signal(depth_in, inc=1, device_id=(me, dep - 1), device_id_type=MESH)

        @pl.when(jnp.logical_and(has_left, jnp.logical_not(is_tile)))
        def _():
            for copy in x_copies(False):
                copy.start()

    fast = jnp.logical_or(me == 0, me % 2 == 1)
    with jax.named_scope("entry_fast"):
        pl.when(fast)(enter)

    lane = lax.broadcasted_iota(jnp.int32, (cz, wide), 1)
    lane_one = lax.broadcasted_iota(jnp.int32, (cz, 128), 1)
    my_tile = jnp.clip(me - first_tile, 0, tiles - 1)
    with jax.named_scope("params_wait"):
        for load in small:
            load.wait()
    with jax.named_scope("params"):
        blocks = [jnp.zeros((cz, wide), jnp.float32) for _ in range(tiles)]
        params = [pb[j].T for j in range(per)]
        for f in range(4):
            mine = jnp.full((cz, 128), 1.0, jnp.float32)
            for j in range(per):
                column = po[me * per + j]
                value = params[j][:, f : f + 1]
                mine = jnp.where(lane_one == cx + j, value, mine)
                for t in range(tiles):
                    local = column - t * cx
                    held = jnp.logical_and(local >= 0, local < cx)
                    place = jnp.where(held, f * cx + local, -1)
                    blocks[t] = jnp.where(lane == place, value, blocks[t])
            ownp[f] = mine
        for t in range(tiles):
            packs[t] = blocks[t]
    with jax.named_scope("column_wait"):
        arrived(col, lsem.at[2])
    with jax.named_scope("pack"):

        @pl.when(near)
        def _():
            base = 4 * cx + (me - first_tile) * cx
            normal = jnp.zeros((cz, wide), jnp.float32)
            shear = jnp.zeros((cz, wide), jnp.float32)
            for i in range(cx):
                here = lane == base + i
                normal = jnp.where(here, col[0, i, :, 0:1], normal)
                shear = jnp.where(here, col[1, i, :, 0:1], shear)
            dxx = C_ONE * (normal - pltpu.roll(normal, 1, 1)) + C_TWO * (
                pltpu.roll(normal, wide - 1, 1) - pltpu.roll(normal, 2, 1)
            )
            share = shear + 0.5 * dxx
            inside = jnp.logical_and(lane >= 4 * cx, lane < 4 * cx + fc)
            share = jnp.where(inside, share, 0.0)
            for t in range(tiles):
                packs[t] = packs[t] + share
            recv[me] = packs[my_tile]

        @pl.when(is_last)
        def _():
            halo[...] = col[0, 0]

    with jax.named_scope("entry_slow"):
        pl.when(jnp.logical_not(fast))(enter)

    for j in range(n):

        @pl.when(jnp.logical_and(j < me, sends_to(j)))
        def _():
            pack_copy(j).start()

    @pl.when(is_tile)
    def _():
        for copy in x_copies(False):
            copy.start()

    with jax.named_scope("z_loads"):
        arrived(zout, lsem.at[3])

    @pl.when(has_below)
    def _():
        z_copy(False).start()

    with jax.named_scope("loads"):
        arrived(sx.at[:, pl.ds(2, cx)], lsem.at[4])
        arrived(so, lsem.at[5])
        arrived(mb, lsem.at[6])
        arrived(vb, lsem.at[7])

    yi = lax.broadcasted_iota(jnp.int32, (cz, ny), 1)
    zi = lax.broadcasted_iota(jnp.int32, (cz, ny), 0)

    def y_at(field, offset):
        moved = pltpu.roll(field, (-offset) % ny, 1)
        keep = yi < ny - offset if offset > 0 else yi >= -offset
        return jnp.where(keep, moved, 0.0)

    def z_at(field):
        def at(offset):
            if offset == 0:
                return field
            moved = pltpu.roll(field, (-offset) % cz, 0)
            keep = zi < cz - offset if offset > 0 else zi >= -offset
            return jnp.where(keep, moved, 0.0)

        return at

    def minus(at):
        return C_ONE * (at(0) - at(-1)) + C_TWO * (at(1) - at(-2))

    def plus(at):
        return C_ONE * (at(1) - at(0)) + C_TWO * (at(2) - at(-1))

    def along_x(f, x):
        return lambda offset: sx[f, x + 2 + offset]

    def along_y(field):
        return lambda offset: field if offset == 0 else y_at(field, offset)

    def buoyancy(x):
        material = mb[x]
        b = jnp.full((cz, ny), 0.25 * BUOY[0], jnp.float32)
        for index in range(1, 4):
            b = jnp.where(material == index, 0.25 * BUOY[index], b)
        bb[x] = b
        return b

    def across(x):
        return minus(along_x(0, x)), plus(along_x(1, x)), plus(along_x(2, x))

    def local(x):
        sxz, szz, syz = sx[2, x + 2], so[1, x], so[2, x]
        return (
            minus(along_y(sx[1, x + 2])) + minus(z_at(sxz)),
            plus(along_y(so[0, x])) + minus(z_at(syz)),
            plus(along_y(syz)) + plus(z_at(szz)),
        )

    def inner(x, carry):
        b, along, rest = buoyancy(x), across(x), local(x)
        for c in range(3):
            out[c, x] = vb[c, x] + b * (along[c] + rest[c])
        return carry

    def outer(x):
        b, rest = buoyancy(x), local(x)
        for c in range(3):
            out[c, x] = vb[c, x] + b * rest[c]

    edges = (0, 1, cx - 2, cx - 1)
    with jax.named_scope("outer"):
        for x in edges:
            outer(x)

    with jax.named_scope("wait_next"):

        @pl.when(has_right)
        def _():
            pl.semaphore_wait(next_in, 1)
            for j in range(1, n):

                @pl.when(jnp.logical_and(j == me + 1, sends_to(j)))
                def _():
                    pack_copy(j).start()

                @pl.when(jnp.logical_and(j == me + 1, halo_to(j)))
                def _():
                    halo_copy(j).start()

            for copy in x_copies(True):
                copy.start()

        @pl.when(has_above)
        def _():
            pl.semaphore_wait(depth_in, 1)
            z_copy(True).start()

    middle = cx // 2
    with jax.named_scope("inner"):
        lax.fori_loop(2, middle, inner, 0)

    def send_far(low, high, kind):
        group = [
            (j, jnp.logical_and(j > me + 1, reaches(j))) for j in range(low, high)
        ]
        count = sum(on.astype(jnp.int32) for _, on in group)

        @pl.when(count > 0)
        def _():
            pl.semaphore_wait(far_in.at[kind], count)

        for j, on in group:

            @pl.when(jnp.logical_and(on, sends_to(j)))
            def _():
                pack_copy(j).start()

            @pl.when(jnp.logical_and(on, halo_to(j)))
            def _():
                halo_copy(j).start()

    with jax.named_scope("wait_far"):
        send_far(2, last + 1, 0)
    with jax.named_scope("inner2"):
        lax.fori_loop(middle, cx - 2, inner, 0)
    with jax.named_scope("wait_far2"):
        send_far(last + 1, n, 1)

    with jax.named_scope("z_wait"):

        @pl.when(has_below)
        def _():
            z_copy(True).wait_recv()

        @pl.when(has_above)
        def _():
            z_copy(False).wait_recv()

    first = lax.broadcasted_iota(jnp.int32, (8, ny), 0)

    def face(x, carry):
        def low(k):
            return zin[k, pl.ds(x, 1), :]

        def high(k):
            return zin[5 + k, pl.ds(x, 1), :]

        def put(at, one, two):
            return jnp.where(first == at, one, jnp.where(first == two[0], two[1], 0.0))

        b = bb[x, 0:8]
        out[0, x, 0:8] -= b * put(0, C_ONE * low(1) + C_TWO * low(0), (1, C_TWO * low(1)))
        out[1, x, 0:8] -= b * put(0, C_ONE * low(3) + C_TWO * low(2), (1, C_TWO * low(3)))
        out[2, x, 0:8] -= b * jnp.where(first == 0, C_TWO * low(4), 0.0)
        b = bb[x, cz - 8 : cz]
        out[0, x, cz - 8 : cz] += b * jnp.where(first == 7, C_TWO * high(0), 0.0)
        out[1, x, cz - 8 : cz] += b * jnp.where(first == 7, C_TWO * high(1), 0.0)
        out[2, x, cz - 8 : cz] += b * put(
            7, C_ONE * high(2) + C_TWO * high(3), (6, C_TWO * high(2))
        )
        return carry

    with jax.named_scope("face"):
        lax.fori_loop(0, cx, face, 0)

    with jax.named_scope("x_wait"):

        @pl.when(has_left)
        def _():
            arrived(sx.at[0, pl.ds(0, 4)], xrecv.at[0])

        @pl.when(has_right)
        def _():
            arrived(sx.at[0, pl.ds(0, 5)], xrecv.at[1])

    with jax.named_scope("edges"):
        for x in edges:
            along = across(x)
            for c in range(3):
                out[c, x] += bb[x] * along[c]

    with jax.named_scope("pack_wait"):
        @pl.when(is_tile)
        def _():
            arrived(recv.at[pl.ds(0, n - 1)], precv)

        @pl.when(me == first_tile - 1)
        def _():
            arrived(recv.at[pl.ds(0, tiles)], precv)

        @pl.when(jnp.logical_not(near))
        def _():
            arrived(recv.at[pl.ds(0, tiles + 1)], precv)

        @pl.when(jnp.logical_not(is_last))
        def _():
            arrived(halo, hrecv)

    with jax.named_scope("friction"):
        total = recv[first_tile - 1]
        for j in range(n):
            if j != first_tile - 1:
                total = total + recv[j]
        edge = 0.5 * C_TWO * halo[:, 0:1]
        total = total + jnp.where(lane == 4 * cx + fc - 1, edge, 0.0)
        used = lane_one < cx
        fields = []
        for f in range(4):
            moved = total if f == 0 else pltpu.roll(total, wide - f * cx, 1)
            fields.append(jnp.where(used, moved[:, :128], ownp[f]))
        tau = jnp.zeros((cz, 128), jnp.float32)
        for t in range(tiles):
            moved = pltpu.roll(total, wide - (4 + t) * cx, 1)[:, :128]
            tau = jnp.where(jnp.logical_and(used, my_tile == t), moved, tau)
        for j in range(per):
            picked = jnp.where(lane == 4 * cx + po[me * per + j], total, 0.0)
            tau = jnp.where(
                lane_one == cx + j, jnp.sum(picked, axis=1, keepdims=True), tau
            )
        rate = friction(tau + fields[3], fields[0], fields[1], fields[2])
        slip[...] = rate.T[cx : cx + per]

    with jax.named_scope("fix"):

        @pl.when(is_tile)
        def _():
            for i in range(cx):
                s = 0.5 * rate[:, i : i + 1]
                low = out[0, i, :, row - 128 : row]
                high = out[0, i, :, row : row + 128]
                middle = 0.5 * (high + pltpu.roll(low, 1, 1))
                out[0, i, :, row : row + 128] = jnp.where(lane_one == 0, middle + s, high)
                out[0, i, :, row - 128 : row] = jnp.where(
                    lane_one == 127, pltpu.roll(middle, 127, 1) - s, low
                )

    with jax.named_scope("sends_done"):
        @pl.when(near)
        def _():
            arrived(recv.at[pl.ds(0, n - 1)], psend)

        @pl.when(jnp.logical_not(near))
        def _():
            arrived(recv.at[pl.ds(0, tiles)], psend)

        @pl.when(is_last)
        def _():
            arrived(recv.at[pl.ds(0, n - 1), :, pl.ds(0, 128)], hsend)

        @pl.when(has_above)
        def _():
            z_copy(True).wait_send()

        @pl.when(has_below)
        def _():
            z_copy(False).wait_send()

        @pl.when(has_right)
        def _():
            arrived(sx.at[0, pl.ds(0, 4)], xsend.at[0])

        @pl.when(has_left)
        def _():
            arrived(sx.at[0, pl.ds(0, 5)], xsend.at[1])


def write_out(held, slip, out, slip_out, sem):
    copies = [
        pltpu.make_async_copy(slip, slip_out, sem.at[0]),
        pltpu.make_async_copy(held, out, sem.at[1]),
    ]
    for copy in copies:
        copy.start()
    for copy in copies:
        copy.wait()


def per_device(n, nd, velocity, stress, material, patch_order, fault_params):
    _, cx, cz, ny = stress.shape
    fc = patch_order.shape[0]
    per = fc // n
    wide = -(-(4 * cx + fc + 2) // 128) * 128
    dims = (n, nd, cx, cz, ny, fc, wide)
    tiles = fc // cx
    f32 = jnp.float32
    anywhere = pl.BlockSpec(memory_space=pltpu.HBM)
    dma = pltpu.SemaphoreType.DMA
    params = jnp.transpose(fault_params, (2, 0, 1))
    big = (velocity, stress, material, patch_order, params)
    held = pl.pallas_call(
        functools.partial(kernel, dims),
        out_shape=(
            jax.ShapeDtypeStruct(velocity.shape, f32),
            jax.ShapeDtypeStruct((per, cz), f32),
        ),
        in_specs=[anywhere] * 5,
        out_specs=(pl.BlockSpec(memory_space=pltpu.VMEM), pl.BlockSpec(memory_space=pltpu.VMEM)),
        scratch_shapes=[
            pltpu.SMEM((fc,), jnp.int32),
            pltpu.VMEM((2, cx, cz, 128), f32),
            pltpu.VMEM((3, cx + 4, cz, ny), f32),
            pltpu.VMEM((3, cx, cz, ny), f32),
            pltpu.VMEM((3, cx, cz, ny), f32),
            pltpu.VMEM((cx, cz, ny), jnp.int32),
            pltpu.VMEM((cx, cz, ny), f32),
            pltpu.VMEM((per, 4, cz), f32),
            pltpu.VMEM((4, cz, 128), f32),
            pltpu.VMEM((9, cx, ny), f32),
            pltpu.VMEM((9, cx, ny), f32),
            pltpu.VMEM((tiles, cz, wide), f32),
            pltpu.VMEM((n, cz, wide), f32),
            pltpu.VMEM((cz, 128), f32),
            dma((8,)),
            dma,
            dma,
            dma,
            dma,
            dma((2,)),
            dma((2,)),
            dma((2,)),
            dma((2,)),
            pltpu.SemaphoreType.REGULAR,
            pltpu.SemaphoreType.REGULAR((2,)),
            pltpu.SemaphoreType.REGULAR,
        ],
        compiler_params=pltpu.CompilerParams(collective_id=0, has_side_effects=True, vmem_limit_bytes=12 << 20),
    )(*[pltpu.with_memory_space_constraint(v, pltpu.HBM) for v in big])
    resident = pl.BlockSpec(memory_space=pltpu.VMEM)
    moved, slip = pl.pallas_call(
        write_out,
        out_shape=(
            jax.ShapeDtypeStruct(velocity.shape, f32),
            jax.ShapeDtypeStruct((per, cz), f32),
        ),
        in_specs=[resident, resident],
        out_specs=(anywhere, anywhere),
        scratch_shapes=[dma((2,))],
        compiler_params=pltpu.CompilerParams(vmem_limit_bytes=4 << 20),
    )(*held)
    return moved, slip.T


def solution(mesh):
    n, nd = mesh.shape["strike"], mesh.shape["depth"]
    return jax.shard_map(
        functools.partial(per_device, n, nd),
        mesh=mesh,
        in_specs=(
            P(None, "strike", "depth", None),
            P(None, "strike", "depth", None),
            P("strike", "depth", None),
            P(),
            P(None, "depth", "strike"),
        ),
        out_specs=(P(None, "strike", "depth", None), P("depth", "strike")),
        check_vma=False,
    )
```

```python
import functools

import jax
import jax.numpy as jnp
from jax import lax
from jax.experimental import pallas as pl
from jax.experimental.pallas import tpu as pltpu
from jax.sharding import PartitionSpec as P

NEWTON = 8
BUOY = (1.0, 0.8, 0.6, 1.25)
C_ONE = 9.0 / 8.0
C_TWO = -1.0 / 24.0
MESH = pl.DeviceIdType.MESH


def friction(tau_total, coef, psi, normal_stress):
    half_q = 0.5 * jnp.exp(psi / coef)
    scale = normal_stress * coef
    stiff = scale * half_q
    rate = 0.35 * tau_total / (1.0 + stiff)
    for _ in range(NEWTON - 1):
        arg_val = rate * half_q
        square = 1.0 + arg_val * arg_val
        inverse = lax.rsqrt(square)
        magnitude = jnp.log(jnp.abs(arg_val) + square * inverse)
        resid = tau_total - rate - scale * jnp.where(arg_val < 0, -magnitude, magnitude)
        rate = rate + 0.35 * resid / (1.0 + stiff * inverse)
    return rate


def kernel(
    dims, vel, st, mat, order, fp, out, state,
    po, col, sx, so, vb, mb, bb, pb, ownp, zout, zin, packs, recv, halo, rates,
    lsem, psend, precv, hsend, hrecv, xsend, xrecv, zsend, zrecv, next_in, far_in, depth_in,
):
    n, nd, cx, cz, ny, fc, wide = dims
    row = ny // 2
    per = fc // n
    first_tile = n // 4
    tiles = fc // cx
    me = lax.axis_index("strike")
    dep = lax.axis_index("depth")
    has_left, has_right = me > 0, me < n - 1
    has_below, has_above = dep > 0, dep < nd - 1
    is_tile = jnp.logical_and(me >= first_tile, me < first_tile + tiles)
    near = jnp.logical_and(me >= first_tile - 1, me < first_tile + tiles)

    def tile_at(j):
        return first_tile <= j < first_tile + tiles

    def near_at(j):
        return first_tile - 1 <= j < first_tile + tiles

    last = first_tile + tiles
    is_last = me == last

    def pairs(j):
        return jnp.logical_and(
            j % 2 == 0, jnp.logical_and(j >= first_tile, j < last - 2)
        )

    paired = pairs(me)

    def sends_to(j):
        return jnp.logical_and(me != j, jnp.logical_or(near, tile_at(j)))

    def halo_to(j):
        return jnp.logical_and(is_last, me != j)

    def reaches(j):
        return jnp.logical_or(sends_to(j), halo_to(j))

    def reached_by(j):
        return jnp.logical_and(me != j, jnp.logical_or(is_tile, near_at(j) or j == last))

    def partner(j):
        beside = jnp.logical_or(me == j - 1, me == j + 1)
        return jnp.logical_or(beside, jnp.logical_or(reaches(j), reached_by(j)))

    barrier = pltpu.get_barrier_semaphore()
    for j in range(n):

        back = jnp.logical_and(j == me - 1, pairs(j))

        @pl.when(jnp.logical_or(jnp.logical_and(j > me, partner(j)), back))
        def _():
            pl.semaphore_signal(barrier, inc=1, device_id=(j, dep), device_id_type=MESH)

    @pl.when(has_above)
    def _():
        pl.semaphore_signal(barrier, inc=1, device_id=(me, dep + 1), device_id_type=MESH)

    step = cx // 4
    columns = [
        pltpu.make_async_copy(
            st.at[3 * f, pl.ds(k * step, step), :, pl.ds(row, 128)],
            col.at[f, pl.ds(k * step, step)],
            lsem.at[2],
        )
        for k in range(4)
        for f in range(2)
    ]
    small = [
        pltpu.make_async_copy(order, po, lsem.at[0]),
        pltpu.make_async_copy(fp, pb, lsem.at[1]),
    ]
    z_rows = (
        (4, cz - 2), (4, cz - 1), (5, cz - 2), (5, cz - 1), (2, cz - 1),
        (4, 0), (5, 0), (2, 0), (2, 1),
    )
    zloads = [
        pltpu.make_async_copy(st.at[f, :, r], zout.at[k], lsem.at[3])
        for k, (f, r) in enumerate(z_rows)
    ]
    loads = [
        pltpu.make_async_copy(st.at[0], sx.at[0, pl.ds(2, cx)], lsem.at[4]),
        pltpu.make_async_copy(
            st.at[pl.ds(3, 2)], sx.at[pl.ds(1, 2), pl.ds(2, cx)], lsem.at[4]
        ),
        pltpu.make_async_copy(st.at[pl.ds(1, 2)], so.at[pl.ds(0, 2)], lsem.at[5]),
        pltpu.make_async_copy(st.at[5], so.at[2], lsem.at[5]),
        pltpu.make_async_copy(mat, mb, lsem.at[6]),
        pltpu.make_async_copy(vel, vb, lsem.at[7]),
    ]
    for load in small + columns + zloads + loads:
        load.start()

    def arrived(ref, sem):
        pltpu.make_async_copy(ref, ref, sem).wait()

    zlo, zhi = zin.at[pl.ds(0, 5)], zin.at[pl.ds(5, 4)]
    zero_row = jnp.zeros((2, cz, ny), jnp.float32)

    @pl.when(jnp.logical_not(has_left))
    def _():
        for f in range(3):
            sx[f, 0:2] = zero_row

    @pl.when(jnp.logical_not(has_right))
    def _():
        for f in range(3):
            sx[f, cx + 2 : cx + 4] = zero_row

    @pl.when(jnp.logical_not(has_below))
    def _():
        zin[0:5] = jnp.zeros((5, cx, ny), jnp.float32)

    @pl.when(jnp.logical_not(has_above))
    def _():
        zin[5:9] = jnp.zeros((4, cx, ny), jnp.float32)

    for j in range(n):
        if not near_at(j):

            @pl.when(jnp.logical_not(is_tile))
            def _():
                recv[j] = jnp.zeros(recv.shape[1:], jnp.float32)

    def x_copies(up):
        pairs = []
        for f, fields in ((0, 1), (1, 2)):
            if up:
                rows = 2 if f == 0 else 1
                src, dst, to = cx - rows, 2 - rows, me + 1
            else:
                rows = 1 if f == 0 else 2
                src, dst, to = 0, cx + 2, me - 1
            slot = 0 if up else 1
            pairs.append(
                pltpu.make_async_remote_copy(
                    src_ref=st.at[pl.ds(3 * f, fields), pl.ds(src, rows)],
                    dst_ref=sx.at[pl.ds(f, fields), pl.ds(dst, rows)],
                    send_sem=xsend.at[slot],
                    recv_sem=xrecv.at[slot],
                    device_id=(to, dep),
                    device_id_type=MESH,
                )
            )
        return pairs

    def z_copy(up):
        return pltpu.make_async_remote_copy(
            src_ref=zout.at[pl.ds(0, 5)] if up else zout.at[pl.ds(5, 4)],
            dst_ref=zlo if up else zhi,
            send_sem=zsend.at[0 if up else 1],
            recv_sem=zrecv.at[0 if up else 1],
            device_id=(me, dep + 1 if up else dep - 1),
            device_id_type=MESH,
        )

    def pack_copy(j):
        return pltpu.make_async_remote_copy(
            src_ref=packs.at[min(max(j - first_tile, 0), tiles - 1)],
            dst_ref=recv.at[me],
            send_sem=psend,
            recv_sem=precv,
            device_id=(j, dep),
            device_id_type=MESH,
        )

    def pack_next():
        for j in range(1, n):

            @pl.when(jnp.logical_and(j == me + 1, sends_to(j)))
            def _():
                pack_copy(j).start()

            @pl.when(jnp.logical_and(j == me + 1, halo_to(j)))
            def _():
                halo_copy(j).start()

    def halo_copy(j):
        return pltpu.make_async_remote_copy(
            src_ref=st.at[0, 0, :, pl.ds(row, 128)],
            dst_ref=halo,
            send_sem=hsend,
            recv_sem=hrecv,
            device_id=(j, dep),
            device_id_type=MESH,
        )

    earlier = has_below.astype(jnp.int32) + paired.astype(jnp.int32)
    for j in range(n):
        earlier = earlier + jnp.logical_and(j < me, partner(j)).astype(jnp.int32)
    late = me > last

    def enter():
        @pl.when(earlier > 0)
        def _():
            pl.semaphore_wait(barrier, earlier)

        @pl.when(is_last)
        def _():
            for j in range(last):
                halo_copy(j).start()

        for j in range(n):
            told = jnp.logical_and(j < me - 1, reached_by(j))

            @pl.when(told)
            def _():
                pl.semaphore_signal(
                    far_in.at[late.astype(jnp.int32)],
                    inc=1,
                    device_id=(j, dep),
                    device_id_type=MESH,
                )

        @pl.when(jnp.logical_and(has_left, jnp.logical_not(pairs(me - 1))))
        def _():
            pl.semaphore_signal(next_in, inc=1, device_id=(me - 1, dep), device_id_type=MESH)

        @pl.when(has_below)
        def _():
            pl.semaphore_signal(depth_in, inc=1, device_id=(me, dep - 1), device_id_type=MESH)

        @pl.when(has_left)
        def _():
            for copy in x_copies(False):
                copy.start()

        @pl.when(paired)
        def _():
            for copy in x_copies(True):
                copy.start()

    fast = jnp.logical_or(me == 0, me % 2 == 1)
    with jax.named_scope("entry_fast"):
        pl.when(fast)(enter)

    lane = lax.broadcasted_iota(jnp.int32, (cz, wide), 1)
    lane_one = lax.broadcasted_iota(jnp.int32, (cz, 128), 1)
    my_tile = jnp.clip(me - first_tile, 0, tiles - 1)
    with jax.named_scope("params_wait"):
        for load in small:
            load.wait()
    with jax.named_scope("params"):
        blocks = [jnp.zeros((cz, wide), jnp.float32) for _ in range(tiles)]
        params = [pb[j].T for j in range(per)]
        for f in range(4):
            mine = jnp.full((cz, 128), 1.0, jnp.float32)
            for j in range(per):
                column = po[me * per + j]
                value = params[j][:, f : f + 1]
                mine = jnp.where(lane_one == cx + j, value, mine)
                for t in range(tiles):
                    local = column - t * cx
                    held = jnp.logical_and(local >= 0, local < cx)
                    place = jnp.where(held, f * cx + local, -1)
                    blocks[t] = jnp.where(lane == place, value, blocks[t])
            ownp[f] = mine
        for t in range(tiles):
            packs[t] = blocks[t]
    with jax.named_scope("column_wait"):
        arrived(col, lsem.at[2])
    with jax.named_scope("pack"):

        @pl.when(near)
        def _():
            base = 4 * cx + (me - first_tile) * cx
            normal = jnp.zeros((cz, wide), jnp.float32)
            shear = jnp.zeros((cz, wide), jnp.float32)
            for i in range(cx):
                here = lane == base + i
                normal = jnp.where(here, col[0, i, :, 0:1], normal)
                shear = jnp.where(here, col[1, i, :, 0:1], shear)
            dxx = C_ONE * (normal - pltpu.roll(normal, 1, 1)) + C_TWO * (
                pltpu.roll(normal, wide - 1, 1) - pltpu.roll(normal, 2, 1)
            )
            share = shear + 0.5 * dxx
            inside = jnp.logical_and(lane >= 4 * cx, lane < 4 * cx + fc)
            share = jnp.where(inside, share, 0.0)
            for t in range(tiles):
                packs[t] = packs[t] + share
            recv[me] = packs[my_tile]

        @pl.when(is_last)
        def _():
            halo[...] = col[0, 0]

    with jax.named_scope("entry_slow"):
        pl.when(jnp.logical_not(fast))(enter)

    for j in range(n):

        @pl.when(jnp.logical_and(j < me, sends_to(j)))
        def _():
            pack_copy(j).start()

    @pl.when(paired)
    def _():
        pack_next()

    with jax.named_scope("z_loads"):
        arrived(zout, lsem.at[3])

    @pl.when(has_below)
    def _():
        z_copy(False).start()

    with jax.named_scope("loads"):
        arrived(sx.at[:, pl.ds(2, cx)], lsem.at[4])
        arrived(so, lsem.at[5])
        arrived(mb, lsem.at[6])
        arrived(vb, lsem.at[7])

    yi = lax.broadcasted_iota(jnp.int32, (cz, ny), 1)
    zi = lax.broadcasted_iota(jnp.int32, (cz, ny), 0)

    def y_at(field, offset):
        moved = pltpu.roll(field, (-offset) % ny, 1)
        keep = yi < ny - offset if offset > 0 else yi >= -offset
        return jnp.where(keep, moved, 0.0)

    def z_at(field):
        def at(offset):
            if offset == 0:
                return field
            moved = pltpu.roll(field, (-offset) % cz, 0)
            keep = zi < cz - offset if offset > 0 else zi >= -offset
            return jnp.where(keep, moved, 0.0)

        return at

    def minus(at):
        return C_ONE * (at(0) - at(-1)) + C_TWO * (at(1) - at(-2))

    def plus(at):
        return C_ONE * (at(1) - at(0)) + C_TWO * (at(2) - at(-1))

    def along_x(f, x):
        return lambda offset: sx[f, x + 2 + offset]

    def along_y(field):
        return lambda offset: field if offset == 0 else y_at(field, offset)

    def buoyancy(x):
        material = mb[x]
        b = jnp.full((cz, ny), 0.25 * BUOY[0], jnp.float32)
        for index in range(1, 4):
            b = jnp.where(material == index, 0.25 * BUOY[index], b)
        bb[x] = b
        return b

    def across(x):
        return minus(along_x(0, x)), plus(along_x(1, x)), plus(along_x(2, x))

    def local(x):
        sxz, szz, syz = sx[2, x + 2], so[1, x], so[2, x]
        return (
            minus(along_y(sx[1, x + 2])) + minus(z_at(sxz)),
            plus(along_y(so[0, x])) + minus(z_at(syz)),
            plus(along_y(syz)) + plus(z_at(szz)),
        )

    def inner(x, carry):
        b, along, rest = buoyancy(x), across(x), local(x)
        for c in range(3):
            out[c, x] = vb[c, x] + b * (along[c] + rest[c])
        return carry

    def outer(x):
        b, rest = buoyancy(x), local(x)
        for c in range(3):
            out[c, x] = vb[c, x] + b * rest[c]

    edges = (0, 1, cx - 2, cx - 1)
    with jax.named_scope("outer"):
        for x in edges:
            outer(x)

    with jax.named_scope("wait_next"):

        @pl.when(jnp.logical_and(has_right, jnp.logical_not(paired)))
        def _():
            pl.semaphore_wait(next_in, 1)
            pack_next()
            for copy in x_copies(True):
                copy.start()

        @pl.when(has_above)
        def _():
            pl.semaphore_wait(depth_in, 1)
            z_copy(True).start()

    middle = cx // 2
    with jax.named_scope("inner"):
        lax.fori_loop(2, middle, inner, 0)

    def send_far(low, high, kind):
        group = [
            (j, jnp.logical_and(j > me + 1, reaches(j))) for j in range(low, high)
        ]
        count = sum(on.astype(jnp.int32) for _, on in group)

        @pl.when(count > 0)
        def _():
            pl.semaphore_wait(far_in.at[kind], count)

        for j, on in group:

            @pl.when(jnp.logical_and(on, sends_to(j)))
            def _():
                pack_copy(j).start()

            @pl.when(jnp.logical_and(on, halo_to(j)))
            def _():
                halo_copy(j).start()

    with jax.named_scope("wait_far"):
        send_far(2, last + 1, 0)
    with jax.named_scope("inner2"):
        lax.fori_loop(middle, cx - 2, inner, 0)
    with jax.named_scope("wait_far2"):
        send_far(last + 1, n, 1)

    with jax.named_scope("z_wait"):

        @pl.when(has_below)
        def _():
            z_copy(True).wait_recv()

        @pl.when(has_above)
        def _():
            z_copy(False).wait_recv()

    first = lax.broadcasted_iota(jnp.int32, (8, ny), 0)

    def face(x, carry):
        def low(k):
            return zin[k, pl.ds(x, 1), :]

        def high(k):
            return zin[5 + k, pl.ds(x, 1), :]

        def put(at, one, two):
            return jnp.where(first == at, one, jnp.where(first == two[0], two[1], 0.0))

        b = bb[x, 0:8]
        out[0, x, 0:8] -= b * put(0, C_ONE * low(1) + C_TWO * low(0), (1, C_TWO * low(1)))
        out[1, x, 0:8] -= b * put(0, C_ONE * low(3) + C_TWO * low(2), (1, C_TWO * low(3)))
        out[2, x, 0:8] -= b * jnp.where(first == 0, C_TWO * low(4), 0.0)
        b = bb[x, cz - 8 : cz]
        out[0, x, cz - 8 : cz] += b * jnp.where(first == 7, C_TWO * high(0), 0.0)
        out[1, x, cz - 8 : cz] += b * jnp.where(first == 7, C_TWO * high(1), 0.0)
        out[2, x, cz - 8 : cz] += b * put(
            7, C_ONE * high(2) + C_TWO * high(3), (6, C_TWO * high(2))
        )
        return carry

    with jax.named_scope("face"):
        lax.fori_loop(0, cx, face, 0)

    with jax.named_scope("pack_wait"):
        @pl.when(is_tile)
        def _():
            arrived(recv.at[pl.ds(0, n - 1)], precv)

        @pl.when(me == first_tile - 1)
        def _():
            arrived(recv.at[pl.ds(0, tiles)], precv)

        @pl.when(jnp.logical_not(near))
        def _():
            arrived(recv.at[pl.ds(0, tiles + 1)], precv)

        @pl.when(jnp.logical_not(is_last))
        def _():
            arrived(halo, hrecv)

    with jax.named_scope("friction"):
        total = recv[first_tile - 1]
        for j in range(n):
            if j != first_tile - 1:
                total = total + recv[j]
        edge = 0.5 * C_TWO * halo[:, 0:1]
        total = total + jnp.where(lane == 4 * cx + fc - 1, edge, 0.0)
        used = lane_one < cx
        fields = []
        for f in range(4):
            moved = total if f == 0 else pltpu.roll(total, wide - f * cx, 1)
            fields.append(jnp.where(used, moved[:, :128], ownp[f]))
        tau = jnp.zeros((cz, 128), jnp.float32)
        for t in range(tiles):
            moved = pltpu.roll(total, wide - (4 + t) * cx, 1)[:, :128]
            tau = jnp.where(jnp.logical_and(used, my_tile == t), moved, tau)
        for j in range(per):
            picked = jnp.where(lane == 4 * cx + po[me * per + j], total, 0.0)
            tau = jnp.where(
                lane_one == cx + j, jnp.sum(picked, axis=1, keepdims=True), tau
            )
        fields = [tau + fields[3]] + fields[:3]
        for k in range(4):
            state[k] = fields[k]

        @pl.when(is_tile)
        def _():
            rates[...] = 0.5 * friction(*fields)

    def fix(columns):
        parts = []
        for i in columns:
            low = out[0, i, :, row - 128 : row]
            high = out[0, i, :, row : row + 128]
            middle = 0.5 * (high + pltpu.roll(low, 1, 1))
            s = rates[:, i : i + 1]
            above = jnp.where(lane_one == 0, middle + s, high)
            below = jnp.where(lane_one == 127, pltpu.roll(middle, 127, 1) - s, low)
            parts.append((i, below, above))
        for i, below, above in parts:
            out[0, i, :, row - 128 : row] = below
            out[0, i, :, row : row + 128] = above

    with jax.named_scope("fix"):

        @pl.when(is_tile)
        def _():
            for i in range(2, cx - 2, 4):
                fix(range(i, min(i + 4, cx - 2)))

    with jax.named_scope("x_wait"):

        @pl.when(has_left)
        def _():
            arrived(sx.at[0, pl.ds(0, 4)], xrecv.at[0])

        @pl.when(has_right)
        def _():
            arrived(sx.at[0, pl.ds(0, 5)], xrecv.at[1])

    with jax.named_scope("edges"):
        for x in edges:
            along = across(x)
            for c in range(3):
                out[c, x] += bb[x] * along[c]

    with jax.named_scope("fix2"):

        @pl.when(is_tile)
        def _():
            fix(edges)

    with jax.named_scope("sends_done"):
        @pl.when(near)
        def _():
            arrived(recv.at[pl.ds(0, n - 1)], psend)

        @pl.when(jnp.logical_not(near))
        def _():
            arrived(recv.at[pl.ds(0, tiles)], psend)

        @pl.when(is_last)
        def _():
            arrived(recv.at[pl.ds(0, n - 1), :, pl.ds(0, 128)], hsend)

        @pl.when(has_above)
        def _():
            z_copy(True).wait_send()

        @pl.when(has_below)
        def _():
            z_copy(False).wait_send()

        @pl.when(has_right)
        def _():
            arrived(sx.at[0, pl.ds(0, 4)], xsend.at[0])

        @pl.when(has_left)
        def _():
            arrived(sx.at[0, pl.ds(0, 5)], xsend.at[1])


def write_out(first, held, state, out, slip_out, slip, sem):
    velocity = pltpu.make_async_copy(held, out, sem.at[0])
    velocity.start()
    rate = friction(state[0], state[1], state[2], state[3])
    slip[...] = rate.T[first : first + slip.shape[0]]
    rates = pltpu.make_async_copy(slip, slip_out, sem.at[1])
    rates.start()
    velocity.wait()
    rates.wait()


def per_device(n, nd, velocity, stress, material, patch_order, fault_params):
    _, cx, cz, ny = stress.shape
    fc = patch_order.shape[0]
    per = fc // n
    wide = -(-(4 * cx + fc + 2) // 128) * 128
    dims = (n, nd, cx, cz, ny, fc, wide)
    tiles = fc // cx
    f32 = jnp.float32
    anywhere = pl.BlockSpec(memory_space=pltpu.HBM)
    dma = pltpu.SemaphoreType.DMA
    params = jnp.transpose(fault_params, (2, 0, 1))
    big = (velocity, stress, material, patch_order, params)
    held = pl.pallas_call(
        functools.partial(kernel, dims),
        out_shape=(
            jax.ShapeDtypeStruct(velocity.shape, f32),
            jax.ShapeDtypeStruct((4, cz, 128), f32),
        ),
        in_specs=[anywhere] * 5,
        out_specs=(pl.BlockSpec(memory_space=pltpu.VMEM), pl.BlockSpec(memory_space=pltpu.VMEM)),
        scratch_shapes=[
            pltpu.SMEM((fc,), jnp.int32),
            pltpu.VMEM((2, cx, cz, 128), f32),
            pltpu.VMEM((3, cx + 4, cz, ny), f32),
            pltpu.VMEM((3, cx, cz, ny), f32),
            pltpu.VMEM((3, cx, cz, ny), f32),
            pltpu.VMEM((cx, cz, ny), jnp.int32),
            pltpu.VMEM((cx, cz, ny), f32),
            pltpu.VMEM((per, 4, cz), f32),
            pltpu.VMEM((4, cz, 128), f32),
            pltpu.VMEM((9, cx, ny), f32),
            pltpu.VMEM((9, cx, ny), f32),
            pltpu.VMEM((tiles, cz, wide), f32),
            pltpu.VMEM((n, cz, wide), f32),
            pltpu.VMEM((cz, 128), f32),
            pltpu.VMEM((cz, 128), f32),
            dma((8,)),
            dma,
            dma,
            dma,
            dma,
            dma((2,)),
            dma((2,)),
            dma((2,)),
            dma((2,)),
            pltpu.SemaphoreType.REGULAR,
            pltpu.SemaphoreType.REGULAR((2,)),
            pltpu.SemaphoreType.REGULAR,
        ],
        compiler_params=pltpu.CompilerParams(collective_id=0, has_side_effects=True, vmem_limit_bytes=12 << 20),
    )(*[pltpu.with_memory_space_constraint(v, pltpu.HBM) for v in big])
    resident = pl.BlockSpec(memory_space=pltpu.VMEM)
    moved, slip = pl.pallas_call(
        functools.partial(write_out, cx),
        out_shape=(
            jax.ShapeDtypeStruct(velocity.shape, f32),
            jax.ShapeDtypeStruct((per, cz), f32),
        ),
        in_specs=[resident, resident],
        out_specs=(anywhere, anywhere),
        scratch_shapes=[pltpu.VMEM((per, cz), f32), dma((2,))],
        compiler_params=pltpu.CompilerParams(vmem_limit_bytes=4 << 20),
    )(*held)
    return moved, slip.T


def solution(mesh):
    n, nd = mesh.shape["strike"], mesh.shape["depth"]
    return jax.shard_map(
        functools.partial(per_device, n, nd),
        mesh=mesh,
        in_specs=(
            P(None, "strike", "depth", None),
            P(None, "strike", "depth", None),
            P("strike", "depth", None),
            P(),
            P(None, "depth", "strike"),
        ),
        out_specs=(P(None, "strike", "depth", None), P("depth", "strike")),
        check_vma=False,
    )
```

```python
import functools

import jax
import jax.numpy as jnp
from jax import lax
from jax.experimental import pallas as pl
from jax.experimental.pallas import tpu as pltpu
from jax.sharding import PartitionSpec as P

NEWTON = 8
BUOY = (1.0, 0.8, 0.6, 1.25)
C_ONE = 9.0 / 8.0
C_TWO = -1.0 / 24.0
MESH = pl.DeviceIdType.MESH


def friction(tau_total, coef, psi, normal_stress):
    half_q = 0.5 * jnp.exp(psi / coef)
    scale = normal_stress * coef
    stiff = scale * half_q
    rate = 0.35 * tau_total / (1.0 + stiff)
    for _ in range(NEWTON - 1):
        arg_val = rate * half_q
        square = 1.0 + arg_val * arg_val
        inverse = lax.rsqrt(square)
        magnitude = jnp.log(jnp.abs(arg_val) + square * inverse)
        resid = tau_total - rate - scale * jnp.where(arg_val < 0, -magnitude, magnitude)
        rate = rate + 0.35 * resid / (1.0 + stiff * inverse)
    return rate


def kernel(
    dims, vel, st, mat, order, fp, out, state,
    po, col, sx, so, vb, mb, bb, pb, ownp, zout, zin, packs, recv, halo, rates,
    lsem, psend, precv, hsend, hrecv, xsend, xrecv, zsend, zrecv, next_in, far_in, depth_in,
):
    n, nd, cx, cz, ny, fc, wide = dims
    row = ny // 2
    per = fc // n
    first_tile = n // 4
    tiles = fc // cx
    me = lax.axis_index("strike")
    dep = lax.axis_index("depth")
    has_left, has_right = me > 0, me < n - 1
    has_below, has_above = dep > 0, dep < nd - 1
    is_tile = jnp.logical_and(me >= first_tile, me < first_tile + tiles)
    near = jnp.logical_and(me >= first_tile - 1, me < first_tile + tiles)

    def tile_at(j):
        return first_tile <= j < first_tile + tiles

    def near_at(j):
        return first_tile - 1 <= j < first_tile + tiles

    last = first_tile + tiles
    is_last = me == last

    def pairs(j):
        return jnp.logical_and(
            j % 2 == 0, jnp.logical_and(j >= first_tile, j < last - 2)
        )

    paired = pairs(me)

    def sends_to(j):
        return jnp.logical_and(me != j, jnp.logical_or(near, tile_at(j)))

    def halo_to(j):
        return jnp.logical_and(is_last, me != j)

    def reaches(j):
        return jnp.logical_or(sends_to(j), halo_to(j))

    def reached_by(j):
        return jnp.logical_and(me != j, jnp.logical_or(is_tile, near_at(j) or j == last))

    def partner(j):
        beside = jnp.logical_or(me == j - 1, me == j + 1)
        return jnp.logical_or(beside, jnp.logical_or(reaches(j), reached_by(j)))

    barrier = pltpu.get_barrier_semaphore()
    for j in range(n):

        back = jnp.logical_and(j == me - 1, pairs(j))

        @pl.when(jnp.logical_or(jnp.logical_and(j > me, partner(j)), back))
        def _():
            pl.semaphore_signal(barrier, inc=1, device_id=(j, dep), device_id_type=MESH)

    @pl.when(has_above)
    def _():
        pl.semaphore_signal(barrier, inc=1, device_id=(me, dep + 1), device_id_type=MESH)

    step = cx // 4
    columns = [
        pltpu.make_async_copy(
            st.at[3 * f, pl.ds(k * step, step), :, pl.ds(row, 128)],
            col.at[f, pl.ds(k * step, step)],
            lsem.at[2],
        )
        for k in range(4)
        for f in range(2)
    ]
    small = [
        pltpu.make_async_copy(order, po, lsem.at[0]),
        pltpu.make_async_copy(fp, pb, lsem.at[1]),
    ]
    z_rows = (
        (4, cz - 2), (4, cz - 1), (5, cz - 2), (5, cz - 1), (2, cz - 1),
        (4, 0), (5, 0), (2, 0), (2, 1),
    )
    zloads = [
        pltpu.make_async_copy(st.at[f, :, r], zout.at[k], lsem.at[3])
        for k, (f, r) in enumerate(z_rows)
    ]
    loads = [
        pltpu.make_async_copy(st.at[0], sx.at[0, pl.ds(2, cx)], lsem.at[4]),
        pltpu.make_async_copy(
            st.at[pl.ds(3, 2)], sx.at[pl.ds(1, 2), pl.ds(2, cx)], lsem.at[4]
        ),
        pltpu.make_async_copy(st.at[pl.ds(1, 2)], so.at[pl.ds(0, 2)], lsem.at[5]),
        pltpu.make_async_copy(st.at[5], so.at[2], lsem.at[5]),
        pltpu.make_async_copy(mat, mb, lsem.at[6]),
        pltpu.make_async_copy(vel, vb, lsem.at[7]),
    ]
    for load in small + columns + zloads + loads:
        load.start()

    def arrived(ref, sem):
        pltpu.make_async_copy(ref, ref, sem).wait()

    zlo, zhi = zin.at[pl.ds(0, 5)], zin.at[pl.ds(5, 4)]
    zero_row = jnp.zeros((2, cz, ny), jnp.float32)

    @pl.when(jnp.logical_not(has_left))
    def _():
        for f in range(3):
            sx[f, 0:2] = zero_row

    @pl.when(jnp.logical_not(has_right))
    def _():
        for f in range(3):
            sx[f, cx + 2 : cx + 4] = zero_row

    @pl.when(jnp.logical_not(has_below))
    def _():
        zin[0:5] = jnp.zeros((5, cx, ny), jnp.float32)

    @pl.when(jnp.logical_not(has_above))
    def _():
        zin[5:9] = jnp.zeros((4, cx, ny), jnp.float32)

    for j in range(n):
        if not near_at(j):

            @pl.when(jnp.logical_not(is_tile))
            def _():
                recv[j] = jnp.zeros(recv.shape[1:], jnp.float32)

    def x_copies(up):
        pairs = []
        for f, fields in ((0, 1), (1, 2)):
            if up:
                rows = 2 if f == 0 else 1
                src, dst, to = cx - rows, 2 - rows, me + 1
            else:
                rows = 1 if f == 0 else 2
                src, dst, to = 0, cx + 2, me - 1
            slot = 0 if up else 1
            pairs.append(
                pltpu.make_async_remote_copy(
                    src_ref=st.at[pl.ds(3 * f, fields), pl.ds(src, rows)],
                    dst_ref=sx.at[pl.ds(f, fields), pl.ds(dst, rows)],
                    send_sem=xsend.at[slot],
                    recv_sem=xrecv.at[slot],
                    device_id=(to, dep),
                    device_id_type=MESH,
                )
            )
        return pairs

    def z_copy(up):
        return pltpu.make_async_remote_copy(
            src_ref=zout.at[pl.ds(0, 5)] if up else zout.at[pl.ds(5, 4)],
            dst_ref=zlo if up else zhi,
            send_sem=zsend.at[0 if up else 1],
            recv_sem=zrecv.at[0 if up else 1],
            device_id=(me, dep + 1 if up else dep - 1),
            device_id_type=MESH,
        )

    def pack_copy(j):
        return pltpu.make_async_remote_copy(
            src_ref=packs.at[min(max(j - first_tile, 0), tiles - 1)],
            dst_ref=recv.at[me],
            send_sem=psend,
            recv_sem=precv,
            device_id=(j, dep),
            device_id_type=MESH,
        )

    def pack_next():
        for j in range(1, n):

            @pl.when(jnp.logical_and(j == me + 1, sends_to(j)))
            def _():
                pack_copy(j).start()

            @pl.when(jnp.logical_and(j == me + 1, halo_to(j)))
            def _():
                halo_copy(j).start()

    def halo_copy(j):
        return pltpu.make_async_remote_copy(
            src_ref=st.at[0, 0, :, pl.ds(row, 128)],
            dst_ref=halo,
            send_sem=hsend,
            recv_sem=hrecv,
            device_id=(j, dep),
            device_id_type=MESH,
        )

    earlier = has_below.astype(jnp.int32) + paired.astype(jnp.int32)
    for j in range(n):
        earlier = earlier + jnp.logical_and(j < me, partner(j)).astype(jnp.int32)
    late = me > last

    fast = jnp.logical_or(me == 0, me % 2 == 1)

    def enter():
        @pl.when(earlier > 0)
        def _():
            pl.semaphore_wait(barrier, earlier)

        @pl.when(is_last)
        def _():
            for j in range(last):
                halo_copy(j).start()

        for j in range(n):
            told = jnp.logical_and(j < me - 1, reached_by(j))

            @pl.when(told)
            def _():
                pl.semaphore_signal(
                    far_in.at[late.astype(jnp.int32)],
                    inc=1,
                    device_id=(j, dep),
                    device_id_type=MESH,
                )

        @pl.when(jnp.logical_and(has_left, jnp.logical_not(pairs(me - 1))))
        def _():
            pl.semaphore_signal(next_in, inc=1, device_id=(me - 1, dep), device_id_type=MESH)

        @pl.when(has_below)
        def _():
            pl.semaphore_signal(depth_in, inc=1, device_id=(me, dep - 1), device_id_type=MESH)

        @pl.when(jnp.logical_and(has_left, fast))
        def _():
            for copy in x_copies(False):
                copy.start()

    with jax.named_scope("entry_fast"):
        pl.when(fast)(enter)

    lane = lax.broadcasted_iota(jnp.int32, (cz, wide), 1)
    lane_one = lax.broadcasted_iota(jnp.int32, (cz, 128), 1)
    my_tile = jnp.clip(me - first_tile, 0, tiles - 1)
    with jax.named_scope("params_wait"):
        for load in small:
            load.wait()
    with jax.named_scope("params"):
        blocks = [jnp.zeros((cz, wide), jnp.float32) for _ in range(tiles)]
        params = [pb[j].T for j in range(per)]
        for f in range(4):
            mine = jnp.full((cz, 128), 1.0, jnp.float32)
            for j in range(per):
                column = po[me * per + j]
                value = params[j][:, f : f + 1]
                mine = jnp.where(lane_one == cx + j, value, mine)
                for t in range(tiles):
                    local = column - t * cx
                    held = jnp.logical_and(local >= 0, local < cx)
                    place = jnp.where(held, f * cx + local, -1)
                    blocks[t] = jnp.where(lane == place, value, blocks[t])
            ownp[f] = mine
        for t in range(tiles):
            packs[t] = blocks[t]
    with jax.named_scope("column_wait"):
        arrived(col, lsem.at[2])
    with jax.named_scope("pack"):

        @pl.when(near)
        def _():
            base = 4 * cx + (me - first_tile) * cx
            normal = jnp.zeros((cz, wide), jnp.float32)
            shear = jnp.zeros((cz, wide), jnp.float32)
            for i in range(cx):
                here = lane == base + i
                normal = jnp.where(here, col[0, i, :, 0:1], normal)
                shear = jnp.where(here, col[1, i, :, 0:1], shear)
            dxx = C_ONE * (normal - pltpu.roll(normal, 1, 1)) + C_TWO * (
                pltpu.roll(normal, wide - 1, 1) - pltpu.roll(normal, 2, 1)
            )
            share = shear + 0.5 * dxx
            inside = jnp.logical_and(lane >= 4 * cx, lane < 4 * cx + fc)
            share = jnp.where(inside, share, 0.0)
            for t in range(tiles):
                packs[t] = packs[t] + share
            recv[me] = packs[my_tile]

        @pl.when(is_last)
        def _():
            halo[...] = col[0, 0]

    with jax.named_scope("entry_slow"):
        pl.when(jnp.logical_not(fast))(enter)

    for j in range(n):

        @pl.when(jnp.logical_and(j < me, sends_to(j)))
        def _():
            pack_copy(j).start()

    @pl.when(paired)
    def _():
        pack_next()

    @pl.when(jnp.logical_not(fast))
    def _():
        for copy in x_copies(False):
            copy.start()

    @pl.when(paired)
    def _():
        for copy in x_copies(True):
            copy.start()

    with jax.named_scope("z_loads"):
        arrived(zout, lsem.at[3])

    @pl.when(has_below)
    def _():
        z_copy(False).start()

    with jax.named_scope("loads"):
        arrived(sx.at[:, pl.ds(2, cx)], lsem.at[4])
        arrived(so, lsem.at[5])
        arrived(mb, lsem.at[6])
        arrived(vb, lsem.at[7])

    yi = lax.broadcasted_iota(jnp.int32, (cz, ny), 1)
    zi = lax.broadcasted_iota(jnp.int32, (cz, ny), 0)

    def y_at(field, offset):
        moved = pltpu.roll(field, (-offset) % ny, 1)
        keep = yi < ny - offset if offset > 0 else yi >= -offset
        return jnp.where(keep, moved, 0.0)

    def z_at(field):
        def at(offset):
            if offset == 0:
                return field
            moved = pltpu.roll(field, (-offset) % cz, 0)
            keep = zi < cz - offset if offset > 0 else zi >= -offset
            return jnp.where(keep, moved, 0.0)

        return at

    def minus(at):
        return C_ONE * (at(0) - at(-1)) + C_TWO * (at(1) - at(-2))

    def plus(at):
        return C_ONE * (at(1) - at(0)) + C_TWO * (at(2) - at(-1))

    def along_x(f, x):
        return lambda offset: sx[f, x + 2 + offset]

    def along_y(field):
        return lambda offset: field if offset == 0 else y_at(field, offset)

    def buoyancy(x):
        material = mb[x]
        b = jnp.full((cz, ny), 0.25 * BUOY[0], jnp.float32)
        for index in range(1, 4):
            b = jnp.where(material == index, 0.25 * BUOY[index], b)
        bb[x] = b
        return b

    def across(x):
        return minus(along_x(0, x)), plus(along_x(1, x)), plus(along_x(2, x))

    def local(x):
        sxz, szz, syz = sx[2, x + 2], so[1, x], so[2, x]
        return (
            minus(along_y(sx[1, x + 2])) + minus(z_at(sxz)),
            plus(along_y(so[0, x])) + minus(z_at(syz)),
            plus(along_y(syz)) + plus(z_at(szz)),
        )

    def inner(x, carry):
        b, along, rest = buoyancy(x), across(x), local(x)
        for c in range(3):
            out[c, x] = vb[c, x] + b * (along[c] + rest[c])
        return carry

    def outer(x):
        b, rest = buoyancy(x), local(x)
        for c in range(3):
            out[c, x] = vb[c, x] + b * rest[c]

    edges = (0, 1, cx - 2, cx - 1)
    with jax.named_scope("outer"):
        for x in edges:
            outer(x)

    with jax.named_scope("wait_next"):

        @pl.when(jnp.logical_and(has_right, jnp.logical_not(paired)))
        def _():
            pl.semaphore_wait(next_in, 1)
            pack_next()
            for copy in x_copies(True):
                copy.start()

        @pl.when(has_above)
        def _():
            pl.semaphore_wait(depth_in, 1)
            z_copy(True).start()

    middle = cx // 2
    with jax.named_scope("inner"):
        lax.fori_loop(2, middle, inner, 0)

    def send_far(low, high, kind):
        group = [
            (j, jnp.logical_and(j > me + 1, reaches(j))) for j in range(low, high)
        ]
        count = sum(on.astype(jnp.int32) for _, on in group)

        @pl.when(count > 0)
        def _():
            pl.semaphore_wait(far_in.at[kind], count)

        for j, on in group:

            @pl.when(jnp.logical_and(on, sends_to(j)))
            def _():
                pack_copy(j).start()

            @pl.when(jnp.logical_and(on, halo_to(j)))
            def _():
                halo_copy(j).start()

    with jax.named_scope("wait_far"):
        send_far(2, last + 1, 0)
    with jax.named_scope("inner2"):
        lax.fori_loop(middle, cx - 2, inner, 0)
    with jax.named_scope("wait_far2"):
        send_far(last + 1, n, 1)

    with jax.named_scope("z_wait"):

        @pl.when(has_below)
        def _():
            z_copy(True).wait_recv()

        @pl.when(has_above)
        def _():
            z_copy(False).wait_recv()

    first = lax.broadcasted_iota(jnp.int32, (8, ny), 0)

    def face(x, carry):
        def low(k):
            return zin[k, pl.ds(x, 1), :]

        def high(k):
            return zin[5 + k, pl.ds(x, 1), :]

        def put(at, one, two):
            return jnp.where(first == at, one, jnp.where(first == two[0], two[1], 0.0))

        b = bb[x, 0:8]
        out[0, x, 0:8] -= b * put(0, C_ONE * low(1) + C_TWO * low(0), (1, C_TWO * low(1)))
        out[1, x, 0:8] -= b * put(0, C_ONE * low(3) + C_TWO * low(2), (1, C_TWO * low(3)))
        out[2, x, 0:8] -= b * jnp.where(first == 0, C_TWO * low(4), 0.0)
        b = bb[x, cz - 8 : cz]
        out[0, x, cz - 8 : cz] += b * jnp.where(first == 7, C_TWO * high(0), 0.0)
        out[1, x, cz - 8 : cz] += b * jnp.where(first == 7, C_TWO * high(1), 0.0)
        out[2, x, cz - 8 : cz] += b * put(
            7, C_ONE * high(2) + C_TWO * high(3), (6, C_TWO * high(2))
        )
        return carry

    with jax.named_scope("face"):
        lax.fori_loop(0, cx, face, 0)

    with jax.named_scope("pack_wait"):
        @pl.when(is_tile)
        def _():
            arrived(recv.at[pl.ds(0, n - 1)], precv)

        @pl.when(me == first_tile - 1)
        def _():
            arrived(recv.at[pl.ds(0, tiles)], precv)

        @pl.when(jnp.logical_not(near))
        def _():
            arrived(recv.at[pl.ds(0, tiles + 1)], precv)

        @pl.when(jnp.logical_not(is_last))
        def _():
            arrived(halo, hrecv)

    with jax.named_scope("friction"):
        total = recv[first_tile - 1]
        for j in range(n):
            if j != first_tile - 1:
                total = total + recv[j]
        edge = 0.5 * C_TWO * halo[:, 0:1]
        total = total + jnp.where(lane == 4 * cx + fc - 1, edge, 0.0)
        used = lane_one < cx
        fields = []
        for f in range(4):
            moved = total if f == 0 else pltpu.roll(total, wide - f * cx, 1)
            fields.append(jnp.where(used, moved[:, :128], ownp[f]))
        tau = jnp.zeros((cz, 128), jnp.float32)
        for t in range(tiles):
            moved = pltpu.roll(total, wide - (4 + t) * cx, 1)[:, :128]
            tau = jnp.where(jnp.logical_and(used, my_tile == t), moved, tau)
        for j in range(per):
            picked = jnp.where(lane == 4 * cx + po[me * per + j], total, 0.0)
            tau = jnp.where(
                lane_one == cx + j, jnp.sum(picked, axis=1, keepdims=True), tau
            )
        fields = [tau + fields[3]] + fields[:3]
        for k in range(4):
            state[k] = fields[k]

        @pl.when(is_tile)
        def _():
            rates[...] = 0.5 * friction(*fields)

    def fix(columns):
        parts = []
        for i in columns:
            low = out[0, i, :, row - 128 : row]
            high = out[0, i, :, row : row + 128]
            middle = 0.5 * (high + pltpu.roll(low, 1, 1))
            s = rates[:, i : i + 1]
            above = jnp.where(lane_one == 0, middle + s, high)
            below = jnp.where(lane_one == 127, pltpu.roll(middle, 127, 1) - s, low)
            parts.append((i, below, above))
        for i, below, above in parts:
            out[0, i, :, row - 128 : row] = below
            out[0, i, :, row : row + 128] = above

    with jax.named_scope("fix"):

        @pl.when(is_tile)
        def _():
            for i in range(2, cx - 2, 4):
                fix(range(i, min(i + 4, cx - 2)))

    with jax.named_scope("x_wait"):

        @pl.when(has_left)
        def _():
            arrived(sx.at[0, pl.ds(0, 4)], xrecv.at[0])

        @pl.when(has_right)
        def _():
            arrived(sx.at[0, pl.ds(0, 5)], xrecv.at[1])

    with jax.named_scope("edges"):
        for x in edges:
            along = across(x)
            for c in range(3):
                out[c, x] += bb[x] * along[c]

    with jax.named_scope("fix2"):

        @pl.when(is_tile)
        def _():
            fix(edges)

    with jax.named_scope("sends_done"):
        @pl.when(near)
        def _():
            arrived(recv.at[pl.ds(0, n - 1)], psend)

        @pl.when(jnp.logical_not(near))
        def _():
            arrived(recv.at[pl.ds(0, tiles)], psend)

        @pl.when(is_last)
        def _():
            arrived(recv.at[pl.ds(0, n - 1), :, pl.ds(0, 128)], hsend)

        @pl.when(has_above)
        def _():
            z_copy(True).wait_send()

        @pl.when(has_below)
        def _():
            z_copy(False).wait_send()

        @pl.when(has_right)
        def _():
            arrived(sx.at[0, pl.ds(0, 4)], xsend.at[0])

        @pl.when(has_left)
        def _():
            arrived(sx.at[0, pl.ds(0, 5)], xsend.at[1])


def write_out(first, held, state, out, slip_out, slip, sem):
    velocity = pltpu.make_async_copy(held, out, sem.at[0])
    velocity.start()
    rate = friction(state[0], state[1], state[2], state[3])
    slip[...] = rate.T[first : first + slip.shape[0]]
    rates = pltpu.make_async_copy(slip, slip_out, sem.at[1])
    rates.start()
    velocity.wait()
    rates.wait()


def per_device(n, nd, velocity, stress, material, patch_order, fault_params):
    _, cx, cz, ny = stress.shape
    fc = patch_order.shape[0]
    per = fc // n
    wide = -(-(4 * cx + fc + 2) // 128) * 128
    dims = (n, nd, cx, cz, ny, fc, wide)
    tiles = fc // cx
    f32 = jnp.float32
    anywhere = pl.BlockSpec(memory_space=pltpu.HBM)
    dma = pltpu.SemaphoreType.DMA
    params = jnp.transpose(fault_params, (2, 0, 1))
    big = (velocity, stress, material, patch_order, params)
    held = pl.pallas_call(
        functools.partial(kernel, dims),
        out_shape=(
            jax.ShapeDtypeStruct(velocity.shape, f32),
            jax.ShapeDtypeStruct((4, cz, 128), f32),
        ),
        in_specs=[anywhere] * 5,
        out_specs=(pl.BlockSpec(memory_space=pltpu.VMEM), pl.BlockSpec(memory_space=pltpu.VMEM)),
        scratch_shapes=[
            pltpu.SMEM((fc,), jnp.int32),
            pltpu.VMEM((2, cx, cz, 128), f32),
            pltpu.VMEM((3, cx + 4, cz, ny), f32),
            pltpu.VMEM((3, cx, cz, ny), f32),
            pltpu.VMEM((3, cx, cz, ny), f32),
            pltpu.VMEM((cx, cz, ny), jnp.int32),
            pltpu.VMEM((cx, cz, ny), f32),
            pltpu.VMEM((per, 4, cz), f32),
            pltpu.VMEM((4, cz, 128), f32),
            pltpu.VMEM((9, cx, ny), f32),
            pltpu.VMEM((9, cx, ny), f32),
            pltpu.VMEM((tiles, cz, wide), f32),
            pltpu.VMEM((n, cz, wide), f32),
            pltpu.VMEM((cz, 128), f32),
            pltpu.VMEM((cz, 128), f32),
            dma((8,)),
            dma,
            dma,
            dma,
            dma,
            dma((2,)),
            dma((2,)),
            dma((2,)),
            dma((2,)),
            pltpu.SemaphoreType.REGULAR,
            pltpu.SemaphoreType.REGULAR((2,)),
            pltpu.SemaphoreType.REGULAR,
        ],
        compiler_params=pltpu.CompilerParams(collective_id=0, has_side_effects=True, vmem_limit_bytes=12 << 20),
    )(*[pltpu.with_memory_space_constraint(v, pltpu.HBM) for v in big])
    resident = pl.BlockSpec(memory_space=pltpu.VMEM)
    moved, slip = pl.pallas_call(
        functools.partial(write_out, cx),
        out_shape=(
            jax.ShapeDtypeStruct(velocity.shape, f32),
            jax.ShapeDtypeStruct((per, cz), f32),
        ),
        in_specs=[resident, resident],
        out_specs=(anywhere, anywhere),
        scratch_shapes=[pltpu.VMEM((per, cz), f32), dma((2,))],
        compiler_params=pltpu.CompilerParams(vmem_limit_bytes=4 << 20),
    )(*held)
    return moved, slip.T


def solution(mesh):
    n, nd = mesh.shape["strike"], mesh.shape["depth"]
    return jax.shard_map(
        functools.partial(per_device, n, nd),
        mesh=mesh,
        in_specs=(
            P(None, "strike", "depth", None),
            P(None, "strike", "depth", None),
            P("strike", "depth", None),
            P(),
            P(None, "depth", "strike"),
        ),
        out_specs=(P(None, "strike", "depth", None), P("depth", "strike")),
        check_vma=False,
    )
```

```python
import functools

import jax
import jax.numpy as jnp
from jax import lax
from jax.experimental import pallas as pl
from jax.experimental.pallas import tpu as pltpu
from jax.sharding import PartitionSpec as P

NEWTON = 8
BUOY = (1.0, 0.8, 0.6, 1.25)
C_ONE = 9.0 / 8.0
C_TWO = -1.0 / 24.0
MESH = pl.DeviceIdType.MESH


def friction(tau_total, coef, psi, normal_stress):
    half_q = 0.5 * jnp.exp(psi / coef)
    scale = normal_stress * coef
    stiff = scale * half_q
    rate = 0.35 * tau_total / (1.0 + stiff)
    for _ in range(NEWTON - 1):
        arg_val = rate * half_q
        square = 1.0 + arg_val * arg_val
        inverse = lax.rsqrt(square)
        magnitude = jnp.log(jnp.abs(arg_val) + square * inverse)
        resid = tau_total - rate - scale * jnp.where(arg_val < 0, -magnitude, magnitude)
        rate = rate + 0.35 * resid / (1.0 + stiff * inverse)
    return rate


def kernel(
    dims, vel, st, mat, order, fp, out, state,
    po, col, sx, so, vb, mb, bb, pb, ownp, zout, zin, packs, recv, halo, rates,
    lsem, psend, precv, hsend, hrecv, xsend, xrecv, zsend, zrecv, next_in, far_in, depth_in,
):
    n, nd, cx, cz, ny, fc, wide = dims
    row = ny // 2
    per = fc // n
    first_tile = n // 4
    tiles = fc // cx
    me = lax.axis_index("strike")
    dep = lax.axis_index("depth")
    has_left, has_right = me > 0, me < n - 1
    has_below, has_above = dep > 0, dep < nd - 1
    is_tile = jnp.logical_and(me >= first_tile, me < first_tile + tiles)
    near = jnp.logical_and(me >= first_tile - 1, me < first_tile + tiles)

    def tile_at(j):
        return first_tile <= j < first_tile + tiles

    def near_at(j):
        return first_tile - 1 <= j < first_tile + tiles

    last = first_tile + tiles
    is_last = me == last

    def pairs(j):
        inside = jnp.logical_and(j >= first_tile, j < last - 2)
        return jnp.logical_or(j == 0, jnp.logical_and(j % 2 == 0, inside))

    paired = pairs(me)

    def sends_to(j):
        return jnp.logical_and(me != j, jnp.logical_or(near, tile_at(j)))

    def halo_to(j):
        return jnp.logical_and(is_last, me != j)

    def reaches(j):
        return jnp.logical_or(sends_to(j), halo_to(j))

    def reached_by(j):
        return jnp.logical_and(me != j, jnp.logical_or(is_tile, near_at(j) or j == last))

    def partner(j):
        beside = jnp.logical_or(me == j - 1, me == j + 1)
        return jnp.logical_or(beside, jnp.logical_or(reaches(j), reached_by(j)))

    barrier = pltpu.get_barrier_semaphore()
    for j in range(n):

        back = jnp.logical_and(j == me - 1, pairs(j))

        @pl.when(jnp.logical_or(jnp.logical_and(j > me, partner(j)), back))
        def _():
            pl.semaphore_signal(barrier, inc=1, device_id=(j, dep), device_id_type=MESH)

    @pl.when(has_above)
    def _():
        pl.semaphore_signal(barrier, inc=1, device_id=(me, dep + 1), device_id_type=MESH)

    step = cx // 4
    columns = [
        pltpu.make_async_copy(
            st.at[3 * f, pl.ds(k * step, step), :, pl.ds(row, 128)],
            col.at[f, pl.ds(k * step, step)],
            lsem.at[2],
        )
        for k in range(4)
        for f in range(2)
    ]
    small = [
        pltpu.make_async_copy(order, po, lsem.at[0]),
        pltpu.make_async_copy(fp, pb, lsem.at[1]),
    ]
    z_rows = (
        (4, cz - 2), (4, cz - 1), (5, cz - 2), (5, cz - 1), (2, cz - 1),
        (4, 0), (5, 0), (2, 0), (2, 1),
    )
    zloads = [
        pltpu.make_async_copy(st.at[f, :, r], zout.at[k], lsem.at[3])
        for k, (f, r) in enumerate(z_rows)
    ]
    loads = [
        pltpu.make_async_copy(st.at[0], sx.at[0, pl.ds(2, cx)], lsem.at[4]),
        pltpu.make_async_copy(
            st.at[pl.ds(3, 2)], sx.at[pl.ds(1, 2), pl.ds(2, cx)], lsem.at[4]
        ),
        pltpu.make_async_copy(st.at[pl.ds(1, 2)], so.at[pl.ds(0, 2)], lsem.at[5]),
        pltpu.make_async_copy(st.at[5], so.at[2], lsem.at[5]),
        pltpu.make_async_copy(mat, mb, lsem.at[6]),
        pltpu.make_async_copy(vel, vb, lsem.at[7]),
    ]
    for load in small + columns + zloads + loads:
        load.start()

    def arrived(ref, sem):
        pltpu.make_async_copy(ref, ref, sem).wait()

    zlo, zhi = zin.at[pl.ds(0, 5)], zin.at[pl.ds(5, 4)]
    zero_row = jnp.zeros((2, cz, ny), jnp.float32)

    @pl.when(jnp.logical_not(has_left))
    def _():
        for f in range(3):
            sx[f, 0:2] = zero_row

    @pl.when(jnp.logical_not(has_right))
    def _():
        for f in range(3):
            sx[f, cx + 2 : cx + 4] = zero_row

    @pl.when(jnp.logical_not(has_below))
    def _():
        zin[0:5] = jnp.zeros((5, cx, ny), jnp.float32)

    @pl.when(jnp.logical_not(has_above))
    def _():
        zin[5:9] = jnp.zeros((4, cx, ny), jnp.float32)

    for j in range(n):
        if not near_at(j):

            @pl.when(jnp.logical_not(is_tile))
            def _():
                recv[j] = jnp.zeros(recv.shape[1:], jnp.float32)

    def x_copies(up):
        pairs = []
        for f, fields in ((0, 1), (1, 2)):
            if up:
                rows = 2 if f == 0 else 1
                src, dst, to = cx - rows, 2 - rows, me + 1
            else:
                rows = 1 if f == 0 else 2
                src, dst, to = 0, cx + 2, me - 1
            slot = 0 if up else 1
            pairs.append(
                pltpu.make_async_remote_copy(
                    src_ref=st.at[pl.ds(3 * f, fields), pl.ds(src, rows)],
                    dst_ref=sx.at[pl.ds(f, fields), pl.ds(dst, rows)],
                    send_sem=xsend.at[slot],
                    recv_sem=xrecv.at[slot],
                    device_id=(to, dep),
                    device_id_type=MESH,
                )
            )
        return pairs

    def z_copy(up):
        return pltpu.make_async_remote_copy(
            src_ref=zout.at[pl.ds(0, 5)] if up else zout.at[pl.ds(5, 4)],
            dst_ref=zlo if up else zhi,
            send_sem=zsend.at[0 if up else 1],
            recv_sem=zrecv.at[0 if up else 1],
            device_id=(me, dep + 1 if up else dep - 1),
            device_id_type=MESH,
        )

    def pack_copy(j):
        return pltpu.make_async_remote_copy(
            src_ref=packs.at[min(max(j - first_tile, 0), tiles - 1)],
            dst_ref=recv.at[me],
            send_sem=psend,
            recv_sem=precv,
            device_id=(j, dep),
            device_id_type=MESH,
        )

    def pack_next():
        for j in range(1, n):

            @pl.when(jnp.logical_and(j == me + 1, sends_to(j)))
            def _():
                pack_copy(j).start()

            @pl.when(jnp.logical_and(j == me + 1, halo_to(j)))
            def _():
                halo_copy(j).start()

    def halo_copy(j):
        return pltpu.make_async_remote_copy(
            src_ref=st.at[0, 0, :, pl.ds(row, 128)],
            dst_ref=halo,
            send_sem=hsend,
            recv_sem=hrecv,
            device_id=(j, dep),
            device_id_type=MESH,
        )

    earlier = has_below.astype(jnp.int32) + paired.astype(jnp.int32)
    for j in range(n):
        earlier = earlier + jnp.logical_and(j < me, partner(j)).astype(jnp.int32)
    late = me > last

    fast = me % 2 == 1

    def enter():
        @pl.when(earlier > 0)
        def _():
            pl.semaphore_wait(barrier, earlier)

        @pl.when(is_last)
        def _():
            for j in range(last):
                halo_copy(j).start()

        for j in range(n):
            told = jnp.logical_and(j < me - 1, reached_by(j))

            @pl.when(told)
            def _():
                pl.semaphore_signal(
                    far_in.at[late.astype(jnp.int32)],
                    inc=1,
                    device_id=(j, dep),
                    device_id_type=MESH,
                )

        @pl.when(jnp.logical_and(has_left, jnp.logical_not(pairs(me - 1))))
        def _():
            pl.semaphore_signal(next_in, inc=1, device_id=(me - 1, dep), device_id_type=MESH)

        @pl.when(has_below)
        def _():
            pl.semaphore_signal(depth_in, inc=1, device_id=(me, dep - 1), device_id_type=MESH)

        @pl.when(jnp.logical_and(has_left, fast))
        def _():
            for copy in x_copies(False):
                copy.start()

    with jax.named_scope("entry_fast"):
        pl.when(fast)(enter)

    lane = lax.broadcasted_iota(jnp.int32, (cz, wide), 1)
    lane_one = lax.broadcasted_iota(jnp.int32, (cz, 128), 1)
    my_tile = jnp.clip(me - first_tile, 0, tiles - 1)
    with jax.named_scope("params_wait"):
        for load in small:
            load.wait()
    with jax.named_scope("params"):
        blocks = [jnp.zeros((cz, wide), jnp.float32) for _ in range(tiles)]
        params = [pb[j].T for j in range(per)]
        for f in range(4):
            mine = jnp.full((cz, 128), 1.0, jnp.float32)
            for j in range(per):
                column = po[me * per + j]
                value = params[j][:, f : f + 1]
                mine = jnp.where(lane_one == cx + j, value, mine)
                for t in range(tiles):
                    local = column - t * cx
                    held = jnp.logical_and(local >= 0, local < cx)
                    place = jnp.where(held, f * cx + local, -1)
                    blocks[t] = jnp.where(lane == place, value, blocks[t])
            ownp[f] = mine
        for t in range(tiles):
            packs[t] = blocks[t]
    with jax.named_scope("column_wait"):
        arrived(col, lsem.at[2])
    with jax.named_scope("pack"):

        @pl.when(near)
        def _():
            base = 4 * cx + (me - first_tile) * cx
            normal = jnp.zeros((cz, wide), jnp.float32)
            shear = jnp.zeros((cz, wide), jnp.float32)
            for i in range(cx):
                here = lane == base + i
                normal = jnp.where(here, col[0, i, :, 0:1], normal)
                shear = jnp.where(here, col[1, i, :, 0:1], shear)
            dxx = C_ONE * (normal - pltpu.roll(normal, 1, 1)) + C_TWO * (
                pltpu.roll(normal, wide - 1, 1) - pltpu.roll(normal, 2, 1)
            )
            share = shear + 0.5 * dxx
            inside = jnp.logical_and(lane >= 4 * cx, lane < 4 * cx + fc)
            share = jnp.where(inside, share, 0.0)
            for t in range(tiles):
                packs[t] = packs[t] + share
            recv[me] = packs[my_tile]

        @pl.when(is_last)
        def _():
            halo[...] = col[0, 0]

    with jax.named_scope("entry_slow"):
        pl.when(jnp.logical_not(fast))(enter)

    for j in range(n):

        @pl.when(jnp.logical_and(j < me, sends_to(j)))
        def _():
            pack_copy(j).start()

    @pl.when(paired)
    def _():
        pack_next()

    @pl.when(jnp.logical_and(has_left, jnp.logical_not(fast)))
    def _():
        for copy in x_copies(False):
            copy.start()

    @pl.when(paired)
    def _():
        for copy in x_copies(True):
            copy.start()

    with jax.named_scope("z_loads"):
        arrived(zout, lsem.at[3])

    @pl.when(has_below)
    def _():
        z_copy(False).start()

    with jax.named_scope("wait_next"):

        @pl.when(jnp.logical_and(has_right, jnp.logical_not(paired)))
        def _():
            pl.semaphore_wait(next_in, 1)
            pack_next()
            for copy in x_copies(True):
                copy.start()

        @pl.when(has_above)
        def _():
            pl.semaphore_wait(depth_in, 1)
            z_copy(True).start()

    with jax.named_scope("loads"):
        arrived(sx.at[:, pl.ds(2, cx)], lsem.at[4])
        arrived(so, lsem.at[5])
        arrived(mb, lsem.at[6])
        arrived(vb, lsem.at[7])

    yi = lax.broadcasted_iota(jnp.int32, (cz, ny), 1)
    zi = lax.broadcasted_iota(jnp.int32, (cz, ny), 0)

    def y_at(field, offset):
        moved = pltpu.roll(field, (-offset) % ny, 1)
        keep = yi < ny - offset if offset > 0 else yi >= -offset
        return jnp.where(keep, moved, 0.0)

    def z_at(field):
        def at(offset):
            if offset == 0:
                return field
            moved = pltpu.roll(field, (-offset) % cz, 0)
            keep = zi < cz - offset if offset > 0 else zi >= -offset
            return jnp.where(keep, moved, 0.0)

        return at

    def minus(at):
        return C_ONE * (at(0) - at(-1)) + C_TWO * (at(1) - at(-2))

    def plus(at):
        return C_ONE * (at(1) - at(0)) + C_TWO * (at(2) - at(-1))

    def along_x(f, x):
        return lambda offset: sx[f, x + 2 + offset]

    def along_y(field):
        return lambda offset: field if offset == 0 else y_at(field, offset)

    def buoyancy(x):
        material = mb[x]
        b = jnp.full((cz, ny), 0.25 * BUOY[0], jnp.float32)
        for index in range(1, 4):
            b = jnp.where(material == index, 0.25 * BUOY[index], b)
        bb[x] = b
        return b

    def across(x):
        return minus(along_x(0, x)), plus(along_x(1, x)), plus(along_x(2, x))

    def local(x):
        sxz, szz, syz = sx[2, x + 2], so[1, x], so[2, x]
        return (
            minus(along_y(sx[1, x + 2])) + minus(z_at(sxz)),
            plus(along_y(so[0, x])) + minus(z_at(syz)),
            plus(along_y(syz)) + plus(z_at(szz)),
        )

    def inner(x, carry):
        b, along, rest = buoyancy(x), across(x), local(x)
        for c in range(3):
            out[c, x] = vb[c, x] + b * (along[c] + rest[c])
        return carry

    def outer(x):
        b, rest = buoyancy(x), local(x)
        for c in range(3):
            out[c, x] = vb[c, x] + b * rest[c]

    edges = (0, 1, cx - 2, cx - 1)
    with jax.named_scope("outer"):
        for x in edges:
            outer(x)

    middle = cx // 2
    with jax.named_scope("inner"):
        lax.fori_loop(2, middle, inner, 0)

    def send_far(low, high, kind):
        group = [
            (j, jnp.logical_and(j > me + 1, reaches(j))) for j in range(low, high)
        ]
        count = sum(on.astype(jnp.int32) for _, on in group)

        @pl.when(count > 0)
        def _():
            pl.semaphore_wait(far_in.at[kind], count)

        for j, on in group:

            @pl.when(jnp.logical_and(on, sends_to(j)))
            def _():
                pack_copy(j).start()

            @pl.when(jnp.logical_and(on, halo_to(j)))
            def _():
                halo_copy(j).start()

    with jax.named_scope("wait_far"):
        send_far(2, last + 1, 0)
    with jax.named_scope("wait_far2"):
        send_far(last + 1, n, 1)

    with jax.named_scope("inner2"):
        lax.fori_loop(middle, cx - 2, inner, 0)
    with jax.named_scope("z_wait"):

        @pl.when(has_below)
        def _():
            z_copy(True).wait_recv()

        @pl.when(has_above)
        def _():
            z_copy(False).wait_recv()

    first = lax.broadcasted_iota(jnp.int32, (8, ny), 0)

    def face(x, carry):
        def low(k):
            return zin[k, pl.ds(x, 1), :]

        def high(k):
            return zin[5 + k, pl.ds(x, 1), :]

        def put(at, one, two):
            return jnp.where(first == at, one, jnp.where(first == two[0], two[1], 0.0))

        b = bb[x, 0:8]
        out[0, x, 0:8] -= b * put(0, C_ONE * low(1) + C_TWO * low(0), (1, C_TWO * low(1)))
        out[1, x, 0:8] -= b * put(0, C_ONE * low(3) + C_TWO * low(2), (1, C_TWO * low(3)))
        out[2, x, 0:8] -= b * jnp.where(first == 0, C_TWO * low(4), 0.0)
        b = bb[x, cz - 8 : cz]
        out[0, x, cz - 8 : cz] += b * jnp.where(first == 7, C_TWO * high(0), 0.0)
        out[1, x, cz - 8 : cz] += b * jnp.where(first == 7, C_TWO * high(1), 0.0)
        out[2, x, cz - 8 : cz] += b * put(
            7, C_ONE * high(2) + C_TWO * high(3), (6, C_TWO * high(2))
        )
        return carry

    with jax.named_scope("face"):
        lax.fori_loop(0, cx, face, 0)

    inside_columns = tuple(range(2, cx - 2))

    def level(columns):
        for start in range(0, len(columns), 4):
            parts = []
            for i in columns[start : start + 4]:
                low = out[0, i, :, row - 128 : row]
                high = out[0, i, :, row : row + 128]
                mean = 0.5 * (high + pltpu.roll(low, 1, 1))
                low = jnp.where(lane_one == 127, pltpu.roll(mean, 127, 1), low)
                parts.append((i, low, jnp.where(lane_one == 0, mean, high)))
            for i, low, high in parts:
                out[0, i, :, row - 128 : row] = low
                out[0, i, :, row : row + 128] = high

    with jax.named_scope("mean"):

        @pl.when(is_tile)
        def _():
            level(inside_columns)

    with jax.named_scope("pack_wait"):
        @pl.when(is_tile)
        def _():
            arrived(recv.at[pl.ds(0, n - 1)], precv)

        @pl.when(me == first_tile - 1)
        def _():
            arrived(recv.at[pl.ds(0, tiles)], precv)

        @pl.when(jnp.logical_not(near))
        def _():
            arrived(recv.at[pl.ds(0, tiles + 1)], precv)

        @pl.when(jnp.logical_not(is_last))
        def _():
            arrived(halo, hrecv)

    with jax.named_scope("friction"):
        total = recv[first_tile - 1]
        for j in range(n):
            if j != first_tile - 1:
                total = total + recv[j]
        edge = 0.5 * C_TWO * halo[:, 0:1]
        total = total + jnp.where(lane == 4 * cx + fc - 1, edge, 0.0)
        own = jnp.zeros((cz, 128), jnp.float32)
        for j in range(per):
            picked = jnp.where(lane == 4 * cx + po[me * per + j], total, 0.0)
            own = jnp.where(
                lane_one == cx + j, jnp.sum(picked, axis=1, keepdims=True), own
            )
        state[0] = own + ownp[3]
        for k in range(3):
            state[1 + k] = ownp[k]

        @pl.when(is_tile)
        def _():
            fields = [total[:, :128]]
            for f in range(1, 4):
                fields.append(pltpu.roll(total, wide - f * cx, 1)[:, :128])
            used = lane_one < cx
            fields = [jnp.where(used, field, 1.0) for field in fields]
            tau = fields[3]
            for t in range(tiles):
                moved = pltpu.roll(total, wide - (4 + t) * cx, 1)[:, :128]
                tau = tau + jnp.where(jnp.logical_and(used, my_tile == t), moved, 0.0)
            rates[...] = 0.5 * friction(tau, *fields[:3])

    def fix(columns):
        for start in range(0, len(columns), 4):
            parts = []
            for i in columns[start : start + 4]:
                s = rates[:, i : i + 1]
                low = out[0, i, :, row - 128 : row]
                high = out[0, i, :, row : row + 128]
                low = low - jnp.where(lane_one == 127, s, 0.0)
                high = high + jnp.where(lane_one == 0, s, 0.0)
                parts.append((i, low, high))
            for i, low, high in parts:
                out[0, i, :, row - 128 : row] = low
                out[0, i, :, row : row + 128] = high

    with jax.named_scope("fix"):

        @pl.when(is_tile)
        def _():
            fix(inside_columns)

    with jax.named_scope("x_wait"):

        @pl.when(has_left)
        def _():
            arrived(sx.at[0, pl.ds(0, 4)], xrecv.at[0])

        @pl.when(has_right)
        def _():
            arrived(sx.at[0, pl.ds(0, 5)], xrecv.at[1])

    with jax.named_scope("edges"):
        for x in edges:
            along = across(x)
            for c in range(3):
                out[c, x] += bb[x] * along[c]

    with jax.named_scope("fix2"):

        @pl.when(is_tile)
        def _():
            level(edges)
            fix(edges)

    with jax.named_scope("sends_done"):
        @pl.when(near)
        def _():
            arrived(recv.at[pl.ds(0, n - 1)], psend)

        @pl.when(jnp.logical_not(near))
        def _():
            arrived(recv.at[pl.ds(0, tiles)], psend)

        @pl.when(is_last)
        def _():
            arrived(recv.at[pl.ds(0, n - 1), :, pl.ds(0, 128)], hsend)

        @pl.when(has_above)
        def _():
            z_copy(True).wait_send()

        @pl.when(has_below)
        def _():
            z_copy(False).wait_send()

        @pl.when(has_right)
        def _():
            arrived(sx.at[0, pl.ds(0, 4)], xsend.at[0])

        @pl.when(has_left)
        def _():
            arrived(sx.at[0, pl.ds(0, 5)], xsend.at[1])


def write_out(first, held, state, out, slip_out, slip, sem):
    velocity = pltpu.make_async_copy(held, out, sem.at[0])
    velocity.start()
    rate = friction(state[0], state[1], state[2], state[3])
    slip[...] = rate.T[first : first + slip.shape[0]]
    rates = pltpu.make_async_copy(slip, slip_out, sem.at[1])
    rates.start()
    velocity.wait()
    rates.wait()


def per_device(n, nd, velocity, stress, material, patch_order, fault_params):
    _, cx, cz, ny = stress.shape
    fc = patch_order.shape[0]
    per = fc // n
    wide = -(-(4 * cx + fc + 2) // 128) * 128
    dims = (n, nd, cx, cz, ny, fc, wide)
    tiles = fc // cx
    f32 = jnp.float32
    anywhere = pl.BlockSpec(memory_space=pltpu.HBM)
    dma = pltpu.SemaphoreType.DMA
    params = jnp.transpose(fault_params, (2, 0, 1))
    big = (velocity, stress, material, patch_order, params)
    held = pl.pallas_call(
        functools.partial(kernel, dims),
        out_shape=(
            jax.ShapeDtypeStruct(velocity.shape, f32),
            jax.ShapeDtypeStruct((4, cz, 128), f32),
        ),
        in_specs=[anywhere] * 5,
        out_specs=(pl.BlockSpec(memory_space=pltpu.VMEM), pl.BlockSpec(memory_space=pltpu.VMEM)),
        scratch_shapes=[
            pltpu.SMEM((fc,), jnp.int32),
            pltpu.VMEM((2, cx, cz, 128), f32),
            pltpu.VMEM((3, cx + 4, cz, ny), f32),
            pltpu.VMEM((3, cx, cz, ny), f32),
            pltpu.VMEM((3, cx, cz, ny), f32),
            pltpu.VMEM((cx, cz, ny), jnp.int32),
            pltpu.VMEM((cx, cz, ny), f32),
            pltpu.VMEM((per, 4, cz), f32),
            pltpu.VMEM((4, cz, 128), f32),
            pltpu.VMEM((9, cx, ny), f32),
            pltpu.VMEM((9, cx, ny), f32),
            pltpu.VMEM((tiles, cz, wide), f32),
            pltpu.VMEM((n, cz, wide), f32),
            pltpu.VMEM((cz, 128), f32),
            pltpu.VMEM((cz, 128), f32),
            dma((8,)),
            dma,
            dma,
            dma,
            dma,
            dma((2,)),
            dma((2,)),
            dma((2,)),
            dma((2,)),
            pltpu.SemaphoreType.REGULAR,
            pltpu.SemaphoreType.REGULAR((2,)),
            pltpu.SemaphoreType.REGULAR,
        ],
        compiler_params=pltpu.CompilerParams(collective_id=0, has_side_effects=True, vmem_limit_bytes=12 << 20),
    )(*[pltpu.with_memory_space_constraint(v, pltpu.HBM) for v in big])
    resident = pl.BlockSpec(memory_space=pltpu.VMEM)
    moved, slip = pl.pallas_call(
        functools.partial(write_out, cx),
        out_shape=(
            jax.ShapeDtypeStruct(velocity.shape, f32),
            jax.ShapeDtypeStruct((per, cz), f32),
        ),
        in_specs=[resident, resident],
        out_specs=(anywhere, anywhere),
        scratch_shapes=[pltpu.VMEM((per, cz), f32), dma((2,))],
        compiler_params=pltpu.CompilerParams(vmem_limit_bytes=4 << 20),
    )(*held)
    return moved, slip.T


def solution(mesh):
    n, nd = mesh.shape["strike"], mesh.shape["depth"]
    return jax.shard_map(
        functools.partial(per_device, n, nd),
        mesh=mesh,
        in_specs=(
            P(None, "strike", "depth", None),
            P(None, "strike", "depth", None),
            P("strike", "depth", None),
            P(),
            P(None, "depth", "strike"),
        ),
        out_specs=(P(None, "strike", "depth", None), P("depth", "strike")),
        check_vma=False,
    )
```

```python
import functools

import jax
import jax.numpy as jnp
from jax import lax
from jax.experimental import pallas as pl
from jax.experimental.pallas import tpu as pltpu
from jax.sharding import PartitionSpec as P

NEWTON = 8
BUOY = (1.0, 0.8, 0.6, 1.25)
C_ONE = 9.0 / 8.0
C_TWO = -1.0 / 24.0
MESH = pl.DeviceIdType.MESH


def friction(tau_total, coef, psi, normal_stress):
    half_q = 0.5 * jnp.exp(psi / coef)
    scale = normal_stress * coef
    stiff = scale * half_q
    rate = 0.35 * tau_total / (1.0 + stiff)
    for _ in range(NEWTON - 1):
        arg_val = rate * half_q
        square = 1.0 + arg_val * arg_val
        inverse = lax.rsqrt(square)
        magnitude = jnp.log(jnp.abs(arg_val) + square * inverse)
        resid = tau_total - rate - scale * jnp.where(arg_val < 0, -magnitude, magnitude)
        rate = rate + 0.35 * resid / (1.0 + stiff * inverse)
    return rate


def kernel(
    dims, vel, st, mat, order, fp, out, state,
    po, col, sx, so, vb, mb, bb, pb, ownp, zout, zin, packs, recv, halo, rates, picks,
    lsem, psend, precv, hsend, hrecv, xsend, xrecv, zsend, zrecv, next_in, far_in, depth_in, core_in,
):
    n, nd, cx, cz, ny, fc, wide = dims
    row = ny // 2
    per = fc // n
    first_tile = n // 4
    tiles = fc // cx
    me = lax.axis_index("strike")
    dep = lax.axis_index("depth")
    has_left, has_right = me > 0, me < n - 1
    has_below, has_above = dep > 0, dep < nd - 1
    is_tile = jnp.logical_and(me >= first_tile, me < first_tile + tiles)
    near = jnp.logical_and(me >= first_tile - 1, me < first_tile + tiles)

    def tile_at(j):
        return first_tile <= j < first_tile + tiles

    def near_at(j):
        return first_tile - 1 <= j < first_tile + tiles

    last = first_tile + tiles
    is_last = me == last

    def pairs(j):
        inside = jnp.logical_and(j >= first_tile, j < last - 2)
        return jnp.logical_or(j == 0, jnp.logical_and(j % 2 == first_tile % 2, inside))

    paired = pairs(me)
    core = dep % 2
    head = first_tile - 1
    lead = me == head
    beyond = me == last + 1
    relays = [j for j in range(head, last - 1, 2)][:0]
    relay = jnp.logical_and(me >= head, me < 0)
    relay_left = relay
    for j in relays:
        relay = jnp.logical_or(relay, me == j)
        relay_left = jnp.logical_or(relay_left, me - 1 == j)
    relay_low = jnp.logical_and(relay, core == 0)
    relay_high = jnp.logical_and(relay, core == 1)

    def sends_to(j):
        return jnp.logical_and(me != j, jnp.logical_or(near, tile_at(j)))

    def halo_to(j):
        return jnp.logical_and(is_last, me != j)

    def reaches(j):
        return jnp.logical_or(sends_to(j), halo_to(j))

    def reached_by(j):
        return jnp.logical_and(me != j, jnp.logical_or(is_tile, near_at(j) or j == last))

    def partner(j):
        beside = jnp.logical_or(me == j - 1, me == j + 1)
        return jnp.logical_or(beside, jnp.logical_or(reaches(j), reached_by(j)))

    barrier = pltpu.get_barrier_semaphore()
    for j in range(n):

        back = jnp.logical_and(j == me - 1, pairs(j))

        ahead = jnp.logical_and(j > me, partner(j))
        at = dep - core if j in relays else dep
        if False and j == last + 1:
            at = jnp.where(lead, dep - core + 1, dep)

        @pl.when(jnp.logical_or(ahead, back))
        def _():
            pl.semaphore_signal(barrier, inc=1, device_id=(j, at), device_id_type=MESH)

    @pl.when(relay_left)
    def _():
        pl.semaphore_signal(
            barrier, inc=1, device_id=(me - 1, dep - core + 1), device_id_type=MESH
        )

    @pl.when(relay_high)
    def _():
        pl.semaphore_signal(barrier, inc=1, device_id=(me, dep - 1), device_id_type=MESH)

    @pl.when(jnp.logical_and(has_above, jnp.logical_not(relay_low)))
    def _():
        pl.semaphore_signal(barrier, inc=1, device_id=(me, dep + 1), device_id_type=MESH)

    step = cx // 4
    columns = [
        pltpu.make_async_copy(
            st.at[3 * f, pl.ds(k * step, step), :, pl.ds(row, 128)],
            col.at[f, pl.ds(k * step, step)],
            lsem.at[2],
        )
        for k in range(4)
        for f in range(2)
    ]
    small = [
        pltpu.make_async_copy(order, po, lsem.at[0]),
        pltpu.make_async_copy(fp, pb, lsem.at[1]),
    ]
    z_rows = (
        (4, cz - 2), (4, cz - 1), (5, cz - 2), (5, cz - 1), (2, cz - 1),
        (4, 0), (5, 0), (2, 0), (2, 1),
    )
    zloads = [
        pltpu.make_async_copy(st.at[f, :, r], zout.at[k], lsem.at[3])
        for k, (f, r) in enumerate(z_rows)
    ]
    loads = [
        pltpu.make_async_copy(st.at[0], sx.at[0, pl.ds(2, cx)], lsem.at[4]),
        pltpu.make_async_copy(
            st.at[pl.ds(3, 2)], sx.at[pl.ds(1, 2), pl.ds(2, cx)], lsem.at[4]
        ),
        pltpu.make_async_copy(st.at[pl.ds(1, 2)], so.at[pl.ds(0, 2)], lsem.at[5]),
        pltpu.make_async_copy(st.at[5], so.at[2], lsem.at[5]),
        pltpu.make_async_copy(mat, mb, lsem.at[6]),
        pltpu.make_async_copy(vel, vb, lsem.at[7]),
    ]
    for load in small + columns + zloads + loads:
        load.start()

    def arrived(ref, sem):
        pltpu.make_async_copy(ref, ref, sem).wait()

    zlo, zhi = zin.at[pl.ds(0, 5)], zin.at[pl.ds(5, 4)]
    zero_row = jnp.zeros((2, cz, ny), jnp.float32)

    @pl.when(jnp.logical_not(has_left))
    def _():
        for f in range(3):
            sx[f, 0:2] = zero_row

    @pl.when(jnp.logical_not(has_right))
    def _():
        for f in range(3):
            sx[f, cx + 2 : cx + 4] = zero_row

    @pl.when(jnp.logical_not(has_below))
    def _():
        zin[0:5] = jnp.zeros((5, cx, ny), jnp.float32)

    @pl.when(jnp.logical_not(has_above))
    def _():
        zin[5:9] = jnp.zeros((4, cx, ny), jnp.float32)

    for j in range(n):
        if not near_at(j):

            @pl.when(jnp.logical_not(is_tile))
            def _():
                recv[j] = jnp.zeros(recv.shape[1:], jnp.float32)

    def x_copies(up):
        pairs = []
        for f, fields in ((0, 1), (1, 2)):
            if up:
                rows = 2 if f == 0 else 1
                src, dst, to = cx - rows, 2 - rows, me + 1
            else:
                rows = 1 if f == 0 else 2
                src, dst, to = 0, cx + 2, me - 1
            slot = 0 if up else 1
            pairs.append(
                pltpu.make_async_remote_copy(
                    src_ref=st.at[pl.ds(3 * f, fields), pl.ds(src, rows)],
                    dst_ref=sx.at[pl.ds(f, fields), pl.ds(dst, rows)],
                    send_sem=xsend.at[slot],
                    recv_sem=xrecv.at[slot],
                    device_id=(to, dep),
                    device_id_type=MESH,
                )
            )
        return pairs

    def z_copy(up):
        return pltpu.make_async_remote_copy(
            src_ref=zout.at[pl.ds(0, 5)] if up else zout.at[pl.ds(5, 4)],
            dst_ref=zlo if up else zhi,
            send_sem=zsend.at[0 if up else 1],
            recv_sem=zrecv.at[0 if up else 1],
            device_id=(me, dep + 1 if up else dep - 1),
            device_id_type=MESH,
        )

    def pack_copy(j):
        return pltpu.make_async_remote_copy(
            src_ref=packs.at[min(max(j - first_tile, 0), tiles - 1)],
            dst_ref=recv.at[me],
            send_sem=psend,
            recv_sem=precv,
            device_id=(j, dep),
            device_id_type=MESH,
        )

    def pack_next():
        for j in range(1, n):

            @pl.when(jnp.logical_and(j == me + 1, sends_to(j)))
            def _():
                pack_copy(j).start()

            @pl.when(jnp.logical_and(j == me + 1, halo_to(j)))
            def _():
                halo_copy(j).start()

    def halo_copy(j):
        return pltpu.make_async_remote_copy(
            src_ref=st.at[0, 0, :, pl.ds(row, 128)],
            dst_ref=halo,
            send_sem=hsend,
            recv_sem=hrecv,
            device_id=(j, dep),
            device_id_type=MESH,
        )

    ahead_of_me = jnp.int32(0)
    for j in range(n):
        ahead_of_me = ahead_of_me + jnp.logical_and(j < me, partner(j)).astype(jnp.int32)
    earlier = ahead_of_me + has_below.astype(jnp.int32) + paired.astype(jnp.int32)
    earlier = jnp.where(relay_low, earlier + ahead_of_me + 1, earlier)
    earlier = jnp.where(relay_high, 0, earlier)
    late = me > last

    fast = me % 2 == 1

    def enter():
        @pl.when(earlier > 0)
        def _():
            pl.semaphore_wait(barrier, earlier)

        @pl.when(relay_low)
        def _():
            pl.semaphore_signal(core_in, inc=1, device_id=(me, dep + 1), device_id_type=MESH)

        @pl.when(relay_high)
        def _():
            pl.semaphore_wait(core_in, 1)

        @pl.when(is_last)
        def _():
            for j in range(last):
                halo_copy(j).start()

        for j in range(n):
            told = jnp.logical_and(j < me - 1, reached_by(j))

            @pl.when(told)
            def _():
                pl.semaphore_signal(
                    far_in.at[late.astype(jnp.int32)],
                    inc=1,
                    device_id=(j, dep),
                    device_id_type=MESH,
                )

        silent = jnp.logical_or(pairs(me - 1), relay_left)

        @pl.when(jnp.logical_and(has_left, jnp.logical_not(silent)))
        def _():
            pl.semaphore_signal(next_in, inc=1, device_id=(me - 1, dep), device_id_type=MESH)

        @pl.when(jnp.logical_and(has_below, jnp.logical_not(relay_high)))
        def _():
            pl.semaphore_signal(depth_in, inc=1, device_id=(me, dep - 1), device_id_type=MESH)

        @pl.when(jnp.logical_and(has_left, fast))
        def _():
            for copy in x_copies(False):
                copy.start()

    with jax.named_scope("entry_fast"):
        pl.when(fast)(enter)

    lane = lax.broadcasted_iota(jnp.int32, (cz, wide), 1)
    lane_one = lax.broadcasted_iota(jnp.int32, (cz, 128), 1)
    my_tile = jnp.clip(me - first_tile, 0, tiles - 1)
    with jax.named_scope("params_wait"):
        for load in small:
            load.wait()
    with jax.named_scope("params"):
        blocks = [jnp.zeros((cz, wide), jnp.float32) for _ in range(tiles)]
        params = [pb[j].T for j in range(per)]
        for f in range(4):
            mine = jnp.full((cz, 128), 1.0, jnp.float32)
            for j in range(per):
                column = po[me * per + j]
                value = params[j][:, f : f + 1]
                mine = jnp.where(lane_one == cx + j, value, mine)
                for t in range(tiles):
                    local = column - t * cx
                    held = jnp.logical_and(local >= 0, local < cx)
                    place = jnp.where(held, f * cx + local, -1)
                    blocks[t] = jnp.where(lane == place, value, blocks[t])
            ownp[f] = mine
            if f < 3:
                state[1 + f] = mine
        for j in range(per):
            slot_lane = lane[0:1] == 4 * cx + po[me * per + j]
            picks[j : j + 1] = jnp.where(slot_lane, 1.0, 0.0)
        for t in range(tiles):
            packs[t] = blocks[t]
    with jax.named_scope("column_wait"):
        arrived(col, lsem.at[2])
    with jax.named_scope("pack"):

        @pl.when(near)
        def _():
            base = 4 * cx + (me - first_tile) * cx
            normal = jnp.zeros((cz, wide), jnp.float32)
            shear = jnp.zeros((cz, wide), jnp.float32)
            for i in range(cx):
                here = lane == base + i
                normal = jnp.where(here, col[0, i, :, 0:1], normal)
                shear = jnp.where(here, col[1, i, :, 0:1], shear)
            dxx = C_ONE * (normal - pltpu.roll(normal, 1, 1)) + C_TWO * (
                pltpu.roll(normal, wide - 1, 1) - pltpu.roll(normal, 2, 1)
            )
            share = shear + 0.5 * dxx
            inside = jnp.logical_and(lane >= 4 * cx, lane < 4 * cx + fc)
            share = jnp.where(inside, share, 0.0)
            for t in range(tiles):
                packs[t] = packs[t] + share
            recv[me] = packs[my_tile]

        @pl.when(is_last)
        def _():
            halo[...] = col[0, 0]

    with jax.named_scope("entry_slow"):
        pl.when(jnp.logical_not(fast))(enter)

    for j in range(n):

        @pl.when(jnp.logical_and(j < me, sends_to(j)))
        def _():
            pack_copy(j).start()

    @pl.when(paired)
    def _():
        pack_next()

    @pl.when(jnp.logical_and(has_left, jnp.logical_not(fast)))
    def _():
        for copy in x_copies(False):
            copy.start()

    @pl.when(paired)
    def _():
        for copy in x_copies(True):
            copy.start()

    with jax.named_scope("z_loads"):
        arrived(zout, lsem.at[3])

    @pl.when(has_below)
    def _():
        z_copy(False).start()

    def send_far(low, high, kind):
        group = [
            (j, jnp.logical_and(j > me + 1, reaches(j))) for j in range(low, high)
        ]
        count = sum(on.astype(jnp.int32) for _, on in group)

        @pl.when(count > 0)
        def _():
            pl.semaphore_wait(far_in.at[kind], count)

        for j, on in group:

            @pl.when(jnp.logical_and(on, sends_to(j)))
            def _():
                pack_copy(j).start()

            @pl.when(jnp.logical_and(on, halo_to(j)))
            def _():
                halo_copy(j).start()

    with jax.named_scope("wait_next"):

        @pl.when(relay_high)
        def _():
            pl.semaphore_wait(barrier, 2)
            pl.semaphore_signal(depth_in, inc=1, device_id=(me, dep - 1), device_id_type=MESH)

        @pl.when(relay_low)
        def _():
            pl.semaphore_wait(depth_in, 1)

        @pl.when(jnp.logical_and(has_right, jnp.logical_not(paired)))
        def _():
            @pl.when(jnp.logical_not(relay))
            def _():
                pl.semaphore_wait(next_in, 1)

            pack_next()
            for copy in x_copies(True):
                copy.start()

        @pl.when(has_above)
        def _():
            @pl.when(jnp.logical_not(relay_low))
            def _():
                pl.semaphore_wait(depth_in, 1)

            z_copy(True).start()

    with jax.named_scope("lead_far"):
        @pl.when(lead)
        def _():
            send_far(2, last + 1, 0)
            send_far(last + 1, n, 1)

    with jax.named_scope("loads"):
        arrived(sx.at[:, pl.ds(2, cx)], lsem.at[4])
        arrived(so, lsem.at[5])
        arrived(mb, lsem.at[6])
        arrived(vb, lsem.at[7])

    yi = lax.broadcasted_iota(jnp.int32, (cz, ny), 1)
    zi = lax.broadcasted_iota(jnp.int32, (cz, ny), 0)

    def y_at(field, offset):
        moved = pltpu.roll(field, (-offset) % ny, 1)
        keep = yi < ny - offset if offset > 0 else yi >= -offset
        return jnp.where(keep, moved, 0.0)

    def z_at(field):
        def at(offset):
            if offset == 0:
                return field
            moved = pltpu.roll(field, (-offset) % cz, 0)
            keep = zi < cz - offset if offset > 0 else zi >= -offset
            return jnp.where(keep, moved, 0.0)

        return at

    def minus(at):
        return C_ONE * (at(0) - at(-1)) + C_TWO * (at(1) - at(-2))

    def plus(at):
        return C_ONE * (at(1) - at(0)) + C_TWO * (at(2) - at(-1))

    def along_x(f, x):
        return lambda offset: sx[f, x + 2 + offset]

    def along_y(field):
        return lambda offset: field if offset == 0 else y_at(field, offset)

    def buoyancy(x):
        material = mb[x]
        b = jnp.full((cz, ny), 0.25 * BUOY[0], jnp.float32)
        for index in range(1, 4):
            b = jnp.where(material == index, 0.25 * BUOY[index], b)
        bb[x] = b
        return b

    def across(x):
        return minus(along_x(0, x)), plus(along_x(1, x)), plus(along_x(2, x))

    def local(x):
        sxz, szz, syz = sx[2, x + 2], so[1, x], so[2, x]
        return (
            minus(along_y(sx[1, x + 2])) + minus(z_at(sxz)),
            plus(along_y(so[0, x])) + minus(z_at(syz)),
            plus(along_y(syz)) + plus(z_at(szz)),
        )

    def inner(x, carry):
        b, along, rest = buoyancy(x), across(x), local(x)
        for c in range(3):
            out[c, x] = vb[c, x] + b * (along[c] + rest[c])
        return carry

    def outer(x):
        b, rest = buoyancy(x), local(x)
        for c in range(3):
            out[c, x] = vb[c, x] + b * rest[c]

    edges = (0, 1, cx - 2, cx - 1)
    with jax.named_scope("outer"):
        for x in edges:
            outer(x)

    middle = cx // 2
    with jax.named_scope("inner"):
        lax.fori_loop(2, middle, inner, 0)

    with jax.named_scope("wait_far"):
        pl.when(jnp.logical_not(lead))(lambda: send_far(2, last + 1, 0))
    with jax.named_scope("wait_far2"):
        pl.when(jnp.logical_not(lead))(lambda: send_far(last + 1, n, 1))

    with jax.named_scope("inner2"):
        lax.fori_loop(middle, cx - 2, inner, 0)
    with jax.named_scope("z_wait"):

        @pl.when(has_below)
        def _():
            z_copy(True).wait_recv()

        @pl.when(has_above)
        def _():
            z_copy(False).wait_recv()

    first = lax.broadcasted_iota(jnp.int32, (8, ny), 0)

    def face(x, carry):
        def low(k):
            return zin[k, pl.ds(x, 1), :]

        def high(k):
            return zin[5 + k, pl.ds(x, 1), :]

        def put(at, one, two):
            return jnp.where(first == at, one, jnp.where(first == two[0], two[1], 0.0))

        b = bb[x, 0:8]
        out[0, x, 0:8] -= b * put(0, C_ONE * low(1) + C_TWO * low(0), (1, C_TWO * low(1)))
        out[1, x, 0:8] -= b * put(0, C_ONE * low(3) + C_TWO * low(2), (1, C_TWO * low(3)))
        out[2, x, 0:8] -= b * jnp.where(first == 0, C_TWO * low(4), 0.0)
        b = bb[x, cz - 8 : cz]
        out[0, x, cz - 8 : cz] += b * jnp.where(first == 7, C_TWO * high(0), 0.0)
        out[1, x, cz - 8 : cz] += b * jnp.where(first == 7, C_TWO * high(1), 0.0)
        out[2, x, cz - 8 : cz] += b * put(
            7, C_ONE * high(2) + C_TWO * high(3), (6, C_TWO * high(2))
        )
        return carry

    with jax.named_scope("face"):
        lax.fori_loop(0, cx, face, 0)

    def level(columns):
        for start in range(0, len(columns), 4):
            parts = []
            for i in columns[start : start + 4]:
                low = out[0, i, :, row - 128 : row]
                high = out[0, i, :, row : row + 128]
                mean = 0.5 * (high + pltpu.roll(low, 1, 1))
                low = jnp.where(lane_one == 127, pltpu.roll(mean, 127, 1), low)
                parts.append((i, low, jnp.where(lane_one == 0, mean, high)))
            for i, low, high in parts:
                out[0, i, :, row - 128 : row] = low
                out[0, i, :, row : row + 128] = high

    with jax.named_scope("mean_inside"):

        @pl.when(is_tile)
        def _():
            level(range(2, cx - 2))

    with jax.named_scope("x_wait"):

        @pl.when(has_left)
        def _():
            arrived(sx.at[0, pl.ds(0, 4)], xrecv.at[0])

        @pl.when(has_right)
        def _():
            arrived(sx.at[0, pl.ds(0, 5)], xrecv.at[1])

    with jax.named_scope("edges"):
        for x in edges:
            along = across(x)
            for c in range(3):
                out[c, x] += bb[x] * along[c]

    with jax.named_scope("mean"):

        @pl.when(is_tile)
        def _():
            level(edges)

    with jax.named_scope("pack_wait"):
        @pl.when(is_tile)
        def _():
            arrived(recv.at[pl.ds(0, n - 1)], precv)

        @pl.when(me == first_tile - 1)
        def _():
            arrived(recv.at[pl.ds(0, tiles)], precv)

        @pl.when(jnp.logical_not(near))
        def _():
            arrived(recv.at[pl.ds(0, tiles + 1)], precv)

        @pl.when(jnp.logical_not(is_last))
        def _():
            arrived(halo, hrecv)

    with jax.named_scope("friction"):
        total = recv[first_tile - 1]
        for j in range(n):
            if j != first_tile - 1:
                total = total + recv[j]
        edge = 0.5 * C_TWO * halo[:, 0:1]
        total = total + jnp.where(lane == 4 * cx + fc - 1, edge, 0.0)

        def own_slots():
            own = ownp[3]
            for j in range(per):
                picked = jnp.sum(total * picks[j : j + 1], axis=1, keepdims=True)
                own = own + jnp.where(lane_one == cx + j, picked, 0.0)
            state[0] = own

        @pl.when(is_tile)
        def _():
            fields = [total[:, :128]]
            for f in range(1, 4):
                fields.append(pltpu.roll(total, wide - f * cx, 1)[:, :128])
            used = lane_one < cx
            fields = [jnp.where(used, field, 1.0) for field in fields]
            tau = fields[3]
            for t in range(tiles):
                moved = pltpu.roll(total, wide - (4 + t) * cx, 1)[:, :128]
                tau = tau + jnp.where(jnp.logical_and(used, my_tile == t), moved, 0.0)
            rates[...] = 0.5 * friction(tau, *fields[:3])
            own_slots()

        pl.when(jnp.logical_not(is_tile))(own_slots)

    def fix(columns):
        for start in range(0, len(columns), 4):
            parts = []
            for i in columns[start : start + 4]:
                s = rates[:, i : i + 1]
                low = out[0, i, :, row - 128 : row]
                high = out[0, i, :, row : row + 128]
                low = low - jnp.where(lane_one == 127, s, 0.0)
                high = high + jnp.where(lane_one == 0, s, 0.0)
                parts.append((i, low, high))
            for i, low, high in parts:
                out[0, i, :, row - 128 : row] = low
                out[0, i, :, row : row + 128] = high

    with jax.named_scope("fix"):

        @pl.when(is_tile)
        def _():
            fix(range(cx))

    with jax.named_scope("sends_done"):
        @pl.when(near)
        def _():
            arrived(recv.at[pl.ds(0, n - 1)], psend)

        @pl.when(jnp.logical_not(near))
        def _():
            arrived(recv.at[pl.ds(0, tiles)], psend)

        @pl.when(is_last)
        def _():
            arrived(recv.at[pl.ds(0, n - 1), :, pl.ds(0, 128)], hsend)

        @pl.when(has_above)
        def _():
            z_copy(True).wait_send()

        @pl.when(has_below)
        def _():
            z_copy(False).wait_send()

        @pl.when(has_right)
        def _():
            arrived(sx.at[0, pl.ds(0, 4)], xsend.at[0])

        @pl.when(has_left)
        def _():
            arrived(sx.at[0, pl.ds(0, 5)], xsend.at[1])


def write_out(first, held, state, out, slip_out, slip, sem):
    velocity = pltpu.make_async_copy(held, out, sem.at[0])
    velocity.start()
    rate = friction(state[0], state[1], state[2], state[3])
    slip[...] = rate.T[first : first + slip.shape[0]]
    rates = pltpu.make_async_copy(slip, slip_out, sem.at[1])
    rates.start()
    velocity.wait()
    rates.wait()


def per_device(n, nd, velocity, stress, material, patch_order, fault_params):
    _, cx, cz, ny = stress.shape
    fc = patch_order.shape[0]
    per = fc // n
    wide = -(-(4 * cx + fc + 2) // 128) * 128
    dims = (n, nd, cx, cz, ny, fc, wide)
    tiles = fc // cx
    f32 = jnp.float32
    anywhere = pl.BlockSpec(memory_space=pltpu.HBM)
    dma = pltpu.SemaphoreType.DMA
    params = jnp.transpose(fault_params, (2, 0, 1))
    big = (velocity, stress, material, patch_order, params)
    held = pl.pallas_call(
        functools.partial(kernel, dims),
        out_shape=(
            jax.ShapeDtypeStruct(velocity.shape, f32),
            jax.ShapeDtypeStruct((4, cz, 128), f32),
        ),
        in_specs=[anywhere] * 5,
        out_specs=(pl.BlockSpec(memory_space=pltpu.VMEM), pl.BlockSpec(memory_space=pltpu.VMEM)),
        scratch_shapes=[
            pltpu.SMEM((fc,), jnp.int32),
            pltpu.VMEM((2, cx, cz, 128), f32),
            pltpu.VMEM((3, cx + 4, cz, ny), f32),
            pltpu.VMEM((3, cx, cz, ny), f32),
            pltpu.VMEM((3, cx, cz, ny), f32),
            pltpu.VMEM((cx, cz, ny), jnp.int32),
            pltpu.VMEM((cx, cz, ny), f32),
            pltpu.VMEM((per, 4, cz), f32),
            pltpu.VMEM((4, cz, 128), f32),
            pltpu.VMEM((9, cx, ny), f32),
            pltpu.VMEM((9, cx, ny), f32),
            pltpu.VMEM((tiles, cz, wide), f32),
            pltpu.VMEM((n, cz, wide), f32),
            pltpu.VMEM((cz, 128), f32),
            pltpu.VMEM((cz, 128), f32),
            pltpu.VMEM((-(-per // 8) * 8, wide), f32),
            dma((8,)),
            dma,
            dma,
            dma,
            dma,
            dma((2,)),
            dma((2,)),
            dma((2,)),
            dma((2,)),
            pltpu.SemaphoreType.REGULAR,
            pltpu.SemaphoreType.REGULAR((2,)),
            pltpu.SemaphoreType.REGULAR,
            pltpu.SemaphoreType.REGULAR,
        ],
        compiler_params=pltpu.CompilerParams(collective_id=0, has_side_effects=True, vmem_limit_bytes=12 << 20),
    )(*[pltpu.with_memory_space_constraint(v, pltpu.HBM) for v in big])
    resident = pl.BlockSpec(memory_space=pltpu.VMEM)
    moved, slip = pl.pallas_call(
        functools.partial(write_out, cx),
        out_shape=(
            jax.ShapeDtypeStruct(velocity.shape, f32),
            jax.ShapeDtypeStruct((per, cz), f32),
        ),
        in_specs=[resident, resident],
        out_specs=(anywhere, anywhere),
        scratch_shapes=[pltpu.VMEM((per, cz), f32), dma((2,))],
        compiler_params=pltpu.CompilerParams(vmem_limit_bytes=4 << 20),
    )(*held)
    return moved, slip.T


def solution(mesh):
    n, nd = mesh.shape["strike"], mesh.shape["depth"]
    return jax.shard_map(
        functools.partial(per_device, n, nd),
        mesh=mesh,
        in_specs=(
            P(None, "strike", "depth", None),
            P(None, "strike", "depth", None),
            P("strike", "depth", None),
            P(),
            P(None, "depth", "strike"),
        ),
        out_specs=(P(None, "strike", "depth", None), P("depth", "strike")),
        check_vma=False,
    )
```

```python
import functools

import jax
import jax.numpy as jnp
from jax import lax
from jax.experimental import pallas as pl
from jax.experimental.pallas import tpu as pltpu
from jax.sharding import PartitionSpec as P

NEWTON = 8
BUOY = (1.0, 0.8, 0.6, 1.25)
C_ONE = 9.0 / 8.0
C_TWO = -1.0 / 24.0
MESH = pl.DeviceIdType.MESH


def friction(tau_total, coef, psi, normal_stress):
    half_q = 0.5 * jnp.exp(psi / coef)
    scale = normal_stress * coef
    stiff = scale * half_q
    rate = 0.35 * tau_total / (1.0 + stiff)
    for _ in range(NEWTON - 1):
        arg_val = rate * half_q
        square = 1.0 + arg_val * arg_val
        inverse = lax.rsqrt(square)
        magnitude = jnp.log(jnp.abs(arg_val) + square * inverse)
        resid = tau_total - rate - scale * jnp.where(arg_val < 0, -magnitude, magnitude)
        rate = rate + 0.35 * resid / (1.0 + stiff * inverse)
    return rate


def kernel(
    dims, vel, st, mat, order, fp, out, state,
    po, col, sx, so, vb, mb, bb, pb, ownp, zout, zin, packs, recv, halo, rates, picks,
    lsem, psend, precv, hsend, hrecv, xsend, xrecv, zsend, zrecv, next_in, far_in, depth_in,
):
    n, nd, cx, cz, ny, fc, wide = dims
    row = ny // 2
    per = fc // n
    first_tile = n // 4
    tiles = fc // cx
    me = lax.axis_index("strike")
    dep = lax.axis_index("depth")
    has_left, has_right = me > 0, me < n - 1
    has_below, has_above = dep > 0, dep < nd - 1
    is_tile = jnp.logical_and(me >= first_tile, me < first_tile + tiles)
    near = jnp.logical_and(me >= first_tile - 1, me < first_tile + tiles)

    def tile_at(j):
        return first_tile <= j < first_tile + tiles

    def near_at(j):
        return first_tile - 1 <= j < first_tile + tiles

    last = first_tile + tiles
    is_last = me == last

    def pairs(j):
        inside = jnp.logical_and(j >= first_tile, j < last - 2)
        return jnp.logical_or(j == 0, jnp.logical_and(j % 2 == first_tile % 2, inside))

    paired = pairs(me)
    head = first_tile - 1
    lead = me == head
    beyond = me == last + 1
    is_end = me == last - 1

    def sends_to(j):
        return jnp.logical_and(me != j, jnp.logical_or(near, tile_at(j)))

    def halo_to(j):
        return jnp.logical_and(is_last, me != j)

    def reaches(j):
        return jnp.logical_or(sends_to(j), halo_to(j))

    def reached_by(j):
        return jnp.logical_and(me != j, jnp.logical_or(is_tile, near_at(j) or j == last))

    def partner(j):
        beside = jnp.logical_or(me == j - 1, me == j + 1)
        return jnp.logical_or(beside, jnp.logical_or(reaches(j), reached_by(j)))

    barrier = pltpu.get_barrier_semaphore()
    for j in range(n):

        back = jnp.logical_and(j == me - 1, pairs(j))

        ahead = jnp.logical_and(j > me, partner(j))
        if j == last + 1:
            ahead = jnp.logical_and(ahead, jnp.logical_not(lead))

        @pl.when(jnp.logical_or(ahead, back))
        def _():
            pl.semaphore_signal(barrier, inc=1, device_id=(j, dep), device_id_type=MESH)

    @pl.when(jnp.logical_and(me >= 2, pairs(me - 2)))
    def _():
        pl.semaphore_signal(barrier, inc=1, device_id=(me - 2, dep), device_id_type=MESH)

    @pl.when(beyond)
    def _():
        pl.semaphore_signal(barrier, inc=1, device_id=(last - 1, dep), device_id_type=MESH)

    @pl.when(has_above)
    def _():
        pl.semaphore_signal(barrier, inc=1, device_id=(me, dep + 1), device_id_type=MESH)

    step = cx // 4
    columns = [
        pltpu.make_async_copy(
            st.at[3 * f, pl.ds(k * step, step), :, pl.ds(row, 128)],
            col.at[f, pl.ds(k * step, step)],
            lsem.at[2],
        )
        for k in range(4)
        for f in range(2)
    ]
    small = [
        pltpu.make_async_copy(order, po, lsem.at[0]),
        pltpu.make_async_copy(fp, pb, lsem.at[1]),
    ]
    z_rows = (
        (4, cz - 2), (4, cz - 1), (5, cz - 2), (5, cz - 1), (2, cz - 1),
        (4, 0), (5, 0), (2, 0), (2, 1),
    )
    zloads = [
        pltpu.make_async_copy(st.at[f, :, r], zout.at[k], lsem.at[3])
        for k, (f, r) in enumerate(z_rows)
    ]
    loads = [
        pltpu.make_async_copy(st.at[0], sx.at[0, pl.ds(2, cx)], lsem.at[4]),
        pltpu.make_async_copy(
            st.at[pl.ds(3, 2)], sx.at[pl.ds(1, 2), pl.ds(2, cx)], lsem.at[4]
        ),
        pltpu.make_async_copy(st.at[pl.ds(1, 2)], so.at[pl.ds(0, 2)], lsem.at[5]),
        pltpu.make_async_copy(st.at[5], so.at[2], lsem.at[5]),
        pltpu.make_async_copy(mat, mb, lsem.at[6]),
        pltpu.make_async_copy(vel, vb, lsem.at[7]),
    ]
    for load in small + columns + zloads + loads:
        load.start()

    def arrived(ref, sem):
        pltpu.make_async_copy(ref, ref, sem).wait()

    zlo, zhi = zin.at[pl.ds(0, 5)], zin.at[pl.ds(5, 4)]
    zero_row = jnp.zeros((2, cz, ny), jnp.float32)

    @pl.when(jnp.logical_not(has_left))
    def _():
        for f in range(3):
            sx[f, 0:2] = zero_row

    @pl.when(jnp.logical_not(has_right))
    def _():
        for f in range(3):
            sx[f, cx + 2 : cx + 4] = zero_row

    @pl.when(jnp.logical_not(has_below))
    def _():
        zin[0:5] = jnp.zeros((5, cx, ny), jnp.float32)

    @pl.when(jnp.logical_not(has_above))
    def _():
        zin[5:9] = jnp.zeros((4, cx, ny), jnp.float32)

    for j in range(n):
        if not near_at(j):

            @pl.when(jnp.logical_not(is_tile))
            def _():
                recv[j] = jnp.zeros(recv.shape[1:], jnp.float32)

    def x_copies(up, fields=(0, 1, 2)):
        copies = []
        for f in fields:
            plane = (0, 3, 4)[f]
            if up:
                rows = 2 if f == 0 else 1
                src, dst, to = cx - rows, 2 - rows, me + 1
            else:
                rows = 1 if f == 0 else 2
                src, dst, to = 0, cx + 2, me - 1
            slot = 0 if up else 1
            copies.append(
                pltpu.make_async_remote_copy(
                    src_ref=st.at[plane, pl.ds(src, rows)],
                    dst_ref=sx.at[f, pl.ds(dst, rows)],
                    send_sem=xsend.at[slot],
                    recv_sem=xrecv.at[slot],
                    device_id=(to, dep),
                    device_id_type=MESH,
                )
            )
        return copies

    def z_copy(up):
        return pltpu.make_async_remote_copy(
            src_ref=zout.at[pl.ds(0, 5)] if up else zout.at[pl.ds(5, 4)],
            dst_ref=zlo if up else zhi,
            send_sem=zsend.at[0 if up else 1],
            recv_sem=zrecv.at[0 if up else 1],
            device_id=(me, dep + 1 if up else dep - 1),
            device_id_type=MESH,
        )

    def pack_copy(j):
        return pltpu.make_async_remote_copy(
            src_ref=packs.at[min(max(j - first_tile, 0), tiles - 1)],
            dst_ref=recv.at[me],
            send_sem=psend,
            recv_sem=precv,
            device_id=(j, dep),
            device_id_type=MESH,
        )

    def pack_next():
        for j in range(1, n):

            @pl.when(jnp.logical_and(j == me + 1, sends_to(j)))
            def _():
                pack_copy(j).start()

            @pl.when(jnp.logical_and(j == me + 1, halo_to(j)))
            def _():
                halo_copy(j).start()

    def halo_copy(j):
        return pltpu.make_async_remote_copy(
            src_ref=st.at[0, 0, :, pl.ds(row, 128)],
            dst_ref=halo,
            send_sem=hsend,
            recv_sem=hrecv,
            device_id=(j, dep),
            device_id_type=MESH,
        )

    ahead_of_me = jnp.int32(0)
    for j in range(n):
        ahead_of_me = ahead_of_me + jnp.logical_and(j < me, partner(j)).astype(jnp.int32)
    earlier = ahead_of_me + has_below.astype(jnp.int32) + 2 * paired.astype(jnp.int32)
    earlier = earlier + is_end.astype(jnp.int32) - beyond.astype(jnp.int32)
    late = me > last

    fast = me % 2 == 1

    def enter():
        @pl.when(earlier > 0)
        def _():
            pl.semaphore_wait(barrier, earlier)

        @pl.when(is_end)
        def _():
            pl.semaphore_signal(
                far_in.at[1], inc=1, device_id=(head, dep), device_id_type=MESH
            )

        @pl.when(is_last)
        def _():
            for j in range(last):
                halo_copy(j).start()

        for j in range(n):
            told = jnp.logical_and(j < me - 1, reached_by(j))
            if j == head:
                told = jnp.logical_and(told, jnp.logical_not(beyond))

            @pl.when(told)
            def _():
                pl.semaphore_signal(
                    far_in.at[late.astype(jnp.int32)],
                    inc=1,
                    device_id=(j, dep),
                    device_id_type=MESH,
                )

        @pl.when(paired)
        def _():
            pl.semaphore_signal(next_in, inc=1, device_id=(me + 1, dep), device_id_type=MESH)

        silent = jnp.logical_or(pairs(me - 1), jnp.logical_and(me >= 2, pairs(me - 2)))

        @pl.when(jnp.logical_and(has_left, jnp.logical_not(silent)))
        def _():
            pl.semaphore_signal(next_in, inc=1, device_id=(me - 1, dep), device_id_type=MESH)

        @pl.when(has_below)
        def _():
            pl.semaphore_signal(depth_in, inc=1, device_id=(me, dep - 1), device_id_type=MESH)

        @pl.when(jnp.logical_and(has_left, fast))
        def _():
            for copy in x_copies(False, (0, 1)):
                copy.start()

    with jax.named_scope("entry_fast"):
        pl.when(fast)(enter)

    lane = lax.broadcasted_iota(jnp.int32, (cz, wide), 1)
    lane_one = lax.broadcasted_iota(jnp.int32, (cz, 128), 1)
    my_tile = jnp.clip(me - first_tile, 0, tiles - 1)
    with jax.named_scope("params_wait"):
        for load in small:
            load.wait()
    with jax.named_scope("params"):
        blocks = [jnp.zeros((cz, wide), jnp.float32) for _ in range(tiles)]
        params = [pb[j].T for j in range(per)]
        for f in range(4):
            mine = jnp.full((cz, 128), 1.0, jnp.float32)
            for j in range(per):
                column = po[me * per + j]
                value = params[j][:, f : f + 1]
                mine = jnp.where(lane_one == cx + j, value, mine)
                for t in range(tiles):
                    local = column - t * cx
                    held = jnp.logical_and(local >= 0, local < cx)
                    place = jnp.where(held, f * cx + local, -1)
                    blocks[t] = jnp.where(lane == place, value, blocks[t])
            ownp[f] = mine
            if f < 3:
                state[1 + f] = mine
        for j in range(per):
            slot_lane = lane[0:1] == 4 * cx + po[me * per + j]
            picks[j : j + 1] = jnp.where(slot_lane, 1.0, 0.0)
        for t in range(tiles):
            packs[t] = blocks[t]
    with jax.named_scope("column_wait"):
        arrived(col, lsem.at[2])
    with jax.named_scope("pack"):

        @pl.when(near)
        def _():
            base = 4 * cx + (me - first_tile) * cx
            normal = jnp.zeros((cz, wide), jnp.float32)
            shear = jnp.zeros((cz, wide), jnp.float32)
            for i in range(cx):
                here = lane == base + i
                normal = jnp.where(here, col[0, i, :, 0:1], normal)
                shear = jnp.where(here, col[1, i, :, 0:1], shear)
            dxx = C_ONE * (normal - pltpu.roll(normal, 1, 1)) + C_TWO * (
                pltpu.roll(normal, wide - 1, 1) - pltpu.roll(normal, 2, 1)
            )
            share = shear + 0.5 * dxx
            inside = jnp.logical_and(lane >= 4 * cx, lane < 4 * cx + fc)
            share = jnp.where(inside, share, 0.0)
            for t in range(tiles):
                packs[t] = packs[t] + share
            recv[me] = packs[my_tile]

        @pl.when(is_last)
        def _():
            halo[...] = col[0, 0]

    with jax.named_scope("entry_slow"):
        pl.when(jnp.logical_not(fast))(enter)

    for j in range(n):

        @pl.when(jnp.logical_and(j < me, sends_to(j)))
        def _():
            pack_copy(j).start()

    @pl.when(paired)
    def _():
        pack_next()

    @pl.when(jnp.logical_and(has_left, fast))
    def _():
        for copy in x_copies(False, (2,)):
            copy.start()

    @pl.when(jnp.logical_and(has_left, jnp.logical_not(fast)))
    def _():
        for copy in x_copies(False):
            copy.start()

    @pl.when(paired)
    def _():
        for copy in x_copies(True):
            copy.start()

    with jax.named_scope("z_loads"):
        arrived(zout, lsem.at[3])

    @pl.when(has_below)
    def _():
        z_copy(False).start()

    def send_far(low, high, kind):
        group = [
            (j, jnp.logical_and(j > me + 1, reaches(j))) for j in range(low, high)
        ]
        count = sum(on.astype(jnp.int32) for _, on in group)

        @pl.when(count > 0)
        def _():
            pl.semaphore_wait(far_in.at[kind], count)

        for j, on in group:

            @pl.when(jnp.logical_and(on, sends_to(j)))
            def _():
                pack_copy(j).start()

            @pl.when(jnp.logical_and(on, halo_to(j)))
            def _():
                halo_copy(j).start()

    with jax.named_scope("wait_next"):

        @pl.when(jnp.logical_and(has_right, jnp.logical_not(paired)))
        def _():
            pl.semaphore_wait(next_in, 1)
            pack_next()
            for copy in x_copies(True):
                copy.start()

        @pl.when(has_above)
        def _():
            pl.semaphore_wait(depth_in, 1)
            z_copy(True).start()

    with jax.named_scope("lead_far"):
        @pl.when(lead)
        def _():
            send_far(2, last + 1, 0)
            send_far(last + 1, n, 1)

    with jax.named_scope("loads"):
        arrived(sx.at[:, pl.ds(2, cx)], lsem.at[4])
        arrived(so, lsem.at[5])
        arrived(mb, lsem.at[6])
        arrived(vb, lsem.at[7])

    yi = lax.broadcasted_iota(jnp.int32, (cz, ny), 1)
    zi = lax.broadcasted_iota(jnp.int32, (cz, ny), 0)

    def y_at(field, offset):
        moved = pltpu.roll(field, (-offset) % ny, 1)
        keep = yi < ny - offset if offset > 0 else yi >= -offset
        return jnp.where(keep, moved, 0.0)

    def z_at(field):
        def at(offset):
            if offset == 0:
                return field
            moved = pltpu.roll(field, (-offset) % cz, 0)
            keep = zi < cz - offset if offset > 0 else zi >= -offset
            return jnp.where(keep, moved, 0.0)

        return at

    def minus(at):
        return C_ONE * (at(0) - at(-1)) + C_TWO * (at(1) - at(-2))

    def plus(at):
        return C_ONE * (at(1) - at(0)) + C_TWO * (at(2) - at(-1))

    def along_x(f, x):
        return lambda offset: sx[f, x + 2 + offset]

    def along_y(field):
        return lambda offset: field if offset == 0 else y_at(field, offset)

    def buoyancy(x):
        material = mb[x]
        b = jnp.full((cz, ny), 0.25 * BUOY[0], jnp.float32)
        for index in range(1, 4):
            b = jnp.where(material == index, 0.25 * BUOY[index], b)
        bb[x] = b
        return b

    def across(x):
        return minus(along_x(0, x)), plus(along_x(1, x)), plus(along_x(2, x))

    def local(x):
        sxz, szz, syz = sx[2, x + 2], so[1, x], so[2, x]
        return (
            minus(along_y(sx[1, x + 2])) + minus(z_at(sxz)),
            plus(along_y(so[0, x])) + minus(z_at(syz)),
            plus(along_y(syz)) + plus(z_at(szz)),
        )

    def inner(x, carry):
        b, along, rest = buoyancy(x), across(x), local(x)
        for c in range(3):
            out[c, x] = vb[c, x] + b * (along[c] + rest[c])
        return carry

    def outer(x):
        b, rest = buoyancy(x), local(x)
        for c in range(3):
            out[c, x] = vb[c, x] + b * rest[c]

    edges = (0, 1, cx - 2, cx - 1)
    with jax.named_scope("outer"):
        for x in edges:
            outer(x)

    middle = cx // 2
    with jax.named_scope("inner"):
        lax.fori_loop(2, middle, inner, 0)

    with jax.named_scope("wait_far"):
        pl.when(jnp.logical_not(lead))(lambda: send_far(2, last + 1, 0))
    with jax.named_scope("wait_far2"):
        pl.when(jnp.logical_not(lead))(lambda: send_far(last + 1, n, 1))

    with jax.named_scope("inner2"):
        lax.fori_loop(middle, cx - 2, inner, 0)
    with jax.named_scope("z_wait"):

        @pl.when(has_below)
        def _():
            z_copy(True).wait_recv()

        @pl.when(has_above)
        def _():
            z_copy(False).wait_recv()

    first = lax.broadcasted_iota(jnp.int32, (8, ny), 0)

    def face(x, carry):
        def low(k):
            return zin[k, pl.ds(x, 1), :]

        def high(k):
            return zin[5 + k, pl.ds(x, 1), :]

        def put(at, one, two):
            return jnp.where(first == at, one, jnp.where(first == two[0], two[1], 0.0))

        b = bb[x, 0:8]
        out[0, x, 0:8] -= b * put(0, C_ONE * low(1) + C_TWO * low(0), (1, C_TWO * low(1)))
        out[1, x, 0:8] -= b * put(0, C_ONE * low(3) + C_TWO * low(2), (1, C_TWO * low(3)))
        out[2, x, 0:8] -= b * jnp.where(first == 0, C_TWO * low(4), 0.0)
        b = bb[x, cz - 8 : cz]
        out[0, x, cz - 8 : cz] += b * jnp.where(first == 7, C_TWO * high(0), 0.0)
        out[1, x, cz - 8 : cz] += b * jnp.where(first == 7, C_TWO * high(1), 0.0)
        out[2, x, cz - 8 : cz] += b * put(
            7, C_ONE * high(2) + C_TWO * high(3), (6, C_TWO * high(2))
        )
        return carry

    with jax.named_scope("face"):
        lax.fori_loop(0, cx, face, 0)

    def level(columns):
        for start in range(0, len(columns), 4):
            parts = []
            for i in columns[start : start + 4]:
                low = out[0, i, :, row - 128 : row]
                high = out[0, i, :, row : row + 128]
                mean = 0.5 * (high + pltpu.roll(low, 1, 1))
                low = jnp.where(lane_one == 127, pltpu.roll(mean, 127, 1), low)
                parts.append((i, low, jnp.where(lane_one == 0, mean, high)))
            for i, low, high in parts:
                out[0, i, :, row - 128 : row] = low
                out[0, i, :, row : row + 128] = high

    with jax.named_scope("mean_inside"):

        @pl.when(is_tile)
        def _():
            level(range(2, cx - 2))

    outside = jnp.logical_or(me < head, me > last)

    def add_edges():
        with jax.named_scope("x_wait"):

            @pl.when(has_left)
            def _():
                arrived(sx.at[0, pl.ds(0, 4)], xrecv.at[0])

            @pl.when(has_right)
            def _():
                arrived(sx.at[0, pl.ds(0, 5)], xrecv.at[1])

        with jax.named_scope("edges"):
            for x in edges:
                along = across(x)
                for c in range(3):
                    out[c, x] += bb[x] * along[c]

    pl.when(outside)(add_edges)

    with jax.named_scope("pack_wait"):
        @pl.when(is_tile)
        def _():
            arrived(recv.at[pl.ds(0, n - 1)], precv)

        @pl.when(me == first_tile - 1)
        def _():
            arrived(recv.at[pl.ds(0, tiles)], precv)

        @pl.when(jnp.logical_not(near))
        def _():
            arrived(recv.at[pl.ds(0, tiles + 1)], precv)

        @pl.when(jnp.logical_not(is_last))
        def _():
            arrived(halo, hrecv)

    with jax.named_scope("friction"):
        total = recv[first_tile - 1]
        for j in range(n):
            if j != first_tile - 1:
                total = total + recv[j]
        edge = 0.5 * C_TWO * halo[:, 0:1]
        total = total + jnp.where(lane == 4 * cx + fc - 1, edge, 0.0)

        def own_slots():
            own = ownp[3]
            for j in range(per):
                picked = jnp.sum(total * picks[j : j + 1], axis=1, keepdims=True)
                own = own + jnp.where(lane_one == cx + j, picked, 0.0)
            state[0] = own

        @pl.when(is_tile)
        def _():
            fields = [total[:, :128]]
            for f in range(1, 4):
                fields.append(pltpu.roll(total, wide - f * cx, 1)[:, :128])
            used = lane_one < cx
            fields = [jnp.where(used, field, 1.0) for field in fields]
            tau = fields[3]
            for t in range(tiles):
                moved = pltpu.roll(total, wide - (4 + t) * cx, 1)[:, :128]
                tau = tau + jnp.where(jnp.logical_and(used, my_tile == t), moved, 0.0)
            rates[...] = 0.5 * friction(tau, *fields[:3])
            own_slots()

        pl.when(jnp.logical_not(is_tile))(own_slots)

    def fix(columns):
        for start in range(0, len(columns), 4):
            parts = []
            for i in columns[start : start + 4]:
                s = rates[:, i : i + 1]
                low = out[0, i, :, row - 128 : row]
                high = out[0, i, :, row : row + 128]
                low = low - jnp.where(lane_one == 127, s, 0.0)
                high = high + jnp.where(lane_one == 0, s, 0.0)
                parts.append((i, low, high))
            for i, low, high in parts:
                out[0, i, :, row - 128 : row] = low
                out[0, i, :, row : row + 128] = high

    with jax.named_scope("fix"):

        @pl.when(is_tile)
        def _():
            fix(range(2, cx - 2))

    pl.when(jnp.logical_not(outside))(add_edges)

    with jax.named_scope("mean"):

        @pl.when(is_tile)
        def _():
            parts = []
            for i in edges:
                low = out[0, i, :, row - 128 : row]
                high = out[0, i, :, row : row + 128]
                mean = 0.5 * (high + pltpu.roll(low, 1, 1))
                s = rates[:, i : i + 1]
                low = jnp.where(lane_one == 127, pltpu.roll(mean, 127, 1) - s, low)
                parts.append((i, low, jnp.where(lane_one == 0, mean + s, high)))
            for i, low, high in parts:
                out[0, i, :, row - 128 : row] = low
                out[0, i, :, row : row + 128] = high

    with jax.named_scope("sends_done"):
        @pl.when(near)
        def _():
            arrived(recv.at[pl.ds(0, n - 1)], psend)

        @pl.when(jnp.logical_not(near))
        def _():
            arrived(recv.at[pl.ds(0, tiles)], psend)

        @pl.when(is_last)
        def _():
            arrived(recv.at[pl.ds(0, n - 1), :, pl.ds(0, 128)], hsend)

        @pl.when(has_above)
        def _():
            z_copy(True).wait_send()

        @pl.when(has_below)
        def _():
            z_copy(False).wait_send()

        @pl.when(has_right)
        def _():
            arrived(sx.at[0, pl.ds(0, 4)], xsend.at[0])

        @pl.when(has_left)
        def _():
            arrived(sx.at[0, pl.ds(0, 5)], xsend.at[1])


def write_out(first, held, state, out, slip_out, slip, sem):
    velocity = pltpu.make_async_copy(held, out, sem.at[0])
    velocity.start()
    rate = friction(state[0], state[1], state[2], state[3])
    slip[...] = rate.T[first : first + slip.shape[0]]
    rates = pltpu.make_async_copy(slip, slip_out, sem.at[1])
    rates.start()
    velocity.wait()
    rates.wait()


def per_device(n, nd, velocity, stress, material, patch_order, fault_params):
    _, cx, cz, ny = stress.shape
    fc = patch_order.shape[0]
    per = fc // n
    wide = -(-(4 * cx + fc + 2) // 128) * 128
    dims = (n, nd, cx, cz, ny, fc, wide)
    tiles = fc // cx
    f32 = jnp.float32
    anywhere = pl.BlockSpec(memory_space=pltpu.HBM)
    dma = pltpu.SemaphoreType.DMA
    params = jnp.transpose(fault_params, (2, 0, 1))
    big = (velocity, stress, material, patch_order, params)
    held = pl.pallas_call(
        functools.partial(kernel, dims),
        out_shape=(
            jax.ShapeDtypeStruct(velocity.shape, f32),
            jax.ShapeDtypeStruct((4, cz, 128), f32),
        ),
        in_specs=[anywhere] * 5,
        out_specs=(pl.BlockSpec(memory_space=pltpu.VMEM), pl.BlockSpec(memory_space=pltpu.VMEM)),
        scratch_shapes=[
            pltpu.SMEM((fc,), jnp.int32),
            pltpu.VMEM((2, cx, cz, 128), f32),
            pltpu.VMEM((3, cx + 4, cz, ny), f32),
            pltpu.VMEM((3, cx, cz, ny), f32),
            pltpu.VMEM((3, cx, cz, ny), f32),
            pltpu.VMEM((cx, cz, ny), jnp.int32),
            pltpu.VMEM((cx, cz, ny), f32),
            pltpu.VMEM((per, 4, cz), f32),
            pltpu.VMEM((4, cz, 128), f32),
            pltpu.VMEM((9, cx, ny), f32),
            pltpu.VMEM((9, cx, ny), f32),
            pltpu.VMEM((tiles, cz, wide), f32),
            pltpu.VMEM((n, cz, wide), f32),
            pltpu.VMEM((cz, 128), f32),
            pltpu.VMEM((cz, 128), f32),
            pltpu.VMEM((-(-per // 8) * 8, wide), f32),
            dma((8,)),
            dma,
            dma,
            dma,
            dma,
            dma((2,)),
            dma((2,)),
            dma((2,)),
            dma((2,)),
            pltpu.SemaphoreType.REGULAR,
            pltpu.SemaphoreType.REGULAR((2,)),
            pltpu.SemaphoreType.REGULAR,
        ],
        compiler_params=pltpu.CompilerParams(collective_id=0, has_side_effects=True, vmem_limit_bytes=12 << 20),
    )(*[pltpu.with_memory_space_constraint(v, pltpu.HBM) for v in big])
    resident = pl.BlockSpec(memory_space=pltpu.VMEM)
    moved, slip = pl.pallas_call(
        functools.partial(write_out, cx),
        out_shape=(
            jax.ShapeDtypeStruct(velocity.shape, f32),
            jax.ShapeDtypeStruct((per, cz), f32),
        ),
        in_specs=[resident, resident],
        out_specs=(anywhere, anywhere),
        scratch_shapes=[pltpu.VMEM((per, cz), f32), dma((2,))],
        compiler_params=pltpu.CompilerParams(vmem_limit_bytes=4 << 20),
    )(*held)
    return moved, slip.T


def solution(mesh):
    n, nd = mesh.shape["strike"], mesh.shape["depth"]
    return jax.shard_map(
        functools.partial(per_device, n, nd),
        mesh=mesh,
        in_specs=(
            P(None, "strike", "depth", None),
            P(None, "strike", "depth", None),
            P("strike", "depth", None),
            P(),
            P(None, "depth", "strike"),
        ),
        out_specs=(P(None, "strike", "depth", None), P("depth", "strike")),
        check_vma=False,
    )
```

```python
import functools

import jax
import jax.numpy as jnp
from jax import lax
from jax.experimental import pallas as pl
from jax.experimental.pallas import tpu as pltpu
from jax.sharding import PartitionSpec as P

NEWTON = 8
BUOY = (1.0, 0.8, 0.6, 1.25)
C_ONE = 9.0 / 8.0
C_TWO = -1.0 / 24.0
MESH = pl.DeviceIdType.MESH


def friction(tau_total, coef, psi, normal_stress):
    half_q = 0.5 * jnp.exp(psi / coef)
    scale = normal_stress * coef
    stiff = scale * half_q
    rate = 0.35 * tau_total / (1.0 + stiff)
    for _ in range(NEWTON - 1):
        arg_val = rate * half_q
        square = 1.0 + arg_val * arg_val
        inverse = lax.rsqrt(square)
        magnitude = jnp.log(jnp.abs(arg_val) + square * inverse)
        resid = tau_total - rate - scale * jnp.where(arg_val < 0, -magnitude, magnitude)
        rate = rate + 0.35 * resid / (1.0 + stiff * inverse)
    return rate


def kernel(
    dims, vel, st, mat, order, fp, out, state,
    po, col, sx, so, vb, mb, bb, pb, ownp, zout, zin, packs, recv, halo, rates, picks,
    lsem, psend, precv, hsend, hrecv, xsend, xrecv, zsend, zrecv, next_in, far_in, depth_in,
):
    n, nd, cx, cz, ny, fc, wide = dims
    row = ny // 2
    per = fc // n
    first_tile = n // 4
    tiles = fc // cx
    me = lax.axis_index("strike")
    dep = lax.axis_index("depth")
    has_left, has_right = me > 0, me < n - 1
    has_below, has_above = dep > 0, dep < nd - 1
    is_tile = jnp.logical_and(me >= first_tile, me < first_tile + tiles)
    near = jnp.logical_and(me >= first_tile - 1, me < first_tile + tiles)

    def tile_at(j):
        return first_tile <= j < first_tile + tiles

    def near_at(j):
        return first_tile - 1 <= j < first_tile + tiles

    last = first_tile + tiles
    is_last = me == last

    def pairs(j):
        inside = jnp.logical_and(j >= first_tile, j < last - 2)
        return jnp.logical_or(j == 0, jnp.logical_and(j % 2 == first_tile % 2, inside))

    paired = pairs(me)
    head = first_tile - 1
    lead = me == head
    beyond = me == last + 1
    is_end = me == last - 1

    def sends_to(j):
        return jnp.logical_and(me != j, jnp.logical_or(near, tile_at(j)))

    def halo_to(j):
        return jnp.logical_and(is_last, me != j)

    def reaches(j):
        return jnp.logical_or(sends_to(j), halo_to(j))

    def reached_by(j):
        return jnp.logical_and(me != j, jnp.logical_or(is_tile, near_at(j) or j == last))

    def partner(j):
        beside = jnp.logical_or(me == j - 1, me == j + 1)
        return jnp.logical_or(beside, jnp.logical_or(reaches(j), reached_by(j)))

    barrier = pltpu.get_barrier_semaphore()
    for j in range(n):

        back = jnp.logical_and(j == me - 1, pairs(j))

        ahead = jnp.logical_and(j > me, partner(j))
        if j == last + 1:
            ahead = jnp.logical_and(ahead, jnp.logical_not(lead))

        @pl.when(jnp.logical_or(ahead, back))
        def _():
            pl.semaphore_signal(barrier, inc=1, device_id=(j, dep), device_id_type=MESH)

    @pl.when(jnp.logical_and(me >= 2, pairs(me - 2)))
    def _():
        pl.semaphore_signal(barrier, inc=1, device_id=(me - 2, dep), device_id_type=MESH)

    @pl.when(beyond)
    def _():
        pl.semaphore_signal(barrier, inc=1, device_id=(last - 1, dep), device_id_type=MESH)

    @pl.when(has_above)
    def _():
        pl.semaphore_signal(barrier, inc=1, device_id=(me, dep + 1), device_id_type=MESH)

    step = cx // 4
    columns = [
        pltpu.make_async_copy(
            st.at[3 * f, pl.ds(k * step, step), :, pl.ds(row, 128)],
            col.at[f, pl.ds(k * step, step)],
            lsem.at[2],
        )
        for k in range(4)
        for f in range(2)
    ]
    small = [
        pltpu.make_async_copy(order, po, lsem.at[0]),
        pltpu.make_async_copy(fp, pb, lsem.at[1]),
    ]
    z_rows = (
        (4, cz - 2), (4, cz - 1), (5, cz - 2), (5, cz - 1), (2, cz - 1),
        (4, 0), (5, 0), (2, 0), (2, 1),
    )
    zloads = [
        pltpu.make_async_copy(st.at[f, :, r], zout.at[k], lsem.at[3])
        for k, (f, r) in enumerate(z_rows)
    ]
    loads = [
        pltpu.make_async_copy(st.at[0], sx.at[0, pl.ds(2, cx)], lsem.at[4]),
        pltpu.make_async_copy(
            st.at[pl.ds(3, 2)], sx.at[pl.ds(1, 2), pl.ds(2, cx)], lsem.at[4]
        ),
        pltpu.make_async_copy(st.at[pl.ds(1, 2)], so.at[pl.ds(0, 2)], lsem.at[5]),
        pltpu.make_async_copy(st.at[5], so.at[2], lsem.at[5]),
        pltpu.make_async_copy(mat, mb, lsem.at[6]),
        pltpu.make_async_copy(vel, vb, lsem.at[7]),
    ]
    for load in small + columns + zloads + loads:
        load.start()

    def arrived(ref, sem):
        pltpu.make_async_copy(ref, ref, sem).wait()

    zlo, zhi = zin.at[pl.ds(0, 5)], zin.at[pl.ds(5, 4)]
    zero_row = jnp.zeros((2, cz, ny), jnp.float32)

    @pl.when(jnp.logical_not(has_left))
    def _():
        for f in range(3):
            sx[f, 0:2] = zero_row

    @pl.when(jnp.logical_not(has_right))
    def _():
        for f in range(3):
            sx[f, cx + 2 : cx + 4] = zero_row

    @pl.when(jnp.logical_not(has_below))
    def _():
        zin[0:5] = jnp.zeros((5, cx, ny), jnp.float32)

    @pl.when(jnp.logical_not(has_above))
    def _():
        zin[5:9] = jnp.zeros((4, cx, ny), jnp.float32)

    for j in range(n):
        if not near_at(j):

            @pl.when(jnp.logical_not(is_tile))
            def _():
                recv[j] = jnp.zeros(recv.shape[1:], jnp.float32)

    def x_copies(up, fields=(0, 1, 2)):
        copies = []
        for f in fields:
            plane = (0, 3, 4)[f]
            if up:
                rows = 2 if f == 0 else 1
                src, dst, to = cx - rows, 2 - rows, me + 1
            else:
                rows = 1 if f == 0 else 2
                src, dst, to = 0, cx + 2, me - 1
            slot = 0 if up else 1
            copies.append(
                pltpu.make_async_remote_copy(
                    src_ref=st.at[plane, pl.ds(src, rows)],
                    dst_ref=sx.at[f, pl.ds(dst, rows)],
                    send_sem=xsend.at[slot],
                    recv_sem=xrecv.at[slot],
                    device_id=(to, dep),
                    device_id_type=MESH,
                )
            )
        return copies

    def z_copy(up):
        return pltpu.make_async_remote_copy(
            src_ref=zout.at[pl.ds(0, 5)] if up else zout.at[pl.ds(5, 4)],
            dst_ref=zlo if up else zhi,
            send_sem=zsend.at[0 if up else 1],
            recv_sem=zrecv.at[0 if up else 1],
            device_id=(me, dep + 1 if up else dep - 1),
            device_id_type=MESH,
        )

    def pack_copy(j):
        return pltpu.make_async_remote_copy(
            src_ref=packs.at[min(max(j - first_tile, 0), tiles - 1)],
            dst_ref=recv.at[me],
            send_sem=psend,
            recv_sem=precv,
            device_id=(j, dep),
            device_id_type=MESH,
        )

    def pack_next():
        for j in range(1, n):

            @pl.when(jnp.logical_and(j == me + 1, sends_to(j)))
            def _():
                pack_copy(j).start()

            @pl.when(jnp.logical_and(j == me + 1, halo_to(j)))
            def _():
                halo_copy(j).start()

    def halo_copy(j):
        return pltpu.make_async_remote_copy(
            src_ref=st.at[0, 0, :, pl.ds(row, 128)],
            dst_ref=halo,
            send_sem=hsend,
            recv_sem=hrecv,
            device_id=(j, dep),
            device_id_type=MESH,
        )

    ahead_of_me = jnp.int32(0)
    for j in range(n):
        ahead_of_me = ahead_of_me + jnp.logical_and(j < me, partner(j)).astype(jnp.int32)
    earlier = ahead_of_me + has_below.astype(jnp.int32) + 2 * paired.astype(jnp.int32)
    earlier = earlier + is_end.astype(jnp.int32) - beyond.astype(jnp.int32)
    late = me > last

    fast = me % 2 == 1

    def enter():
        @pl.when(earlier > 0)
        def _():
            pl.semaphore_wait(barrier, earlier)

        @pl.when(is_end)
        def _():
            pl.semaphore_signal(
                far_in.at[1], inc=1, device_id=(head, dep), device_id_type=MESH
            )

        @pl.when(is_last)
        def _():
            for j in range(last):
                halo_copy(j).start()

        spoken_for = jnp.logical_and(me > 2, pairs(me - 2))
        for j in range(n):
            told = jnp.logical_and(j < me - 1, reached_by(j))
            if j == head:
                told = jnp.logical_and(told, jnp.logical_not(beyond))
            told = jnp.logical_and(told, jnp.logical_not(jnp.logical_and(spoken_for, j == me - 3)))

            @pl.when(told)
            def _():
                pl.semaphore_signal(
                    far_in.at[late.astype(jnp.int32)],
                    inc=1,
                    device_id=(j, dep),
                    device_id_type=MESH,
                )

        @pl.when(paired)
        def _():
            pl.semaphore_signal(next_in, inc=1, device_id=(me + 1, dep), device_id_type=MESH)

        @pl.when(jnp.logical_and(paired, me > 0))
        def _():
            pl.semaphore_signal(
                far_in.at[0], inc=1, device_id=(me - 1, dep), device_id_type=MESH
            )

        silent = jnp.logical_or(pairs(me - 1), jnp.logical_and(me >= 2, pairs(me - 2)))

        @pl.when(jnp.logical_and(has_left, jnp.logical_not(silent)))
        def _():
            pl.semaphore_signal(next_in, inc=1, device_id=(me - 1, dep), device_id_type=MESH)

        @pl.when(has_below)
        def _():
            pl.semaphore_signal(depth_in, inc=1, device_id=(me, dep - 1), device_id_type=MESH)

        @pl.when(jnp.logical_and(has_left, fast))
        def _():
            for copy in x_copies(False, (0,)):
                copy.start()

    with jax.named_scope("entry_fast"):
        pl.when(fast)(enter)

    lane = lax.broadcasted_iota(jnp.int32, (cz, wide), 1)
    lane_one = lax.broadcasted_iota(jnp.int32, (cz, 128), 1)
    my_tile = jnp.clip(me - first_tile, 0, tiles - 1)
    with jax.named_scope("params_wait"):
        for load in small:
            load.wait()
    with jax.named_scope("params"):
        blocks = [jnp.zeros((cz, wide), jnp.float32) for _ in range(tiles)]
        params = [pb[j].T for j in range(per)]
        for f in range(4):
            mine = jnp.full((cz, 128), 1.0, jnp.float32)
            for j in range(per):
                column = po[me * per + j]
                value = params[j][:, f : f + 1]
                mine = jnp.where(lane_one == cx + j, value, mine)
                for t in range(tiles):
                    local = column - t * cx
                    held = jnp.logical_and(local >= 0, local < cx)
                    place = jnp.where(held, f * cx + local, -1)
                    blocks[t] = jnp.where(lane == place, value, blocks[t])
            ownp[f] = mine
            if f < 3:
                state[1 + f] = mine
        for j in range(per):
            slot_lane = lane[0:1] == 4 * cx + po[me * per + j]
            picks[j : j + 1] = jnp.where(slot_lane, 1.0, 0.0)
        for t in range(tiles):
            packs[t] = blocks[t]
    with jax.named_scope("column_wait"):
        arrived(col, lsem.at[2])
    with jax.named_scope("pack"):

        @pl.when(near)
        def _():
            base = 4 * cx + (me - first_tile) * cx
            normal = jnp.zeros((cz, wide), jnp.float32)
            shear = jnp.zeros((cz, wide), jnp.float32)
            for i in range(cx):
                here = lane == base + i
                normal = jnp.where(here, col[0, i, :, 0:1], normal)
                shear = jnp.where(here, col[1, i, :, 0:1], shear)
            dxx = C_ONE * (normal - pltpu.roll(normal, 1, 1)) + C_TWO * (
                pltpu.roll(normal, wide - 1, 1) - pltpu.roll(normal, 2, 1)
            )
            share = shear + 0.5 * dxx
            inside = jnp.logical_and(lane >= 4 * cx, lane < 4 * cx + fc)
            share = jnp.where(inside, share, 0.0)
            for t in range(tiles):
                packs[t] = packs[t] + share
            recv[me] = packs[my_tile]

        @pl.when(is_last)
        def _():
            halo[...] = col[0, 0]

    with jax.named_scope("entry_slow"):
        pl.when(jnp.logical_not(fast))(enter)

    for j in range(n):

        @pl.when(jnp.logical_and(j < me, sends_to(j)))
        def _():
            pack_copy(j).start()

    @pl.when(paired)
    def _():
        pack_next()

    @pl.when(jnp.logical_and(has_left, fast))
    def _():
        for copy in x_copies(False, (1, 2)):
            copy.start()

    @pl.when(jnp.logical_and(has_left, jnp.logical_not(fast)))
    def _():
        for copy in x_copies(False):
            copy.start()

    @pl.when(paired)
    def _():
        for copy in x_copies(True):
            copy.start()

    with jax.named_scope("z_loads"):
        arrived(zout, lsem.at[3])

    @pl.when(has_below)
    def _():
        z_copy(False).start()

    def send_far(low, high, kind):
        group = [
            (j, jnp.logical_and(j > me + 1, reaches(j))) for j in range(low, high)
        ]
        count = sum(on.astype(jnp.int32) for _, on in group)

        @pl.when(count > 0)
        def _():
            pl.semaphore_wait(far_in.at[kind], count)

        for j, on in group:

            @pl.when(jnp.logical_and(on, sends_to(j)))
            def _():
                pack_copy(j).start()

            @pl.when(jnp.logical_and(on, halo_to(j)))
            def _():
                halo_copy(j).start()

    with jax.named_scope("wait_next"):

        @pl.when(jnp.logical_and(has_right, jnp.logical_not(paired)))
        def _():
            pl.semaphore_wait(next_in, 1)
            pack_next()
            for copy in x_copies(True):
                copy.start()

        @pl.when(has_above)
        def _():
            pl.semaphore_wait(depth_in, 1)
            z_copy(True).start()

    with jax.named_scope("lead_far"):
        @pl.when(lead)
        def _():
            send_far(2, last + 1, 0)
            send_far(last + 1, n, 1)

    with jax.named_scope("loads"):
        arrived(sx.at[:, pl.ds(2, cx)], lsem.at[4])
        arrived(so, lsem.at[5])
        arrived(mb, lsem.at[6])
        arrived(vb, lsem.at[7])

    yi = lax.broadcasted_iota(jnp.int32, (cz, ny), 1)
    zi = lax.broadcasted_iota(jnp.int32, (cz, ny), 0)

    def y_at(field, offset):
        moved = pltpu.roll(field, (-offset) % ny, 1)
        keep = yi < ny - offset if offset > 0 else yi >= -offset
        return jnp.where(keep, moved, 0.0)

    def z_at(field):
        def at(offset):
            if offset == 0:
                return field
            moved = pltpu.roll(field, (-offset) % cz, 0)
            keep = zi < cz - offset if offset > 0 else zi >= -offset
            return jnp.where(keep, moved, 0.0)

        return at

    def minus(at):
        return C_ONE * (at(0) - at(-1)) + C_TWO * (at(1) - at(-2))

    def plus(at):
        return C_ONE * (at(1) - at(0)) + C_TWO * (at(2) - at(-1))

    def along_x(f, x):
        return lambda offset: sx[f, x + 2 + offset]

    def along_y(field):
        return lambda offset: field if offset == 0 else y_at(field, offset)

    def buoyancy(x):
        material = mb[x]
        b = jnp.full((cz, ny), 0.25 * BUOY[0], jnp.float32)
        for index in range(1, 4):
            b = jnp.where(material == index, 0.25 * BUOY[index], b)
        bb[x] = b
        return b

    def across(x):
        return minus(along_x(0, x)), plus(along_x(1, x)), plus(along_x(2, x))

    def local(x):
        sxz, szz, syz = sx[2, x + 2], so[1, x], so[2, x]
        return (
            minus(along_y(sx[1, x + 2])) + minus(z_at(sxz)),
            plus(along_y(so[0, x])) + minus(z_at(syz)),
            plus(along_y(syz)) + plus(z_at(szz)),
        )

    def inner(x, carry):
        b, along, rest = buoyancy(x), across(x), local(x)
        for c in range(3):
            out[c, x] = vb[c, x] + b * (along[c] + rest[c])
        return carry

    def outer(x):
        b, rest = buoyancy(x), local(x)
        for c in range(3):
            out[c, x] = vb[c, x] + b * rest[c]

    edges = (0, 1, cx - 2, cx - 1)
    with jax.named_scope("outer"):
        for x in edges:
            outer(x)

    middle = cx // 2
    with jax.named_scope("inner"):
        lax.fori_loop(2, middle, inner, 0)

    with jax.named_scope("wait_far"):
        pl.when(jnp.logical_not(lead))(lambda: send_far(2, last + 1, 0))
    with jax.named_scope("wait_far2"):
        pl.when(jnp.logical_not(lead))(lambda: send_far(last + 1, n, 1))

    with jax.named_scope("inner2"):
        lax.fori_loop(middle, cx - 2, inner, 0)
    with jax.named_scope("z_wait"):

        @pl.when(has_below)
        def _():
            z_copy(True).wait_recv()

        @pl.when(has_above)
        def _():
            z_copy(False).wait_recv()

    first = lax.broadcasted_iota(jnp.int32, (8, ny), 0)

    def face(x, carry):
        def low(k):
            return zin[k, pl.ds(x, 1), :]

        def high(k):
            return zin[5 + k, pl.ds(x, 1), :]

        def put(at, one, two):
            return jnp.where(first == at, one, jnp.where(first == two[0], two[1], 0.0))

        b = bb[x, 0:8]
        out[0, x, 0:8] -= b * put(0, C_ONE * low(1) + C_TWO * low(0), (1, C_TWO * low(1)))
        out[1, x, 0:8] -= b * put(0, C_ONE * low(3) + C_TWO * low(2), (1, C_TWO * low(3)))
        out[2, x, 0:8] -= b * jnp.where(first == 0, C_TWO * low(4), 0.0)
        b = bb[x, cz - 8 : cz]
        out[0, x, cz - 8 : cz] += b * jnp.where(first == 7, C_TWO * high(0), 0.0)
        out[1, x, cz - 8 : cz] += b * jnp.where(first == 7, C_TWO * high(1), 0.0)
        out[2, x, cz - 8 : cz] += b * put(
            7, C_ONE * high(2) + C_TWO * high(3), (6, C_TWO * high(2))
        )
        return carry

    with jax.named_scope("face"):
        lax.fori_loop(0, cx, face, 0)

    def level(columns):
        for start in range(0, len(columns), 4):
            parts = []
            for i in columns[start : start + 4]:
                low = out[0, i, :, row - 128 : row]
                high = out[0, i, :, row : row + 128]
                above = 0.5 * (high + pltpu.roll(low, 1, 1))
                below = 0.5 * (pltpu.roll(high, 127, 1) + low)
                low = jnp.where(lane_one == 127, below, low)
                parts.append((i, low, jnp.where(lane_one == 0, above, high)))
            for i, low, high in parts:
                out[0, i, :, row - 128 : row] = low
                out[0, i, :, row : row + 128] = high

    with jax.named_scope("mean_inside"):

        @pl.when(is_tile)
        def _():
            level(range(2, cx - 2))

    outside = jnp.logical_or(me < head, me > last)

    def add_edges():
        with jax.named_scope("x_wait"):

            @pl.when(has_left)
            def _():
                arrived(sx.at[0, pl.ds(0, 4)], xrecv.at[0])

            @pl.when(has_right)
            def _():
                arrived(sx.at[0, pl.ds(0, 5)], xrecv.at[1])

        with jax.named_scope("edges"):
            for x in edges:
                along = across(x)
                for c in range(3):
                    out[c, x] += bb[x] * along[c]

    pl.when(outside)(add_edges)

    with jax.named_scope("pack_wait"):
        @pl.when(is_tile)
        def _():
            arrived(recv.at[pl.ds(0, n - 1)], precv)

        @pl.when(me == first_tile - 1)
        def _():
            arrived(recv.at[pl.ds(0, tiles)], precv)

        @pl.when(jnp.logical_not(near))
        def _():
            arrived(recv.at[pl.ds(0, tiles + 1)], precv)

        @pl.when(jnp.logical_not(is_last))
        def _():
            arrived(halo, hrecv)

    with jax.named_scope("friction"):
        total = recv[first_tile - 1]
        for j in range(n):
            if j != first_tile - 1:
                total = total + recv[j]
        edge = 0.5 * C_TWO * halo[:, 0:1]
        total = total + jnp.where(lane == 4 * cx + fc - 1, edge, 0.0)

        def own_slots():
            own = ownp[3]
            for j in range(per):
                picked = jnp.sum(total * picks[j : j + 1], axis=1, keepdims=True)
                own = own + jnp.where(lane_one == cx + j, picked, 0.0)
            state[0] = own

        @pl.when(is_tile)
        def _():
            fields = [total[:, :128]]
            for f in range(1, 4):
                fields.append(pltpu.roll(total, wide - f * cx, 1)[:, :128])
            used = lane_one < cx
            fields = [jnp.where(used, field, 1.0) for field in fields]
            tau = fields[3]
            for t in range(tiles):
                moved = pltpu.roll(total, wide - (4 + t) * cx, 1)[:, :128]
                tau = tau + jnp.where(jnp.logical_and(used, my_tile == t), moved, 0.0)
            rates[...] = 0.5 * friction(tau, *fields[:3])
            own_slots()

        pl.when(jnp.logical_not(is_tile))(own_slots)

    def fix(columns):
        for start in range(0, len(columns), 4):
            parts = []
            for i in columns[start : start + 4]:
                s = rates[:, i : i + 1]
                low = out[0, i, :, row - 128 : row]
                high = out[0, i, :, row : row + 128]
                low = low - jnp.where(lane_one == 127, s, 0.0)
                high = high + jnp.where(lane_one == 0, s, 0.0)
                parts.append((i, low, high))
            for i, low, high in parts:
                out[0, i, :, row - 128 : row] = low
                out[0, i, :, row : row + 128] = high

    with jax.named_scope("fix"):

        @pl.when(is_tile)
        def _():
            fix(range(2, cx - 2))

    pl.when(jnp.logical_not(outside))(add_edges)

    with jax.named_scope("mean"):

        @pl.when(is_tile)
        def _():
            parts = []
            for i in edges:
                low = out[0, i, :, row - 128 : row]
                high = out[0, i, :, row : row + 128]
                above = 0.5 * (high + pltpu.roll(low, 1, 1))
                below = 0.5 * (pltpu.roll(high, 127, 1) + low)
                s = rates[:, i : i + 1]
                low = jnp.where(lane_one == 127, below - s, low)
                parts.append((i, low, jnp.where(lane_one == 0, above + s, high)))
            for i, low, high in parts:
                out[0, i, :, row - 128 : row] = low
                out[0, i, :, row : row + 128] = high

    with jax.named_scope("sends_done"):
        @pl.when(near)
        def _():
            arrived(recv.at[pl.ds(0, n - 1)], psend)

        @pl.when(jnp.logical_not(near))
        def _():
            arrived(recv.at[pl.ds(0, tiles)], psend)

        @pl.when(is_last)
        def _():
            arrived(recv.at[pl.ds(0, n - 1), :, pl.ds(0, 128)], hsend)

        @pl.when(has_above)
        def _():
            z_copy(True).wait_send()

        @pl.when(has_below)
        def _():
            z_copy(False).wait_send()

        @pl.when(has_right)
        def _():
            arrived(sx.at[0, pl.ds(0, 4)], xsend.at[0])

        @pl.when(has_left)
        def _():
            arrived(sx.at[0, pl.ds(0, 5)], xsend.at[1])


def write_out(first, held, state, out, slip_out, slip, sem):
    velocity = pltpu.make_async_copy(held, out, sem.at[0])
    velocity.start()
    rate = friction(state[0], state[1], state[2], state[3])
    slip[...] = rate.T[first : first + slip.shape[0]]
    rates = pltpu.make_async_copy(slip, slip_out, sem.at[1])
    rates.start()
    velocity.wait()
    rates.wait()


def per_device(n, nd, velocity, stress, material, patch_order, fault_params):
    _, cx, cz, ny = stress.shape
    fc = patch_order.shape[0]
    per = fc // n
    wide = -(-(4 * cx + fc + 2) // 128) * 128
    dims = (n, nd, cx, cz, ny, fc, wide)
    tiles = fc // cx
    f32 = jnp.float32
    anywhere = pl.BlockSpec(memory_space=pltpu.HBM)
    dma = pltpu.SemaphoreType.DMA
    params = jnp.transpose(fault_params, (2, 0, 1))
    big = (velocity, stress, material, patch_order, params)
    held = pl.pallas_call(
        functools.partial(kernel, dims),
        out_shape=(
            jax.ShapeDtypeStruct(velocity.shape, f32),
            jax.ShapeDtypeStruct((4, cz, 128), f32),
        ),
        in_specs=[anywhere] * 5,
        out_specs=(pl.BlockSpec(memory_space=pltpu.VMEM), pl.BlockSpec(memory_space=pltpu.VMEM)),
        scratch_shapes=[
            pltpu.SMEM((fc,), jnp.int32),
            pltpu.VMEM((2, cx, cz, 128), f32),
            pltpu.VMEM((3, cx + 4, cz, ny), f32),
            pltpu.VMEM((3, cx, cz, ny), f32),
            pltpu.VMEM((3, cx, cz, ny), f32),
            pltpu.VMEM((cx, cz, ny), jnp.int32),
            pltpu.VMEM((cx, cz, ny), f32),
            pltpu.VMEM((per, 4, cz), f32),
            pltpu.VMEM((4, cz, 128), f32),
            pltpu.VMEM((9, cx, ny), f32),
            pltpu.VMEM((9, cx, ny), f32),
            pltpu.VMEM((tiles, cz, wide), f32),
            pltpu.VMEM((n, cz, wide), f32),
            pltpu.VMEM((cz, 128), f32),
            pltpu.VMEM((cz, 128), f32),
            pltpu.VMEM((-(-per // 8) * 8, wide), f32),
            dma((8,)),
            dma,
            dma,
            dma,
            dma,
            dma((2,)),
            dma((2,)),
            dma((2,)),
            dma((2,)),
            pltpu.SemaphoreType.REGULAR,
            pltpu.SemaphoreType.REGULAR((2,)),
            pltpu.SemaphoreType.REGULAR,
        ],
        compiler_params=pltpu.CompilerParams(collective_id=0, has_side_effects=True, vmem_limit_bytes=12 << 20),
    )(*[pltpu.with_memory_space_constraint(v, pltpu.HBM) for v in big])
    resident = pl.BlockSpec(memory_space=pltpu.VMEM)
    moved, slip = pl.pallas_call(
        functools.partial(write_out, cx),
        out_shape=(
            jax.ShapeDtypeStruct(velocity.shape, f32),
            jax.ShapeDtypeStruct((per, cz), f32),
        ),
        in_specs=[resident, resident],
        out_specs=(anywhere, anywhere),
        scratch_shapes=[pltpu.VMEM((per, cz), f32), dma((2,))],
        compiler_params=pltpu.CompilerParams(vmem_limit_bytes=4 << 20),
    )(*held)
    return moved, slip.T


def solution(mesh):
    n, nd = mesh.shape["strike"], mesh.shape["depth"]
    return jax.shard_map(
        functools.partial(per_device, n, nd),
        mesh=mesh,
        in_specs=(
            P(None, "strike", "depth", None),
            P(None, "strike", "depth", None),
            P("strike", "depth", None),
            P(),
            P(None, "depth", "strike"),
        ),
        out_specs=(P(None, "strike", "depth", None), P("depth", "strike")),
        check_vma=False,
    )
```

```python
import functools

import jax
import jax.numpy as jnp
from jax import lax
from jax.experimental import pallas as pl
from jax.experimental.pallas import tpu as pltpu
from jax.sharding import PartitionSpec as P

NEWTON = 8
BUOY = (1.0, 0.8, 0.6, 1.25)
C_ONE = 9.0 / 8.0
C_TWO = -1.0 / 24.0
MESH = pl.DeviceIdType.MESH


def friction(tau_total, coef, psi, normal_stress):
    half_q = 0.5 * jnp.exp(psi / coef)
    scale = normal_stress * coef
    stiff = scale * half_q
    rate = 0.35 * tau_total / (1.0 + stiff)
    for _ in range(NEWTON - 1):
        arg_val = rate * half_q
        square = 1.0 + arg_val * arg_val
        inverse = lax.rsqrt(square)
        magnitude = jnp.log(jnp.abs(arg_val) + square * inverse)
        resid = tau_total - rate - scale * jnp.where(arg_val < 0, -magnitude, magnitude)
        rate = rate + 0.35 * resid / (1.0 + stiff * inverse)
    return rate


def kernel(
    dims, vel, st, mat, order, fp, out, sums, ownp, picks,
    po, col, sx, so, vb, mb, bb, pb, zout, zin, packs, recv, halo, rates,
    lsem, psend, precv, hsend, hrecv, xsend, xrecv, zsend, zrecv, next_in, far_in, depth_in,
):
    n, nd, cx, cz, ny, fc, wide = dims
    row = ny // 2
    per = fc // n
    first_tile = n // 4
    tiles = fc // cx
    me = lax.axis_index("strike")
    dep = lax.axis_index("depth")
    has_left, has_right = me > 0, me < n - 1
    has_below, has_above = dep > 0, dep < nd - 1
    is_tile = jnp.logical_and(me >= first_tile, me < first_tile + tiles)
    near = jnp.logical_and(me >= first_tile - 1, me < first_tile + tiles)

    def tile_at(j):
        return first_tile <= j < first_tile + tiles

    def near_at(j):
        return first_tile - 1 <= j < first_tile + tiles

    last = first_tile + tiles
    is_last = me == last

    def pairs(j):
        inside = jnp.logical_and(j >= first_tile, j < last - 2)
        return jnp.logical_or(j == 0, jnp.logical_and(j % 2 == first_tile % 2, inside))

    paired = pairs(me)
    head = first_tile - 1
    lead = me == head
    beyond = me == last + 1
    is_end = me == last - 1

    def sends_to(j):
        return jnp.logical_and(me != j, jnp.logical_or(near, tile_at(j)))

    def halo_to(j):
        return jnp.logical_and(is_last, me != j)

    def reaches(j):
        return jnp.logical_or(sends_to(j), halo_to(j))

    def reached_by(j):
        return jnp.logical_and(me != j, jnp.logical_or(is_tile, near_at(j) or j == last))

    def partner(j):
        beside = jnp.logical_or(me == j - 1, me == j + 1)
        return jnp.logical_or(beside, jnp.logical_or(reaches(j), reached_by(j)))

    barrier = pltpu.get_barrier_semaphore()
    for j in range(n):

        back = jnp.logical_and(j == me - 1, pairs(j))

        ahead = jnp.logical_and(j > me, partner(j))
        if j == last + 1:
            ahead = jnp.logical_and(ahead, jnp.logical_not(lead))

        @pl.when(jnp.logical_or(ahead, back))
        def _():
            pl.semaphore_signal(barrier, inc=1, device_id=(j, dep), device_id_type=MESH)

    @pl.when(jnp.logical_and(me >= 2, pairs(me - 2)))
    def _():
        pl.semaphore_signal(barrier, inc=1, device_id=(me - 2, dep), device_id_type=MESH)

    @pl.when(beyond)
    def _():
        pl.semaphore_signal(barrier, inc=1, device_id=(last - 1, dep), device_id_type=MESH)

    @pl.when(has_above)
    def _():
        pl.semaphore_signal(barrier, inc=1, device_id=(me, dep + 1), device_id_type=MESH)

    step = cx // 4
    columns = [
        pltpu.make_async_copy(
            st.at[3 * f, pl.ds(k * step, step), :, pl.ds(row, 128)],
            col.at[f, pl.ds(k * step, step)],
            lsem.at[2],
        )
        for k in range(4)
        for f in range(2)
    ]
    small = [
        pltpu.make_async_copy(order, po, lsem.at[0]),
        pltpu.make_async_copy(fp, pb, lsem.at[1]),
    ]
    z_rows = (
        (4, cz - 2), (4, cz - 1), (5, cz - 2), (5, cz - 1), (2, cz - 1),
        (4, 0), (5, 0), (2, 0), (2, 1),
    )
    zloads = [
        pltpu.make_async_copy(st.at[f, :, r], zout.at[k], lsem.at[3])
        for k, (f, r) in enumerate(z_rows)
    ]
    loads = [
        pltpu.make_async_copy(st.at[0], sx.at[0, pl.ds(2, cx)], lsem.at[4]),
        pltpu.make_async_copy(
            st.at[pl.ds(3, 2)], sx.at[pl.ds(1, 2), pl.ds(2, cx)], lsem.at[4]
        ),
        pltpu.make_async_copy(st.at[pl.ds(1, 2)], so.at[pl.ds(0, 2)], lsem.at[4]),
        pltpu.make_async_copy(st.at[5], so.at[2], lsem.at[4]),
        pltpu.make_async_copy(mat, mb, lsem.at[5]),
        pltpu.make_async_copy(vel, vb, lsem.at[5]),
    ]
    for load in small + columns + zloads + loads:
        load.start()

    def arrived(ref, sem):
        pltpu.make_async_copy(ref, ref, sem).wait()

    def both_arrived(one, other, first_ref, other_ref, whole_ref, sem):
        @pl.when(jnp.logical_and(one, other))
        def _():
            arrived(whole_ref, sem)

        @pl.when(jnp.logical_and(one, jnp.logical_not(other)))
        def _():
            arrived(first_ref, sem)

        @pl.when(jnp.logical_and(other, jnp.logical_not(one)))
        def _():
            arrived(other_ref, sem)

    zlo, zhi = zin.at[pl.ds(0, 5)], zin.at[pl.ds(5, 4)]
    zero_row = jnp.zeros((2, cz, ny), jnp.float32)

    @pl.when(jnp.logical_not(has_left))
    def _():
        for f in range(3):
            sx[f, 0:2] = zero_row

    @pl.when(jnp.logical_not(has_right))
    def _():
        for f in range(3):
            sx[f, cx + 2 : cx + 4] = zero_row

    @pl.when(jnp.logical_not(has_below))
    def _():
        zin[0:5] = jnp.zeros((5, cx, ny), jnp.float32)

    @pl.when(jnp.logical_not(has_above))
    def _():
        zin[5:9] = jnp.zeros((4, cx, ny), jnp.float32)

    for j in range(n):
        if not near_at(j):

            @pl.when(jnp.logical_not(is_tile))
            def _():
                recv[j] = jnp.zeros(recv.shape[1:], jnp.float32)

    def x_copies(up, fields=(0, 1, 2)):
        copies = []
        for f in fields:
            plane = (0, 3, 4)[f]
            if up:
                rows = 2 if f == 0 else 1
                src, dst, to = cx - rows, 2 - rows, me + 1
            else:
                rows = 1 if f == 0 else 2
                src, dst, to = 0, cx + 2, me - 1
            copies.append(
                pltpu.make_async_remote_copy(
                    src_ref=st.at[plane, pl.ds(src, rows)],
                    dst_ref=sx.at[f, pl.ds(dst, rows)],
                    send_sem=xsend,
                    recv_sem=xrecv,
                    device_id=(to, dep),
                    device_id_type=MESH,
                )
            )
        return copies

    def z_copy(up):
        return pltpu.make_async_remote_copy(
            src_ref=zout.at[pl.ds(0, 5)] if up else zout.at[pl.ds(5, 4)],
            dst_ref=zlo if up else zhi,
            send_sem=zsend,
            recv_sem=zrecv,
            device_id=(me, dep + 1 if up else dep - 1),
            device_id_type=MESH,
        )

    def pack_copy(j):
        return pltpu.make_async_remote_copy(
            src_ref=packs.at[min(max(j - first_tile, 0), tiles - 1)],
            dst_ref=recv.at[me],
            send_sem=psend,
            recv_sem=precv,
            device_id=(j, dep),
            device_id_type=MESH,
        )

    def pack_next():
        for j in range(1, n):

            @pl.when(jnp.logical_and(j == me + 1, sends_to(j)))
            def _():
                pack_copy(j).start()

            @pl.when(jnp.logical_and(j == me + 1, halo_to(j)))
            def _():
                halo_copy(j).start()

    def halo_copy(j):
        return pltpu.make_async_remote_copy(
            src_ref=st.at[0, 0, :, pl.ds(row, 128)],
            dst_ref=halo,
            send_sem=hsend,
            recv_sem=hrecv,
            device_id=(j, dep),
            device_id_type=MESH,
        )

    ahead_of_me = jnp.int32(0)
    for j in range(n):
        ahead_of_me = ahead_of_me + jnp.logical_and(j < me, partner(j)).astype(jnp.int32)
    earlier = ahead_of_me + has_below.astype(jnp.int32) + 2 * paired.astype(jnp.int32)
    earlier = earlier + is_end.astype(jnp.int32) - beyond.astype(jnp.int32)
    late = me > last

    fast = me % 2 == 1

    def enter():
        @pl.when(earlier > 0)
        def _():
            pl.semaphore_wait(barrier, earlier)

        @pl.when(is_end)
        def _():
            pl.semaphore_signal(
                far_in.at[1], inc=1, device_id=(head, dep), device_id_type=MESH
            )

        @pl.when(is_last)
        def _():
            for j in range(last):
                halo_copy(j).start()

        spoken_for = jnp.logical_and(me > 2, pairs(me - 2))
        for j in range(n):
            told = jnp.logical_and(j < me - 1, reached_by(j))
            if j == head:
                told = jnp.logical_and(told, jnp.logical_not(beyond))
            told = jnp.logical_and(told, jnp.logical_not(jnp.logical_and(spoken_for, j == me - 3)))

            @pl.when(told)
            def _():
                pl.semaphore_signal(
                    far_in.at[late.astype(jnp.int32)],
                    inc=1,
                    device_id=(j, dep),
                    device_id_type=MESH,
                )

        @pl.when(paired)
        def _():
            pl.semaphore_signal(next_in, inc=1, device_id=(me + 1, dep), device_id_type=MESH)

        @pl.when(jnp.logical_and(paired, me > 0))
        def _():
            pl.semaphore_signal(
                far_in.at[0], inc=1, device_id=(me - 1, dep), device_id_type=MESH
            )

        silent = jnp.logical_or(pairs(me - 1), jnp.logical_and(me >= 2, pairs(me - 2)))

        @pl.when(jnp.logical_and(has_left, jnp.logical_not(silent)))
        def _():
            pl.semaphore_signal(next_in, inc=1, device_id=(me - 1, dep), device_id_type=MESH)

        @pl.when(has_below)
        def _():
            pl.semaphore_signal(depth_in, inc=1, device_id=(me, dep - 1), device_id_type=MESH)

        @pl.when(jnp.logical_and(has_left, fast))
        def _():
            for copy in x_copies(False, (1,)):
                copy.start()

    with jax.named_scope("entry_fast"):
        pl.when(fast)(enter)

    lane = lax.broadcasted_iota(jnp.int32, (cz, wide), 1)
    lane_one = lax.broadcasted_iota(jnp.int32, (cz, 128), 1)
    my_tile = jnp.clip(me - first_tile, 0, tiles - 1)
    with jax.named_scope("params_wait"):
        for load in small:
            load.wait()
    with jax.named_scope("params"):
        blocks = [jnp.zeros((cz, wide), jnp.float32) for _ in range(tiles)]
        params = [pb[j].T for j in range(per)]
        for f in range(4):
            mine = jnp.full((cz, 128), 1.0, jnp.float32)
            for j in range(per):
                column = po[me * per + j]
                value = params[j][:, f : f + 1]
                mine = jnp.where(lane_one == cx + j, value, mine)
                for t in range(tiles):
                    local = column - t * cx
                    held = jnp.logical_and(local >= 0, local < cx)
                    place = jnp.where(held, f * cx + local, -1)
                    blocks[t] = jnp.where(lane == place, value, blocks[t])
            ownp[f] = mine
        for j in range(per):
            slot_lane = lane[0:1] == 4 * cx + po[me * per + j]
            picks[j : j + 1] = jnp.where(slot_lane, 1.0, 0.0)
        for t in range(tiles):
            packs[t] = blocks[t]
    with jax.named_scope("column_wait"):
        arrived(col, lsem.at[2])
    with jax.named_scope("pack"):

        @pl.when(near)
        def _():
            base = 4 * cx + (me - first_tile) * cx
            normal = jnp.zeros((cz, wide), jnp.float32)
            shear = jnp.zeros((cz, wide), jnp.float32)
            for i in range(cx):
                here = lane == base + i
                normal = jnp.where(here, col[0, i, :, 0:1], normal)
                shear = jnp.where(here, col[1, i, :, 0:1], shear)
            dxx = C_ONE * (normal - pltpu.roll(normal, 1, 1)) + C_TWO * (
                pltpu.roll(normal, wide - 1, 1) - pltpu.roll(normal, 2, 1)
            )
            share = shear + 0.5 * dxx
            inside = jnp.logical_and(lane >= 4 * cx, lane < 4 * cx + fc)
            share = jnp.where(inside, share, 0.0)
            for t in range(tiles):
                packs[t] = packs[t] + share
            recv[me] = packs[my_tile]

        @pl.when(is_last)
        def _():
            halo[...] = col[0, 0]

    with jax.named_scope("entry_slow"):
        pl.when(jnp.logical_not(fast))(enter)

    for j in range(n):

        @pl.when(jnp.logical_and(j < me, sends_to(j)))
        def _():
            pack_copy(j).start()

    @pl.when(paired)
    def _():
        pack_next()

    @pl.when(jnp.logical_and(has_left, fast))
    def _():
        for copy in x_copies(False, (0, 2)):
            copy.start()

    @pl.when(jnp.logical_and(has_left, jnp.logical_not(fast)))
    def _():
        for copy in x_copies(False):
            copy.start()

    @pl.when(paired)
    def _():
        for copy in x_copies(True):
            copy.start()

    with jax.named_scope("z_loads"):
        arrived(zout, lsem.at[3])

    @pl.when(has_below)
    def _():
        z_copy(False).start()

    def send_far(low, high, kind):
        group = [
            (j, jnp.logical_and(j > me + 1, reaches(j))) for j in range(low, high)
        ]
        count = sum(on.astype(jnp.int32) for _, on in group)

        @pl.when(count > 0)
        def _():
            pl.semaphore_wait(far_in.at[kind], count)

        for j, on in group:

            @pl.when(jnp.logical_and(on, sends_to(j)))
            def _():
                pack_copy(j).start()

            @pl.when(jnp.logical_and(on, halo_to(j)))
            def _():
                halo_copy(j).start()

    with jax.named_scope("wait_next"):

        @pl.when(jnp.logical_and(has_right, jnp.logical_not(paired)))
        def _():
            pl.semaphore_wait(next_in, 1)
            pack_next()
            for copy in x_copies(True):
                copy.start()

        @pl.when(has_above)
        def _():
            pl.semaphore_wait(depth_in, 1)
            z_copy(True).start()

    with jax.named_scope("lead_far"):
        @pl.when(lead)
        def _():
            send_far(2, last + 1, 0)
            send_far(last + 1, n, 1)

    with jax.named_scope("loads"):
        arrived(st, lsem.at[4])
        arrived(st.at[pl.ds(0, 4)], lsem.at[5])

    yi = lax.broadcasted_iota(jnp.int32, (cz, ny), 1)
    zi = lax.broadcasted_iota(jnp.int32, (cz, ny), 0)

    def y_at(field, offset):
        moved = pltpu.roll(field, (-offset) % ny, 1)
        keep = yi < ny - offset if offset > 0 else yi >= -offset
        return jnp.where(keep, moved, 0.0)

    def z_at(field):
        def at(offset):
            if offset == 0:
                return field
            moved = pltpu.roll(field, (-offset) % cz, 0)
            keep = zi < cz - offset if offset > 0 else zi >= -offset
            return jnp.where(keep, moved, 0.0)

        return at

    def minus(at):
        return C_ONE * (at(0) - at(-1)) + C_TWO * (at(1) - at(-2))

    def plus(at):
        return C_ONE * (at(1) - at(0)) + C_TWO * (at(2) - at(-1))

    def along_x(f, x):
        return lambda offset: sx[f, x + 2 + offset]

    def along_y(field):
        return lambda offset: field if offset == 0 else y_at(field, offset)

    def buoyancy(x):
        material = mb[x]
        b = jnp.full((cz, ny), 0.25 * BUOY[0], jnp.float32)
        for index in range(1, 4):
            b = jnp.where(material == index, 0.25 * BUOY[index], b)
        bb[x] = b
        return b

    def across(x):
        return minus(along_x(0, x)), plus(along_x(1, x)), plus(along_x(2, x))

    def local(x):
        sxz, szz, syz = sx[2, x + 2], so[1, x], so[2, x]
        return (
            minus(along_y(sx[1, x + 2])) + minus(z_at(sxz)),
            plus(along_y(so[0, x])) + minus(z_at(syz)),
            plus(along_y(syz)) + plus(z_at(szz)),
        )

    def inner(x, carry):
        b, along, rest = buoyancy(x), across(x), local(x)
        for c in range(3):
            out[c, x] = vb[c, x] + b * (along[c] + rest[c])
        return carry

    def outer(x):
        b, rest = buoyancy(x), local(x)
        for c in range(3):
            out[c, x] = vb[c, x] + b * rest[c]

    edges = (0, 1, cx - 2, cx - 1)
    with jax.named_scope("outer"):
        for x in edges:
            outer(x)

    middle = cx // 2
    with jax.named_scope("inner"):
        lax.fori_loop(2, middle, inner, 0)

    with jax.named_scope("wait_far"):
        pl.when(jnp.logical_not(lead))(lambda: send_far(2, last + 1, 0))
    with jax.named_scope("wait_far2"):
        pl.when(jnp.logical_not(lead))(lambda: send_far(last + 1, n, 1))

    with jax.named_scope("inner2"):
        lax.fori_loop(middle, cx - 2, inner, 0)
    def z_done(up, down, sem):
        both_arrived(up, down, zin.at[pl.ds(0, 5)], zin.at[pl.ds(0, 4)], zin, sem)

    with jax.named_scope("z_wait"):

        z_done(has_below, has_above, zrecv)

    first = lax.broadcasted_iota(jnp.int32, (8, ny), 0)

    def face(x, carry):
        def low(k):
            return zin[k, pl.ds(x, 1), :]

        def high(k):
            return zin[5 + k, pl.ds(x, 1), :]

        def put(at, one, two):
            return jnp.where(first == at, one, jnp.where(first == two[0], two[1], 0.0))

        b = bb[x, 0:8]
        out[0, x, 0:8] -= b * put(0, C_ONE * low(1) + C_TWO * low(0), (1, C_TWO * low(1)))
        out[1, x, 0:8] -= b * put(0, C_ONE * low(3) + C_TWO * low(2), (1, C_TWO * low(3)))
        out[2, x, 0:8] -= b * jnp.where(first == 0, C_TWO * low(4), 0.0)
        b = bb[x, cz - 8 : cz]
        out[0, x, cz - 8 : cz] += b * jnp.where(first == 7, C_TWO * high(0), 0.0)
        out[1, x, cz - 8 : cz] += b * jnp.where(first == 7, C_TWO * high(1), 0.0)
        out[2, x, cz - 8 : cz] += b * put(
            7, C_ONE * high(2) + C_TWO * high(3), (6, C_TWO * high(2))
        )
        return carry

    with jax.named_scope("face"):
        lax.fori_loop(0, cx, face, 0)

    def level(columns):
        for start in range(0, len(columns), 4):
            parts = []
            for i in columns[start : start + 4]:
                low = out[0, i, :, row - 128 : row]
                high = out[0, i, :, row : row + 128]
                above = 0.5 * (high + pltpu.roll(low, 1, 1))
                below = 0.5 * (pltpu.roll(high, 127, 1) + low)
                low = jnp.where(lane_one == 127, below, low)
                parts.append((i, low, jnp.where(lane_one == 0, above, high)))
            for i, low, high in parts:
                out[0, i, :, row - 128 : row] = low
                out[0, i, :, row : row + 128] = high

    with jax.named_scope("mean_inside"):

        @pl.when(is_tile)
        def _():
            level(range(2, cx - 2))

    outside = jnp.logical_or(me < head, me > last)

    def x_done(up, down, sem):
        line = sx.at[0]
        both_arrived(
            up, down, line.at[pl.ds(0, 4)], line.at[pl.ds(0, 5)], line.at[pl.ds(0, 9)], sem
        )

    def add_edges(on_fault=False):
        with jax.named_scope("x_wait"):

            x_done(has_left, has_right, xrecv)

        with jax.named_scope("edges"):
            for x in edges:
                along = across(x)
                for c in range(1, 3):
                    out[c, x] += bb[x] * along[c]
                value = out[0, x] + bb[x] * along[0]
                if not on_fault:
                    out[0, x] = value
                    continue
                low, high = value[:, row - 128 : row], value[:, row : row + 128]
                above = 0.5 * (high + pltpu.roll(low, 1, 1))
                below = 0.5 * (pltpu.roll(high, 127, 1) + low)
                s = rates[:, x : x + 1]
                low = jnp.where(lane_one == 127, below - s, low)
                high = jnp.where(lane_one == 0, above + s, high)
                out[0, x, :, row - 128 : row] = low
                out[0, x, :, row : row + 128] = high
                if row > 128:
                    out[0, x, :, : row - 128] = value[:, : row - 128]
                    out[0, x, :, row + 128 :] = value[:, row + 128 :]

    pl.when(outside)(add_edges)

    with jax.named_scope("pack_wait"):
        @pl.when(is_tile)
        def _():
            arrived(recv.at[pl.ds(0, n - 1)], precv)

        @pl.when(me == first_tile - 1)
        def _():
            arrived(recv.at[pl.ds(0, tiles)], precv)

        @pl.when(jnp.logical_not(near))
        def _():
            arrived(recv.at[pl.ds(0, tiles + 1)], precv)

        @pl.when(jnp.logical_not(is_last))
        def _():
            arrived(halo, hrecv)

    with jax.named_scope("friction"):
        total = recv[first_tile - 1]
        for j in range(n):
            if j != first_tile - 1:
                total = total + recv[j]
        edge = 0.5 * C_TWO * halo[:, 0:1]
        total = total + jnp.where(lane == 4 * cx + fc - 1, edge, 0.0)

        sums[...] = total

        @pl.when(is_tile)
        def _():
            fields = [total[:, :128]]
            for f in range(1, 4):
                fields.append(pltpu.roll(total, wide - f * cx, 1)[:, :128])
            used = lane_one < cx
            fields = [jnp.where(used, field, 1.0) for field in fields]
            tau = fields[3]
            for t in range(tiles):
                moved = pltpu.roll(total, wide - (4 + t) * cx, 1)[:, :128]
                tau = tau + jnp.where(jnp.logical_and(used, my_tile == t), moved, 0.0)
            rates[...] = 0.5 * friction(tau, *fields[:3])

    def fix(columns):
        for start in range(0, len(columns), 4):
            parts = []
            for i in columns[start : start + 4]:
                s = rates[:, i : i + 1]
                low = out[0, i, :, row - 128 : row]
                high = out[0, i, :, row : row + 128]
                low = low - jnp.where(lane_one == 127, s, 0.0)
                high = high + jnp.where(lane_one == 0, s, 0.0)
                parts.append((i, low, high))
            for i, low, high in parts:
                out[0, i, :, row - 128 : row] = low
                out[0, i, :, row : row + 128] = high

    with jax.named_scope("fix"):

        @pl.when(is_tile)
        def _():
            fix(range(2, cx - 2))

    pl.when(jnp.logical_or(lead, is_last))(add_edges)
    pl.when(is_tile)(functools.partial(add_edges, True))

    with jax.named_scope("sends_done"):
        @pl.when(near)
        def _():
            arrived(recv.at[pl.ds(0, n - 1)], psend)

        @pl.when(jnp.logical_not(near))
        def _():
            arrived(recv.at[pl.ds(0, tiles)], psend)

        @pl.when(is_last)
        def _():
            arrived(recv.at[pl.ds(0, n - 1), :, pl.ds(0, 128)], hsend)

        z_done(has_above, has_below, zsend)
        x_done(has_right, has_left, xsend)


def write_out(first, held, sums, params, picks, out, slip_out, slip, sem):
    velocity = pltpu.make_async_copy(held, out, sem.at[0])
    velocity.start()
    lane = lax.broadcasted_iota(jnp.int32, params.shape[1:], 1)
    total, tau = sums[...], params[3]
    for j in range(slip.shape[0]):
        picked = jnp.sum(total * picks[j : j + 1], axis=1, keepdims=True)
        tau = tau + jnp.where(lane == first + j, picked, 0.0)
    rate = friction(tau, params[0], params[1], params[2])
    slip[...] = rate.T[first : first + slip.shape[0]]
    rates = pltpu.make_async_copy(slip, slip_out, sem.at[1])
    rates.start()
    velocity.wait()
    rates.wait()


def per_device(n, nd, velocity, stress, material, patch_order, fault_params):
    _, cx, cz, ny = stress.shape
    fc = patch_order.shape[0]
    per = fc // n
    wide = -(-(4 * cx + fc + 2) // 128) * 128
    dims = (n, nd, cx, cz, ny, fc, wide)
    tiles = fc // cx
    f32 = jnp.float32
    anywhere = pl.BlockSpec(memory_space=pltpu.HBM)
    dma = pltpu.SemaphoreType.DMA
    params = jnp.transpose(fault_params, (2, 0, 1))
    big = (velocity, stress, material, patch_order, params)
    held = pl.pallas_call(
        functools.partial(kernel, dims),
        out_shape=(
            jax.ShapeDtypeStruct(velocity.shape, f32),
            jax.ShapeDtypeStruct((cz, wide), f32),
            jax.ShapeDtypeStruct((4, cz, 128), f32),
            jax.ShapeDtypeStruct((-(-per // 8) * 8, wide), f32),
        ),
        in_specs=[anywhere] * 5,
        out_specs=(pl.BlockSpec(memory_space=pltpu.VMEM),) * 4,
        scratch_shapes=[
            pltpu.SMEM((fc,), jnp.int32),
            pltpu.VMEM((2, cx, cz, 128), f32),
            pltpu.VMEM((3, cx + 4, cz, ny), f32),
            pltpu.VMEM((3, cx, cz, ny), f32),
            pltpu.VMEM((3, cx, cz, ny), f32),
            pltpu.VMEM((cx, cz, ny), jnp.int32),
            pltpu.VMEM((cx, cz, ny), f32),
            pltpu.VMEM((per, 4, cz), f32),
            pltpu.VMEM((9, cx, ny), f32),
            pltpu.VMEM((9, cx, ny), f32),
            pltpu.VMEM((tiles, cz, wide), f32),
            pltpu.VMEM((n, cz, wide), f32),
            pltpu.VMEM((cz, 128), f32),
            pltpu.VMEM((cz, 128), f32),
            dma((6,)),
            dma,
            dma,
            dma,
            dma,
            dma,
            dma,
            dma,
            dma,
            pltpu.SemaphoreType.REGULAR,
            pltpu.SemaphoreType.REGULAR((2,)),
            pltpu.SemaphoreType.REGULAR,
        ],
        compiler_params=pltpu.CompilerParams(collective_id=0, has_side_effects=True, vmem_limit_bytes=12 << 20),
    )(*[pltpu.with_memory_space_constraint(v, pltpu.HBM) for v in big])
    resident = pl.BlockSpec(memory_space=pltpu.VMEM)
    moved, slip = pl.pallas_call(
        functools.partial(write_out, cx),
        out_shape=(
            jax.ShapeDtypeStruct(velocity.shape, f32),
            jax.ShapeDtypeStruct((per, cz), f32),
        ),
        in_specs=[resident] * 4,
        out_specs=(anywhere, anywhere),
        scratch_shapes=[pltpu.VMEM((per, cz), f32), dma((2,))],
        compiler_params=pltpu.CompilerParams(vmem_limit_bytes=4 << 20),
    )(*held)
    return moved, slip.T


def solution(mesh):
    n, nd = mesh.shape["strike"], mesh.shape["depth"]
    return jax.shard_map(
        functools.partial(per_device, n, nd),
        mesh=mesh,
        in_specs=(
            P(None, "strike", "depth", None),
            P(None, "strike", "depth", None),
            P("strike", "depth", None),
            P(),
            P(None, "depth", "strike"),
        ),
        out_specs=(P(None, "strike", "depth", None), P("depth", "strike")),
        check_vma=False,
    )
```

```python
import functools

import jax
import jax.numpy as jnp
from jax import lax
from jax.experimental import pallas as pl
from jax.experimental.pallas import tpu as pltpu
from jax.sharding import PartitionSpec as P

NEWTON = 8
BUOY = (1.0, 0.8, 0.6, 1.25)
C_ONE = 9.0 / 8.0
C_TWO = -1.0 / 24.0
MESH = pl.DeviceIdType.MESH


def law(coef, psi, normal_stress):
    half_q = 0.5 * jnp.exp(psi / coef)
    scale = normal_stress * coef
    return half_q, scale, scale * half_q


def friction(tau_total, half_q, scale, stiff):
    rate = 0.35 * tau_total / (1.0 + stiff)
    for _ in range(NEWTON - 1):
        arg_val = rate * half_q
        square = 1.0 + arg_val * arg_val
        inverse = lax.rsqrt(square)
        gain = 0.35 / (1.0 + stiff * inverse)
        magnitude = scale * jnp.log(jnp.abs(arg_val) + square * inverse)
        resid = tau_total - rate - jnp.where(arg_val < 0, -magnitude, magnitude)
        rate = rate + resid * gain
    return rate


def kernel(
    dims, vel, st, mat, order, fp, out, sums, ownp, picks,
    po, col, sx, so, vb, mb, bb, pb, zout, zin, packs, recv, halo, rates,
    lsem, psend, precv, hsend, hrecv, xsend, xrecv, zsend, zrecv, next_in, far_in, depth_in,
):
    n, nd, cx, cz, ny, fc, wide = dims
    row = ny // 2
    per = fc // n
    first_tile = n // 4
    tiles = fc // cx
    me = lax.axis_index("strike")
    dep = lax.axis_index("depth")
    has_left, has_right = me > 0, me < n - 1
    has_below, has_above = dep > 0, dep < nd - 1
    is_tile = jnp.logical_and(me >= first_tile, me < first_tile + tiles)
    near = jnp.logical_and(me >= first_tile - 1, me < first_tile + tiles)

    def tile_at(j):
        return first_tile <= j < first_tile + tiles

    def near_at(j):
        return first_tile - 1 <= j < first_tile + tiles

    last = first_tile + tiles
    is_last = me == last

    def pairs(j):
        inside = jnp.logical_and(j >= first_tile, j < last)
        return jnp.logical_or(j == 0, jnp.logical_and(j % 2 == first_tile % 2, inside))

    paired = pairs(me)
    head = first_tile - 1
    lead = me == head
    beyond = me == last + 1
    is_end = me == last - 1

    def sends_to(j):
        return jnp.logical_and(me != j, jnp.logical_or(near, tile_at(j)))

    def halo_to(j):
        return jnp.logical_and(is_last, me != j)

    def reaches(j):
        return jnp.logical_or(sends_to(j), halo_to(j))

    def reached_by(j):
        return jnp.logical_and(me != j, jnp.logical_or(is_tile, near_at(j) or j == last))

    def partner(j):
        beside = jnp.logical_or(me == j - 1, me == j + 1)
        return jnp.logical_or(beside, jnp.logical_or(reaches(j), reached_by(j)))

    barrier = pltpu.get_barrier_semaphore()
    for j in range(n):

        back = jnp.logical_and(j == me - 1, pairs(j))

        ahead = jnp.logical_and(j > me, partner(j))
        if j == last + 1:
            ahead = jnp.logical_and(ahead, jnp.logical_not(lead))

        @pl.when(jnp.logical_or(ahead, back))
        def _():
            pl.semaphore_signal(barrier, inc=1, device_id=(j, dep), device_id_type=MESH)

    @pl.when(jnp.logical_and(me >= 2, pairs(me - 2)))
    def _():
        pl.semaphore_signal(barrier, inc=1, device_id=(me - 2, dep), device_id_type=MESH)

    @pl.when(has_above)
    def _():
        pl.semaphore_signal(barrier, inc=1, device_id=(me, dep + 1), device_id_type=MESH)

    step = cx // 4
    columns = [
        pltpu.make_async_copy(
            st.at[3 * f, pl.ds(k * step, step), :, pl.ds(row, 128)],
            col.at[f, pl.ds(k * step, step)],
            lsem.at[2],
        )
        for k in range(4)
        for f in range(2)
    ]
    small = [
        pltpu.make_async_copy(order, po, lsem.at[0]),
        pltpu.make_async_copy(fp, pb, lsem.at[1]),
    ]
    z_rows = (
        (4, cz - 2), (4, cz - 1), (5, cz - 2), (5, cz - 1), (2, cz - 1),
        (4, 0), (5, 0), (2, 0), (2, 1),
    )
    zloads = [
        pltpu.make_async_copy(st.at[f, :, r], zout.at[k], lsem.at[3])
        for k, (f, r) in enumerate(z_rows)
    ]
    loads = [
        pltpu.make_async_copy(st.at[0], sx.at[0, pl.ds(2, cx)], lsem.at[4]),
        pltpu.make_async_copy(
            st.at[pl.ds(3, 2)], sx.at[pl.ds(1, 2), pl.ds(2, cx)], lsem.at[4]
        ),
        pltpu.make_async_copy(st.at[pl.ds(1, 2)], so.at[pl.ds(0, 2)], lsem.at[4]),
        pltpu.make_async_copy(st.at[5], so.at[2], lsem.at[4]),
        pltpu.make_async_copy(mat, mb, lsem.at[5]),
        pltpu.make_async_copy(vel, vb, lsem.at[5]),
    ]
    for load in small + columns + zloads + loads:
        load.start()

    def arrived(ref, sem):
        pltpu.make_async_copy(ref, ref, sem).wait()

    def both_arrived(one, other, first_ref, other_ref, whole_ref, sem):
        @pl.when(jnp.logical_and(one, other))
        def _():
            arrived(whole_ref, sem)

        @pl.when(jnp.logical_and(one, jnp.logical_not(other)))
        def _():
            arrived(first_ref, sem)

        @pl.when(jnp.logical_and(other, jnp.logical_not(one)))
        def _():
            arrived(other_ref, sem)

    zlo, zhi = zin.at[pl.ds(0, 5)], zin.at[pl.ds(5, 4)]
    zero_row = jnp.zeros((2, cz, ny), jnp.float32)

    @pl.when(jnp.logical_not(has_left))
    def _():
        for f in range(3):
            sx[f, 0:2] = zero_row

    @pl.when(jnp.logical_not(has_right))
    def _():
        for f in range(3):
            sx[f, cx + 2 : cx + 4] = zero_row

    @pl.when(jnp.logical_not(has_below))
    def _():
        zin[0:5] = jnp.zeros((5, cx, ny), jnp.float32)

    @pl.when(jnp.logical_not(has_above))
    def _():
        zin[5:9] = jnp.zeros((4, cx, ny), jnp.float32)

    for j in range(n):
        if not near_at(j):

            @pl.when(jnp.logical_not(is_tile))
            def _():
                recv[j] = jnp.zeros(recv.shape[1:], jnp.float32)

    def x_copies(up, fields=(0, 1, 2)):
        copies = []
        for f in fields:
            plane = (0, 3, 4)[f]
            if up:
                rows = 2 if f == 0 else 1
                src, dst, to = cx - rows, 2 - rows, me + 1
            else:
                rows = 1 if f == 0 else 2
                src, dst, to = 0, cx + 2, me - 1
            copies.append(
                pltpu.make_async_remote_copy(
                    src_ref=st.at[plane, pl.ds(src, rows)],
                    dst_ref=sx.at[f, pl.ds(dst, rows)],
                    send_sem=xsend,
                    recv_sem=xrecv,
                    device_id=(to, dep),
                    device_id_type=MESH,
                )
            )
        return copies

    def z_copy(up):
        return pltpu.make_async_remote_copy(
            src_ref=zout.at[pl.ds(0, 5)] if up else zout.at[pl.ds(5, 4)],
            dst_ref=zlo if up else zhi,
            send_sem=zsend,
            recv_sem=zrecv,
            device_id=(me, dep + 1 if up else dep - 1),
            device_id_type=MESH,
        )

    def pack_copy(j):
        return pltpu.make_async_remote_copy(
            src_ref=packs.at[min(max(j - first_tile, 0), tiles - 1)],
            dst_ref=recv.at[me],
            send_sem=psend,
            recv_sem=precv,
            device_id=(j, dep),
            device_id_type=MESH,
        )

    def pack_next():
        for j in range(1, n):

            @pl.when(jnp.logical_and(j == me + 1, sends_to(j)))
            def _():
                pack_copy(j).start()

            @pl.when(jnp.logical_and(j == me + 1, halo_to(j)))
            def _():
                halo_copy(j).start()

    def halo_copy(j):
        return pltpu.make_async_remote_copy(
            src_ref=st.at[0, 0, :, pl.ds(row, 128)],
            dst_ref=halo,
            send_sem=hsend,
            recv_sem=hrecv,
            device_id=(j, dep),
            device_id_type=MESH,
        )

    ahead_of_me = jnp.int32(0)
    for j in range(n):
        ahead_of_me = ahead_of_me + jnp.logical_and(j < me, partner(j)).astype(jnp.int32)
    earlier = ahead_of_me + has_below.astype(jnp.int32) + 2 * paired.astype(jnp.int32)
    earlier = earlier - beyond.astype(jnp.int32)
    late = me > last

    fast = me % 2 == 1

    def enter():
        @pl.when(earlier > 0)
        def _():
            pl.semaphore_wait(barrier, earlier)

        @pl.when(is_end)
        def _():
            pl.semaphore_signal(
                far_in.at[1], inc=1, device_id=(head, dep), device_id_type=MESH
            )

        @pl.when(is_last)
        def _():
            for j in range(last):
                halo_copy(j).start()

        spoken_for = jnp.logical_and(me > 2, pairs(me - 2))
        for j in range(n):
            told = jnp.logical_and(j < me - 1, reached_by(j))
            if j == head:
                told = jnp.logical_and(told, jnp.logical_not(beyond))
            told = jnp.logical_and(told, jnp.logical_not(jnp.logical_and(spoken_for, j == me - 3)))

            @pl.when(told)
            def _():
                pl.semaphore_signal(
                    far_in.at[late.astype(jnp.int32)],
                    inc=1,
                    device_id=(j, dep),
                    device_id_type=MESH,
                )

        @pl.when(paired)
        def _():
            pl.semaphore_signal(next_in, inc=1, device_id=(me + 1, dep), device_id_type=MESH)

        @pl.when(jnp.logical_and(paired, me > 0))
        def _():
            pl.semaphore_signal(
                far_in.at[is_end.astype(jnp.int32)],
                inc=1,
                device_id=(me - 1, dep),
                device_id_type=MESH,
            )

        silent = jnp.logical_or(pairs(me - 1), jnp.logical_and(me >= 2, pairs(me - 2)))

        @pl.when(jnp.logical_and(has_left, jnp.logical_not(silent)))
        def _():
            pl.semaphore_signal(next_in, inc=1, device_id=(me - 1, dep), device_id_type=MESH)

        @pl.when(has_below)
        def _():
            pl.semaphore_signal(depth_in, inc=1, device_id=(me, dep - 1), device_id_type=MESH)

        @pl.when(jnp.logical_and(has_left, fast))
        def _():
            for copy in x_copies(False, (1,)):
                copy.start()

    with jax.named_scope("entry_fast"):
        pl.when(fast)(enter)

    lane = lax.broadcasted_iota(jnp.int32, (cz, wide), 1)
    lane_one = lax.broadcasted_iota(jnp.int32, (cz, 128), 1)
    my_tile = jnp.clip(me - first_tile, 0, tiles - 1)
    with jax.named_scope("params_wait"):
        for load in small:
            load.wait()
    with jax.named_scope("params"):
        blocks = [jnp.zeros((cz, wide), jnp.float32) for _ in range(tiles)]
        params = [pb[j].T for j in range(per)]
        owned = []
        for f in range(4):
            mine = jnp.full((cz, 128), 1.0, jnp.float32)
            for j in range(per):
                column = po[me * per + j]
                value = params[j][:, f : f + 1]
                mine = jnp.where(lane_one == cx + j, value, mine)
                for t in range(tiles):
                    local = column - t * cx
                    held = jnp.logical_and(local >= 0, local < cx)
                    place = jnp.where(held, f * cx + local, -1)
                    blocks[t] = jnp.where(lane == place, value, blocks[t])
            owned.append(mine)
        for f, value in enumerate(law(*owned[:3]) + (owned[3],)):
            ownp[f] = value
        for j in range(per):
            slot_lane = lane[0:1] == 4 * cx + po[me * per + j]
            picks[j : j + 1] = jnp.where(slot_lane, 1.0, 0.0)
        for t in range(tiles):
            packs[t] = blocks[t]
    with jax.named_scope("column_wait"):
        arrived(col, lsem.at[2])
    with jax.named_scope("pack"):

        @pl.when(near)
        def _():
            base = 4 * cx + (me - first_tile) * cx
            normal = jnp.zeros((cz, wide), jnp.float32)
            shear = jnp.zeros((cz, wide), jnp.float32)
            for i in range(cx):
                here = lane == base + i
                normal = jnp.where(here, col[0, i, :, 0:1], normal)
                shear = jnp.where(here, col[1, i, :, 0:1], shear)
            dxx = C_ONE * (normal - pltpu.roll(normal, 1, 1)) + C_TWO * (
                pltpu.roll(normal, wide - 1, 1) - pltpu.roll(normal, 2, 1)
            )
            share = shear + 0.5 * dxx
            inside = jnp.logical_and(lane >= 4 * cx, lane < 4 * cx + fc)
            share = jnp.where(inside, share, 0.0)
            for t in range(tiles):
                packs[t] = packs[t] + share
            recv[me] = packs[my_tile]

        @pl.when(is_last)
        def _():
            halo[...] = col[0, 0]

    with jax.named_scope("entry_slow"):
        pl.when(jnp.logical_not(fast))(enter)

    for j in range(n):

        @pl.when(jnp.logical_and(j < me, sends_to(j)))
        def _():
            pack_copy(j).start()

    @pl.when(paired)
    def _():
        pack_next()

    @pl.when(jnp.logical_and(has_left, fast))
    def _():
        for copy in x_copies(False, (0, 2)):
            copy.start()

    @pl.when(jnp.logical_and(has_left, jnp.logical_not(fast)))
    def _():
        for copy in x_copies(False):
            copy.start()

    @pl.when(paired)
    def _():
        for copy in x_copies(True):
            copy.start()

    with jax.named_scope("z_loads"):
        arrived(zout, lsem.at[3])

    @pl.when(has_below)
    def _():
        z_copy(False).start()

    def send_far(low, high, kind):
        group = [
            (j, jnp.logical_and(j > me + 1, reaches(j))) for j in range(low, high)
        ]
        count = sum(on.astype(jnp.int32) for _, on in group)

        @pl.when(count > 0)
        def _():
            pl.semaphore_wait(far_in.at[kind], count)

        for j, on in group:

            @pl.when(jnp.logical_and(on, sends_to(j)))
            def _():
                pack_copy(j).start()

            @pl.when(jnp.logical_and(on, halo_to(j)))
            def _():
                halo_copy(j).start()

    with jax.named_scope("wait_next"):

        @pl.when(jnp.logical_and(has_right, jnp.logical_not(paired)))
        def _():
            pl.semaphore_wait(next_in, 1)
            pack_next()
            for copy in x_copies(True):
                copy.start()

        @pl.when(has_above)
        def _():
            pl.semaphore_wait(depth_in, 1)
            z_copy(True).start()

    with jax.named_scope("lead_far"):
        @pl.when(lead)
        def _():
            send_far(2, last + 1, 0)
            send_far(last + 1, n, 1)

    with jax.named_scope("loads"):
        arrived(st, lsem.at[4])
        arrived(st.at[pl.ds(0, 4)], lsem.at[5])

    yi = lax.broadcasted_iota(jnp.int32, (cz, ny), 1)
    zi = lax.broadcasted_iota(jnp.int32, (cz, ny), 0)

    def y_at(field, offset):
        moved = pltpu.roll(field, (-offset) % ny, 1)
        keep = yi < ny - offset if offset > 0 else yi >= -offset
        return jnp.where(keep, moved, 0.0)

    def z_at(field):
        def at(offset):
            if offset == 0:
                return field
            moved = pltpu.roll(field, (-offset) % cz, 0)
            keep = zi < cz - offset if offset > 0 else zi >= -offset
            return jnp.where(keep, moved, 0.0)

        return at

    def minus(at):
        return C_ONE * (at(0) - at(-1)) + C_TWO * (at(1) - at(-2))

    def plus(at):
        return C_ONE * (at(1) - at(0)) + C_TWO * (at(2) - at(-1))

    def along_x(f, x):
        return lambda offset: sx[f, x + 2 + offset]

    def along_y(field):
        return lambda offset: field if offset == 0 else y_at(field, offset)

    def buoyancy(x):
        material = mb[x]
        b = jnp.full((cz, ny), 0.25 * BUOY[0], jnp.float32)
        for index in range(1, 4):
            b = jnp.where(material == index, 0.25 * BUOY[index], b)
        bb[x] = b
        return b

    def across(x):
        return minus(along_x(0, x)), plus(along_x(1, x)), plus(along_x(2, x))

    def local(x):
        sxz, szz, syz = sx[2, x + 2], so[1, x], so[2, x]
        return (
            minus(along_y(sx[1, x + 2])) + minus(z_at(sxz)),
            plus(along_y(so[0, x])) + minus(z_at(syz)),
            plus(along_y(syz)) + plus(z_at(szz)),
        )

    def inner(x, carry):
        b, along, rest = buoyancy(x), across(x), local(x)
        for c in range(3):
            out[c, x] = vb[c, x] + b * (along[c] + rest[c])
        return carry

    def outer(x):
        b, rest = buoyancy(x), local(x)
        for c in range(3):
            out[c, x] = vb[c, x] + b * rest[c]

    edges = (0, 1, cx - 2, cx - 1)
    with jax.named_scope("outer"):
        for x in edges:
            outer(x)

    middle = cx // 2
    with jax.named_scope("inner"):
        lax.fori_loop(2, middle, inner, 0)

    with jax.named_scope("wait_far"):
        pl.when(jnp.logical_not(lead))(lambda: send_far(2, last + 1, 0))
    with jax.named_scope("wait_far2"):
        pl.when(jnp.logical_not(lead))(lambda: send_far(last + 1, n, 1))

    with jax.named_scope("inner2"):
        lax.fori_loop(middle, cx - 2, inner, 0)
    def z_done(up, down, sem):
        both_arrived(up, down, zin.at[pl.ds(0, 5)], zin.at[pl.ds(0, 4)], zin, sem)

    with jax.named_scope("z_wait"):

        z_done(has_below, has_above, zrecv)

    first = lax.broadcasted_iota(jnp.int32, (8, ny), 0)

    def face(x, carry):
        def low(k):
            return zin[k, pl.ds(x, 1), :]

        def high(k):
            return zin[5 + k, pl.ds(x, 1), :]

        def put(at, one, two):
            return jnp.where(first == at, one, jnp.where(first == two[0], two[1], 0.0))

        b = bb[x, 0:8]
        out[0, x, 0:8] -= b * put(0, C_ONE * low(1) + C_TWO * low(0), (1, C_TWO * low(1)))
        out[1, x, 0:8] -= b * put(0, C_ONE * low(3) + C_TWO * low(2), (1, C_TWO * low(3)))
        out[2, x, 0:8] -= b * jnp.where(first == 0, C_TWO * low(4), 0.0)
        b = bb[x, cz - 8 : cz]
        out[0, x, cz - 8 : cz] += b * jnp.where(first == 7, C_TWO * high(0), 0.0)
        out[1, x, cz - 8 : cz] += b * jnp.where(first == 7, C_TWO * high(1), 0.0)
        out[2, x, cz - 8 : cz] += b * put(
            7, C_ONE * high(2) + C_TWO * high(3), (6, C_TWO * high(2))
        )
        return carry

    with jax.named_scope("face"):
        lax.fori_loop(0, cx, face, 0)

    def level(columns):
        for start in range(0, len(columns), 4):
            parts = []
            for i in columns[start : start + 4]:
                low = out[0, i, :, row - 128 : row]
                high = out[0, i, :, row : row + 128]
                above = 0.5 * (high + pltpu.roll(low, 1, 1))
                below = 0.5 * (pltpu.roll(high, 127, 1) + low)
                low = jnp.where(lane_one == 127, below, low)
                parts.append((i, low, jnp.where(lane_one == 0, above, high)))
            for i, low, high in parts:
                out[0, i, :, row - 128 : row] = low
                out[0, i, :, row : row + 128] = high

    with jax.named_scope("mean_inside"):

        @pl.when(is_tile)
        def _():
            level(range(2, cx - 2))

    outside = jnp.logical_or(me < head, me > last)

    def x_done(up, down, sem):
        line = sx.at[0]
        both_arrived(
            up, down, line.at[pl.ds(0, 4)], line.at[pl.ds(0, 5)], line.at[pl.ds(0, 9)], sem
        )

    def add_edges(on_fault=False):
        with jax.named_scope("x_wait"):

            x_done(has_left, has_right, xrecv)

        with jax.named_scope("edges"):
            for x in edges:
                along = across(x)
                for c in range(1, 3):
                    out[c, x] += bb[x] * along[c]
                value = out[0, x] + bb[x] * along[0]
                if not on_fault:
                    out[0, x] = value
                    continue
                low, high = value[:, row - 128 : row], value[:, row : row + 128]
                above = 0.5 * (high + pltpu.roll(low, 1, 1))
                below = 0.5 * (pltpu.roll(high, 127, 1) + low)
                s = rates[:, x : x + 1]
                low = jnp.where(lane_one == 127, below - s, low)
                high = jnp.where(lane_one == 0, above + s, high)
                out[0, x, :, row - 128 : row] = low
                out[0, x, :, row : row + 128] = high
                if row > 128:
                    out[0, x, :, : row - 128] = value[:, : row - 128]
                    out[0, x, :, row + 128 :] = value[:, row + 128 :]

    pl.when(outside)(add_edges)

    with jax.named_scope("pack_wait"):
        @pl.when(is_tile)
        def _():
            arrived(recv.at[pl.ds(0, n - 1)], precv)

        @pl.when(me == first_tile - 1)
        def _():
            arrived(recv.at[pl.ds(0, tiles)], precv)

        @pl.when(jnp.logical_not(near))
        def _():
            arrived(recv.at[pl.ds(0, tiles + 1)], precv)

        @pl.when(jnp.logical_not(is_last))
        def _():
            arrived(halo, hrecv)

    with jax.named_scope("friction"):
        total = recv[first_tile - 1]
        for j in range(n):
            if j != first_tile - 1:
                total = total + recv[j]
        edge = 0.5 * C_TWO * halo[:, 0:1]
        total = total + jnp.where(lane == 4 * cx + fc - 1, edge, 0.0)

        sums[...] = total

        @pl.when(is_tile)
        def _():
            fields = [total[:, :128]]
            for f in range(1, 4):
                fields.append(pltpu.roll(total, wide - f * cx, 1)[:, :128])
            used = lane_one < cx
            fields = [jnp.where(used, field, 1.0) for field in fields]
            tau = fields[3]
            for t in range(tiles):
                moved = pltpu.roll(total, wide - (4 + t) * cx, 1)[:, :128]
                tau = tau + jnp.where(jnp.logical_and(used, my_tile == t), moved, 0.0)
            rates[...] = 0.5 * friction(tau, *law(*fields[:3]))

    def fix(columns):
        for start in range(0, len(columns), 4):
            parts = []
            for i in columns[start : start + 4]:
                s = rates[:, i : i + 1]
                low = out[0, i, :, row - 128 : row]
                high = out[0, i, :, row : row + 128]
                low = low - jnp.where(lane_one == 127, s, 0.0)
                high = high + jnp.where(lane_one == 0, s, 0.0)
                parts.append((i, low, high))
            for i, low, high in parts:
                out[0, i, :, row - 128 : row] = low
                out[0, i, :, row : row + 128] = high

    with jax.named_scope("fix"):

        @pl.when(is_tile)
        def _():
            fix(range(2, cx - 2))

    pl.when(jnp.logical_or(lead, is_last))(add_edges)
    pl.when(is_tile)(functools.partial(add_edges, True))

    with jax.named_scope("sends_done"):
        @pl.when(near)
        def _():
            arrived(recv.at[pl.ds(0, n - 1)], psend)

        @pl.when(jnp.logical_not(near))
        def _():
            arrived(recv.at[pl.ds(0, tiles)], psend)

        @pl.when(is_last)
        def _():
            arrived(recv.at[pl.ds(0, n - 1), :, pl.ds(0, 128)], hsend)

        z_done(has_above, has_below, zsend)
        x_done(has_right, has_left, xsend)


def write_out(first, held, sums, params, picks, out, slip_out, slip, sem):
    velocity = pltpu.make_async_copy(held, out, sem.at[0])
    velocity.start()
    lane = lax.broadcasted_iota(jnp.int32, params.shape[1:], 1)
    total, tau = sums[...], params[3]
    for j in range(slip.shape[0]):
        picked = jnp.sum(total * picks[j : j + 1], axis=1, keepdims=True)
        tau = tau + jnp.where(lane == first + j, picked, 0.0)
    rate = friction(tau, params[0], params[1], params[2])
    slip[...] = rate.T[first : first + slip.shape[0]]
    rates = pltpu.make_async_copy(slip, slip_out, sem.at[1])
    rates.start()
    velocity.wait()
    rates.wait()


def per_device(n, nd, velocity, stress, material, patch_order, fault_params):
    _, cx, cz, ny = stress.shape
    fc = patch_order.shape[0]
    per = fc // n
    wide = -(-(4 * cx + fc + 2) // 128) * 128
    dims = (n, nd, cx, cz, ny, fc, wide)
    tiles = fc // cx
    f32 = jnp.float32
    anywhere = pl.BlockSpec(memory_space=pltpu.HBM)
    dma = pltpu.SemaphoreType.DMA
    params = jnp.transpose(fault_params, (2, 0, 1))
    big = (velocity, stress, material, patch_order, params)
    held = pl.pallas_call(
        functools.partial(kernel, dims),
        out_shape=(
            jax.ShapeDtypeStruct(velocity.shape, f32),
            jax.ShapeDtypeStruct((cz, wide), f32),
            jax.ShapeDtypeStruct((4, cz, 128), f32),
            jax.ShapeDtypeStruct((-(-per // 8) * 8, wide), f32),
        ),
        in_specs=[anywhere] * 5,
        out_specs=(pl.BlockSpec(memory_space=pltpu.VMEM),) * 4,
        scratch_shapes=[
            pltpu.SMEM((fc,), jnp.int32),
            pltpu.VMEM((2, cx, cz, 128), f32),
            pltpu.VMEM((3, cx + 4, cz, ny), f32),
            pltpu.VMEM((3, cx, cz, ny), f32),
            pltpu.VMEM((3, cx, cz, ny), f32),
            pltpu.VMEM((cx, cz, ny), jnp.int32),
            pltpu.VMEM((cx, cz, ny), f32),
            pltpu.VMEM((per, 4, cz), f32),
            pltpu.VMEM((9, cx, ny), f32),
            pltpu.VMEM((9, cx, ny), f32),
            pltpu.VMEM((tiles, cz, wide), f32),
            pltpu.VMEM((n, cz, wide), f32),
            pltpu.VMEM((cz, 128), f32),
            pltpu.VMEM((cz, 128), f32),
            dma((6,)),
            dma,
            dma,
            dma,
            dma,
            dma,
            dma,
            dma,
            dma,
            pltpu.SemaphoreType.REGULAR,
            pltpu.SemaphoreType.REGULAR((2,)),
            pltpu.SemaphoreType.REGULAR,
        ],
        compiler_params=pltpu.CompilerParams(collective_id=0, has_side_effects=True, vmem_limit_bytes=12 << 20),
    )(*[pltpu.with_memory_space_constraint(v, pltpu.HBM) for v in big])
    resident = pl.BlockSpec(memory_space=pltpu.VMEM)
    moved, slip = pl.pallas_call(
        functools.partial(write_out, cx),
        out_shape=(
            jax.ShapeDtypeStruct(velocity.shape, f32),
            jax.ShapeDtypeStruct((per, cz), f32),
        ),
        in_specs=[resident] * 4,
        out_specs=(anywhere, anywhere),
        scratch_shapes=[pltpu.VMEM((per, cz), f32), dma((2,))],
        compiler_params=pltpu.CompilerParams(vmem_limit_bytes=4 << 20),
    )(*held)
    return moved, slip.T


def solution(mesh):
    n, nd = mesh.shape["strike"], mesh.shape["depth"]
    return jax.shard_map(
        functools.partial(per_device, n, nd),
        mesh=mesh,
        in_specs=(
            P(None, "strike", "depth", None),
            P(None, "strike", "depth", None),
            P("strike", "depth", None),
            P(),
            P(None, "depth", "strike"),
        ),
        out_specs=(P(None, "strike", "depth", None), P("depth", "strike")),
        check_vma=False,
    )
```

```python
import functools

import jax
import jax.numpy as jnp
from jax import lax
from jax.experimental import pallas as pl
from jax.experimental.pallas import tpu as pltpu
from jax.sharding import PartitionSpec as P

NEWTON = 8
BUOY = (1.0, 0.8, 0.6, 1.25)
C_ONE = 9.0 / 8.0
C_TWO = -1.0 / 24.0
MESH = pl.DeviceIdType.MESH


def law(coef, psi, normal_stress):
    half_q = 0.5 * jnp.exp(psi / coef)
    scale = normal_stress * coef
    return half_q, scale, scale * half_q


def friction(tau_total, half_q, scale, stiff):
    rate = 0.35 * tau_total / (1.0 + stiff)
    for _ in range(NEWTON - 1):
        arg_val = rate * half_q
        square = 1.0 + arg_val * arg_val
        inverse = lax.rsqrt(square)
        gain = 0.35 / (1.0 + stiff * inverse)
        magnitude = scale * jnp.log(jnp.abs(arg_val) + square * inverse)
        resid = tau_total - rate - jnp.where(arg_val < 0, -magnitude, magnitude)
        rate = rate + resid * gain
    return rate


def kernel(
    dims, vel, st, mat, order, fp, out, sums, ownp, picks,
    po, col, sx, so, vb, mb, bb, pb, zout, zin, packs, recv, halo, rates,
    lsem, psend, precv, hsend, hrecv, xsend, xrecv, zsend, zrecv, next_in, far_in, depth_in,
):
    n, nd, cx, cz, ny, fc, wide = dims
    row = ny // 2
    per = fc // n
    first_tile = n // 4
    tiles = fc // cx
    me = lax.axis_index("strike")
    dep = lax.axis_index("depth")
    has_left, has_right = me > 0, me < n - 1
    has_below, has_above = dep > 0, dep < nd - 1
    is_tile = jnp.logical_and(me >= first_tile, me < first_tile + tiles)
    near = jnp.logical_and(me >= first_tile - 1, me < first_tile + tiles)

    def tile_at(j):
        return first_tile <= j < first_tile + tiles

    def near_at(j):
        return first_tile - 1 <= j < first_tile + tiles

    last = first_tile + tiles
    is_last = me == last

    def pairs(j):
        inside = jnp.logical_and(j >= first_tile, j < last)
        return jnp.logical_or(j == 0, jnp.logical_and(j % 2 == first_tile % 2, inside))

    paired = pairs(me)
    head = first_tile - 1
    lead = me == head
    beyond = me == last + 1
    is_end = me == last - 1

    def sends_to(j):
        return jnp.logical_and(me != j, jnp.logical_or(near, tile_at(j)))

    def halo_to(j):
        return jnp.logical_and(is_last, me != j)

    def reaches(j):
        return jnp.logical_or(sends_to(j), halo_to(j))

    def reached_by(j):
        return jnp.logical_and(me != j, jnp.logical_or(is_tile, near_at(j) or j == last))

    def partner(j):
        beside = jnp.logical_or(me == j - 1, me == j + 1)
        return jnp.logical_or(beside, jnp.logical_or(reaches(j), reached_by(j)))

    barrier = pltpu.get_barrier_semaphore()
    for j in range(n):

        back = jnp.logical_and(j == me - 1, pairs(j))

        ahead = jnp.logical_and(j > me, partner(j))
        if j == last + 1:
            ahead = jnp.logical_and(ahead, jnp.logical_not(lead))

        @pl.when(jnp.logical_or(ahead, back))
        def _():
            pl.semaphore_signal(barrier, inc=1, device_id=(j, dep), device_id_type=MESH)

    @pl.when(jnp.logical_and(me >= 2, pairs(me - 2)))
    def _():
        pl.semaphore_signal(barrier, inc=1, device_id=(me - 2, dep), device_id_type=MESH)

    @pl.when(has_above)
    def _():
        pl.semaphore_signal(barrier, inc=1, device_id=(me, dep + 1), device_id_type=MESH)

    step = cx // 4
    columns = [
        pltpu.make_async_copy(
            st.at[3 * f, pl.ds(k * step, step), :, pl.ds(row, 128)],
            col.at[f, pl.ds(k * step, step)],
            lsem.at[2],
        )
        for k in range(4)
        for f in range(2)
    ]
    small = [
        pltpu.make_async_copy(order, po, lsem.at[0]),
        pltpu.make_async_copy(fp, pb, lsem.at[1]),
    ]
    z_rows = (
        (4, cz - 2), (4, cz - 1), (5, cz - 2), (5, cz - 1), (2, cz - 1),
        (4, 0), (5, 0), (2, 0), (2, 1),
    )
    zloads = [
        pltpu.make_async_copy(st.at[f, :, r], zout.at[k], lsem.at[3])
        for k, (f, r) in enumerate(z_rows)
    ]
    loads = [
        pltpu.make_async_copy(st.at[0], sx.at[0, pl.ds(2, cx)], lsem.at[4]),
        pltpu.make_async_copy(
            st.at[pl.ds(3, 2)], sx.at[pl.ds(1, 2), pl.ds(2, cx)], lsem.at[4]
        ),
        pltpu.make_async_copy(st.at[pl.ds(1, 2)], so.at[pl.ds(0, 2)], lsem.at[4]),
        pltpu.make_async_copy(st.at[5], so.at[2], lsem.at[4]),
        pltpu.make_async_copy(mat, mb, lsem.at[5]),
        pltpu.make_async_copy(vel, vb, lsem.at[5]),
    ]
    for load in small + columns + zloads + loads:
        load.start()

    def arrived(ref, sem):
        pltpu.make_async_copy(ref, ref, sem).wait()

    def both_arrived(one, other, first_ref, other_ref, whole_ref, sem):
        @pl.when(jnp.logical_and(one, other))
        def _():
            arrived(whole_ref, sem)

        @pl.when(jnp.logical_and(one, jnp.logical_not(other)))
        def _():
            arrived(first_ref, sem)

        @pl.when(jnp.logical_and(other, jnp.logical_not(one)))
        def _():
            arrived(other_ref, sem)

    zlo, zhi = zin.at[pl.ds(0, 5)], zin.at[pl.ds(5, 4)]
    zero_row = jnp.zeros((2, cz, ny), jnp.float32)

    @pl.when(jnp.logical_not(has_left))
    def _():
        for f in range(3):
            sx[f, 0:2] = zero_row

    @pl.when(jnp.logical_not(has_right))
    def _():
        for f in range(3):
            sx[f, cx + 2 : cx + 4] = zero_row

    @pl.when(jnp.logical_not(has_below))
    def _():
        zin[0:5] = jnp.zeros((5, cx, ny), jnp.float32)

    @pl.when(jnp.logical_not(has_above))
    def _():
        zin[5:9] = jnp.zeros((4, cx, ny), jnp.float32)

    for j in range(n):
        if not near_at(j):

            @pl.when(jnp.logical_not(is_tile))
            def _():
                recv[j] = jnp.zeros(recv.shape[1:], jnp.float32)

    def x_copies(up, fields=(0, 1, 2)):
        copies = []
        for f in fields:
            plane = (0, 3, 4)[f]
            if up:
                rows = 2 if f == 0 else 1
                src, dst, to = cx - rows, 2 - rows, me + 1
            else:
                rows = 1 if f == 0 else 2
                src, dst, to = 0, cx + 2, me - 1
            copies.append(
                pltpu.make_async_remote_copy(
                    src_ref=st.at[plane, pl.ds(src, rows)],
                    dst_ref=sx.at[f, pl.ds(dst, rows)],
                    send_sem=xsend,
                    recv_sem=xrecv.at[0 if up else 1],
                    device_id=(to, dep),
                    device_id_type=MESH,
                )
            )
        return copies

    def z_copy(up):
        return pltpu.make_async_remote_copy(
            src_ref=zout.at[pl.ds(0, 5)] if up else zout.at[pl.ds(5, 4)],
            dst_ref=zlo if up else zhi,
            send_sem=zsend,
            recv_sem=zrecv,
            device_id=(me, dep + 1 if up else dep - 1),
            device_id_type=MESH,
        )

    def pack_copy(j):
        return pltpu.make_async_remote_copy(
            src_ref=packs.at[min(max(j - first_tile, 0), tiles - 1)],
            dst_ref=recv.at[me],
            send_sem=psend,
            recv_sem=precv,
            device_id=(j, dep),
            device_id_type=MESH,
        )

    def pack_next():
        for j in range(1, n):

            @pl.when(jnp.logical_and(j == me + 1, sends_to(j)))
            def _():
                pack_copy(j).start()

            @pl.when(jnp.logical_and(j == me + 1, halo_to(j)))
            def _():
                halo_copy(j).start()

    def halo_copy(j):
        return pltpu.make_async_remote_copy(
            src_ref=st.at[0, 0, :, pl.ds(row, 128)],
            dst_ref=halo,
            send_sem=hsend,
            recv_sem=hrecv,
            device_id=(j, dep),
            device_id_type=MESH,
        )

    ahead_of_me = jnp.int32(0)
    for j in range(n):
        ahead_of_me = ahead_of_me + jnp.logical_and(j < me, partner(j)).astype(jnp.int32)
    earlier = ahead_of_me + has_below.astype(jnp.int32) + 2 * paired.astype(jnp.int32)
    earlier = earlier - beyond.astype(jnp.int32)
    late = me > last

    fast = me % 2 == 1

    def enter():
        @pl.when(earlier > 0)
        def _():
            pl.semaphore_wait(barrier, earlier)

        @pl.when(is_end)
        def _():
            pl.semaphore_signal(
                far_in.at[1], inc=1, device_id=(head, dep), device_id_type=MESH
            )

        @pl.when(is_last)
        def _():
            for j in range(last):
                halo_copy(j).start()

        spoken_for = jnp.logical_and(me > 2, pairs(me - 2))
        for j in range(n):
            told = jnp.logical_and(j < me - 1, reached_by(j))
            if j == head:
                told = jnp.logical_and(told, jnp.logical_not(beyond))
            told = jnp.logical_and(told, jnp.logical_not(jnp.logical_and(spoken_for, j == me - 3)))

            @pl.when(told)
            def _():
                pl.semaphore_signal(
                    far_in.at[late.astype(jnp.int32)],
                    inc=1,
                    device_id=(j, dep),
                    device_id_type=MESH,
                )

        @pl.when(paired)
        def _():
            pl.semaphore_signal(next_in, inc=1, device_id=(me + 1, dep), device_id_type=MESH)

        @pl.when(jnp.logical_and(paired, me > 0))
        def _():
            pl.semaphore_signal(
                far_in.at[is_end.astype(jnp.int32)],
                inc=1,
                device_id=(me - 1, dep),
                device_id_type=MESH,
            )

        silent = jnp.logical_or(pairs(me - 1), jnp.logical_and(me >= 2, pairs(me - 2)))

        @pl.when(jnp.logical_and(has_left, jnp.logical_not(silent)))
        def _():
            pl.semaphore_signal(next_in, inc=1, device_id=(me - 1, dep), device_id_type=MESH)

        @pl.when(has_below)
        def _():
            pl.semaphore_signal(depth_in, inc=1, device_id=(me, dep - 1), device_id_type=MESH)

        @pl.when(jnp.logical_and(has_left, fast))
        def _():
            for copy in x_copies(False, (1,)):
                copy.start()

    with jax.named_scope("entry_fast"):
        pl.when(fast)(enter)

    lane = lax.broadcasted_iota(jnp.int32, (cz, wide), 1)
    lane_one = lax.broadcasted_iota(jnp.int32, (cz, 128), 1)
    my_tile = jnp.clip(me - first_tile, 0, tiles - 1)
    with jax.named_scope("params_wait"):
        for load in small:
            load.wait()
    with jax.named_scope("params"):
        blocks = [jnp.zeros((cz, wide), jnp.float32) for _ in range(tiles)]
        params = [pb[j].T for j in range(per)]
        owned = []
        for f in range(4):
            mine = jnp.full((cz, 128), 1.0, jnp.float32)
            for j in range(per):
                column = po[me * per + j]
                value = params[j][:, f : f + 1]
                mine = jnp.where(lane_one == cx + j, value, mine)
                for t in range(tiles):
                    local = column - t * cx
                    held = jnp.logical_and(local >= 0, local < cx)
                    place = jnp.where(held, f * cx + local, -1)
                    blocks[t] = jnp.where(lane == place, value, blocks[t])
            owned.append(mine)
        for f, value in enumerate(law(*owned[:3]) + (owned[3],)):
            ownp[f] = value
        for j in range(per):
            slot_lane = lane[0:1] == 4 * cx + po[me * per + j]
            picks[j : j + 1] = jnp.where(slot_lane, 1.0, 0.0)
        for t in range(tiles):
            packs[t] = blocks[t]
    with jax.named_scope("column_wait"):
        arrived(col, lsem.at[2])
    with jax.named_scope("pack"):

        @pl.when(near)
        def _():
            base = 4 * cx + (me - first_tile) * cx
            normal = jnp.zeros((cz, wide), jnp.float32)
            shear = jnp.zeros((cz, wide), jnp.float32)
            for i in range(cx):
                here = lane == base + i
                normal = jnp.where(here, col[0, i, :, 0:1], normal)
                shear = jnp.where(here, col[1, i, :, 0:1], shear)
            dxx = C_ONE * (normal - pltpu.roll(normal, 1, 1)) + C_TWO * (
                pltpu.roll(normal, wide - 1, 1) - pltpu.roll(normal, 2, 1)
            )
            share = shear + 0.5 * dxx
            inside = jnp.logical_and(lane >= 4 * cx, lane < 4 * cx + fc)
            share = jnp.where(inside, share, 0.0)
            for t in range(tiles):
                packs[t] = packs[t] + share
            recv[me] = packs[my_tile]

        @pl.when(is_last)
        def _():
            halo[...] = col[0, 0]

    with jax.named_scope("entry_slow"):
        pl.when(jnp.logical_not(fast))(enter)

    for j in range(n):

        @pl.when(jnp.logical_and(j < me, sends_to(j)))
        def _():
            pack_copy(j).start()

    @pl.when(paired)
    def _():
        pack_next()

    @pl.when(jnp.logical_and(has_left, fast))
    def _():
        for copy in x_copies(False, (0, 2)):
            copy.start()

    @pl.when(jnp.logical_and(has_left, jnp.logical_not(fast)))
    def _():
        for copy in x_copies(False):
            copy.start()

    @pl.when(paired)
    def _():
        for copy in x_copies(True):
            copy.start()

    with jax.named_scope("z_loads"):
        arrived(zout, lsem.at[3])

    @pl.when(has_below)
    def _():
        z_copy(False).start()

    def send_far(low, high, kind):
        group = [
            (j, jnp.logical_and(j > me + 1, reaches(j))) for j in range(low, high)
        ]
        count = sum(on.astype(jnp.int32) for _, on in group)

        @pl.when(count > 0)
        def _():
            pl.semaphore_wait(far_in.at[kind], count)

        for j, on in group:

            @pl.when(jnp.logical_and(on, sends_to(j)))
            def _():
                pack_copy(j).start()

            @pl.when(jnp.logical_and(on, halo_to(j)))
            def _():
                halo_copy(j).start()

    with jax.named_scope("wait_next"):

        @pl.when(jnp.logical_and(has_right, jnp.logical_not(paired)))
        def _():
            pl.semaphore_wait(next_in, 1)
            pack_next()
            for copy in x_copies(True):
                copy.start()

        @pl.when(has_above)
        def _():
            pl.semaphore_wait(depth_in, 1)
            z_copy(True).start()

    with jax.named_scope("lead_far"):
        @pl.when(lead)
        def _():
            send_far(2, last + 1, 0)
            send_far(last + 1, n, 1)

    with jax.named_scope("loads"):
        arrived(st, lsem.at[4])
        arrived(st.at[pl.ds(0, 4)], lsem.at[5])

    yi = lax.broadcasted_iota(jnp.int32, (cz, ny), 1)
    zi = lax.broadcasted_iota(jnp.int32, (cz, ny), 0)

    def y_at(field, offset):
        moved = pltpu.roll(field, (-offset) % ny, 1)
        keep = yi < ny - offset if offset > 0 else yi >= -offset
        return jnp.where(keep, moved, 0.0)

    def z_at(field):
        def at(offset):
            if offset == 0:
                return field
            moved = pltpu.roll(field, (-offset) % cz, 0)
            keep = zi < cz - offset if offset > 0 else zi >= -offset
            return jnp.where(keep, moved, 0.0)

        return at

    def minus(at):
        return C_ONE * (at(0) - at(-1)) + C_TWO * (at(1) - at(-2))

    def plus(at):
        return C_ONE * (at(1) - at(0)) + C_TWO * (at(2) - at(-1))

    def along_x(f, x):
        return lambda offset: sx[f, x + 2 + offset]

    def along_y(field):
        return lambda offset: field if offset == 0 else y_at(field, offset)

    def buoyancy(x):
        material = mb[x]
        b = jnp.full((cz, ny), 0.25 * BUOY[0], jnp.float32)
        for index in range(1, 4):
            b = jnp.where(material == index, 0.25 * BUOY[index], b)
        bb[x] = b
        return b

    def across(x):
        return minus(along_x(0, x)), plus(along_x(1, x)), plus(along_x(2, x))

    def local(x):
        sxz, szz, syz = sx[2, x + 2], so[1, x], so[2, x]
        return (
            minus(along_y(sx[1, x + 2])) + minus(z_at(sxz)),
            plus(along_y(so[0, x])) + minus(z_at(syz)),
            plus(along_y(syz)) + plus(z_at(szz)),
        )

    def inner(x, carry):
        b, along, rest = buoyancy(x), across(x), local(x)
        for c in range(3):
            out[c, x] = vb[c, x] + b * (along[c] + rest[c])
        return carry

    def outer(x):
        b, rest = buoyancy(x), local(x)
        for c in range(3):
            out[c, x] = vb[c, x] + b * rest[c]

    edges = (0, 1, cx - 2, cx - 1)
    with jax.named_scope("outer"):
        for x in edges:
            outer(x)

    middle = cx // 2
    with jax.named_scope("inner"):
        lax.fori_loop(2, middle, inner, 0)

    with jax.named_scope("wait_far"):
        pl.when(jnp.logical_not(lead))(lambda: send_far(2, last + 1, 0))
    with jax.named_scope("wait_far2"):
        pl.when(jnp.logical_not(lead))(lambda: send_far(last + 1, n, 1))

    with jax.named_scope("inner2"):
        lax.fori_loop(middle, cx - 2, inner, 0)
    def z_done(up, down, sem):
        both_arrived(up, down, zin.at[pl.ds(0, 5)], zin.at[pl.ds(0, 4)], zin, sem)

    with jax.named_scope("z_wait"):

        z_done(has_below, has_above, zrecv)

    first = lax.broadcasted_iota(jnp.int32, (8, ny), 0)

    def face(x, carry):
        def low(k):
            return zin[k, pl.ds(x, 1), :]

        def high(k):
            return zin[5 + k, pl.ds(x, 1), :]

        def put(at, one, two):
            return jnp.where(first == at, one, jnp.where(first == two[0], two[1], 0.0))

        b = bb[x, 0:8]
        out[0, x, 0:8] -= b * put(0, C_ONE * low(1) + C_TWO * low(0), (1, C_TWO * low(1)))
        out[1, x, 0:8] -= b * put(0, C_ONE * low(3) + C_TWO * low(2), (1, C_TWO * low(3)))
        out[2, x, 0:8] -= b * jnp.where(first == 0, C_TWO * low(4), 0.0)
        b = bb[x, cz - 8 : cz]
        out[0, x, cz - 8 : cz] += b * jnp.where(first == 7, C_TWO * high(0), 0.0)
        out[1, x, cz - 8 : cz] += b * jnp.where(first == 7, C_TWO * high(1), 0.0)
        out[2, x, cz - 8 : cz] += b * put(
            7, C_ONE * high(2) + C_TWO * high(3), (6, C_TWO * high(2))
        )
        return carry

    with jax.named_scope("face"):
        lax.fori_loop(0, cx, face, 0)

    def level(columns):
        for start in range(0, len(columns), 4):
            parts = []
            for i in columns[start : start + 4]:
                low = out[0, i, :, row - 128 : row]
                high = out[0, i, :, row : row + 128]
                above = 0.5 * (high + pltpu.roll(low, 1, 1))
                below = 0.5 * (pltpu.roll(high, 127, 1) + low)
                low = jnp.where(lane_one == 127, below, low)
                parts.append((i, low, jnp.where(lane_one == 0, above, high)))
            for i, low, high in parts:
                out[0, i, :, row - 128 : row] = low
                out[0, i, :, row : row + 128] = high

    with jax.named_scope("mean_inside"):

        @pl.when(is_tile)
        def _():
            level(range(2, cx - 2))

    outside = jnp.logical_or(me < head, me > last)

    def x_done(up, down, sem):
        line = sx.at[0]
        both_arrived(
            up, down, line.at[pl.ds(0, 4)], line.at[pl.ds(0, 5)], line.at[pl.ds(0, 9)], sem
        )

    def add_edges(on_fault=False):
        for side, planes in enumerate((edges[:2], edges[2:])):
            with jax.named_scope(f"x_wait{side}"):

                @pl.when((has_left, has_right)[side])
                def _():
                    arrived(sx.at[0, pl.ds(0, 4 + side)], xrecv.at[side])

            with jax.named_scope("edges"):
                for x in planes:
                    along = across(x)
                    for c in range(1, 3):
                        out[c, x] += bb[x] * along[c]
                    value = out[0, x] + bb[x] * along[0]
                    if not on_fault:
                        out[0, x] = value
                        continue
                    low, high = value[:, row - 128 : row], value[:, row : row + 128]
                    above = 0.5 * (high + pltpu.roll(low, 1, 1))
                    below = 0.5 * (pltpu.roll(high, 127, 1) + low)
                    s = rates[:, x : x + 1]
                    low = jnp.where(lane_one == 127, below - s, low)
                    high = jnp.where(lane_one == 0, above + s, high)
                    out[0, x, :, row - 128 : row] = low
                    out[0, x, :, row : row + 128] = high
                    if row > 128:
                        out[0, x, :, : row - 128] = value[:, : row - 128]
                        out[0, x, :, row + 128 :] = value[:, row + 128 :]

    pl.when(outside)(add_edges)

    with jax.named_scope("pack_wait"):
        @pl.when(is_tile)
        def _():
            arrived(recv.at[pl.ds(0, n - 1)], precv)

        @pl.when(me == first_tile - 1)
        def _():
            arrived(recv.at[pl.ds(0, tiles)], precv)

        @pl.when(jnp.logical_not(near))
        def _():
            arrived(recv.at[pl.ds(0, tiles + 1)], precv)

        @pl.when(jnp.logical_not(is_last))
        def _():
            arrived(halo, hrecv)

    with jax.named_scope("friction"):
        total = recv[first_tile - 1]
        for j in range(n):
            if j != first_tile - 1:
                total = total + recv[j]
        edge = 0.5 * C_TWO * halo[:, 0:1]
        total = total + jnp.where(lane == 4 * cx + fc - 1, edge, 0.0)

        sums[...] = total

        @pl.when(is_tile)
        def _():
            fields = [total[:, :128]]
            for f in range(1, 4):
                fields.append(pltpu.roll(total, wide - f * cx, 1)[:, :128])
            used = lane_one < cx
            fields = [jnp.where(used, field, 1.0) for field in fields]
            tau = fields[3]
            for t in range(tiles):
                moved = pltpu.roll(total, wide - (4 + t) * cx, 1)[:, :128]
                tau = tau + jnp.where(jnp.logical_and(used, my_tile == t), moved, 0.0)
            rates[...] = 0.5 * friction(tau, *law(*fields[:3]))

    def fix(columns):
        for start in range(0, len(columns), 4):
            parts = []
            for i in columns[start : start + 4]:
                s = rates[:, i : i + 1]
                low = out[0, i, :, row - 128 : row]
                high = out[0, i, :, row : row + 128]
                low = low - jnp.where(lane_one == 127, s, 0.0)
                high = high + jnp.where(lane_one == 0, s, 0.0)
                parts.append((i, low, high))
            for i, low, high in parts:
                out[0, i, :, row - 128 : row] = low
                out[0, i, :, row : row + 128] = high

    with jax.named_scope("fix"):

        @pl.when(is_tile)
        def _():
            fix(range(2, cx - 2))

    pl.when(jnp.logical_or(lead, is_last))(add_edges)
    pl.when(is_tile)(functools.partial(add_edges, True))

    with jax.named_scope("sends_done"):
        @pl.when(near)
        def _():
            arrived(recv.at[pl.ds(0, n - 1)], psend)

        @pl.when(jnp.logical_not(near))
        def _():
            arrived(recv.at[pl.ds(0, tiles)], psend)

        @pl.when(is_last)
        def _():
            arrived(recv.at[pl.ds(0, n - 1), :, pl.ds(0, 128)], hsend)

        z_done(has_above, has_below, zsend)
        x_done(has_right, has_left, xsend)


def write_out(first, held, sums, params, picks, out, slip_out, slip, sem):
    velocity = pltpu.make_async_copy(held, out, sem.at[0])
    velocity.start()
    lane = lax.broadcasted_iota(jnp.int32, params.shape[1:], 1)
    total, tau = sums[...], params[3]
    for j in range(slip.shape[0]):
        picked = jnp.sum(total * picks[j : j + 1], axis=1, keepdims=True)
        tau = tau + jnp.where(lane == first + j, picked, 0.0)
    rate = friction(tau, params[0], params[1], params[2])
    slip[...] = rate.T[first : first + slip.shape[0]]
    rates = pltpu.make_async_copy(slip, slip_out, sem.at[1])
    rates.start()
    velocity.wait()
    rates.wait()


def per_device(n, nd, velocity, stress, material, patch_order, fault_params):
    _, cx, cz, ny = stress.shape
    fc = patch_order.shape[0]
    per = fc // n
    wide = -(-(4 * cx + fc + 2) // 128) * 128
    dims = (n, nd, cx, cz, ny, fc, wide)
    tiles = fc // cx
    f32 = jnp.float32
    anywhere = pl.BlockSpec(memory_space=pltpu.HBM)
    dma = pltpu.SemaphoreType.DMA
    params = jnp.transpose(fault_params, (2, 0, 1))
    big = (velocity, stress, material, patch_order, params)
    held = pl.pallas_call(
        functools.partial(kernel, dims),
        out_shape=(
            jax.ShapeDtypeStruct(velocity.shape, f32),
            jax.ShapeDtypeStruct((cz, wide), f32),
            jax.ShapeDtypeStruct((4, cz, 128), f32),
            jax.ShapeDtypeStruct((-(-per // 8) * 8, wide), f32),
        ),
        in_specs=[anywhere] * 5,
        out_specs=(pl.BlockSpec(memory_space=pltpu.VMEM),) * 4,
        scratch_shapes=[
            pltpu.SMEM((fc,), jnp.int32),
            pltpu.VMEM((2, cx, cz, 128), f32),
            pltpu.VMEM((3, cx + 4, cz, ny), f32),
            pltpu.VMEM((3, cx, cz, ny), f32),
            pltpu.VMEM((3, cx, cz, ny), f32),
            pltpu.VMEM((cx, cz, ny), jnp.int32),
            pltpu.VMEM((cx, cz, ny), f32),
            pltpu.VMEM((per, 4, cz), f32),
            pltpu.VMEM((9, cx, ny), f32),
            pltpu.VMEM((9, cx, ny), f32),
            pltpu.VMEM((tiles, cz, wide), f32),
            pltpu.VMEM((n, cz, wide), f32),
            pltpu.VMEM((cz, 128), f32),
            pltpu.VMEM((cz, 128), f32),
            dma((6,)),
            dma,
            dma,
            dma,
            dma,
            dma,
            dma((2,)),
            dma,
            dma,
            pltpu.SemaphoreType.REGULAR,
            pltpu.SemaphoreType.REGULAR((2,)),
            pltpu.SemaphoreType.REGULAR,
        ],
        compiler_params=pltpu.CompilerParams(collective_id=0, has_side_effects=True, vmem_limit_bytes=12 << 20),
    )(*[pltpu.with_memory_space_constraint(v, pltpu.HBM) for v in big])
    resident = pl.BlockSpec(memory_space=pltpu.VMEM)
    moved, slip = pl.pallas_call(
        functools.partial(write_out, cx),
        out_shape=(
            jax.ShapeDtypeStruct(velocity.shape, f32),
            jax.ShapeDtypeStruct((per, cz), f32),
        ),
        in_specs=[resident] * 4,
        out_specs=(anywhere, anywhere),
        scratch_shapes=[pltpu.VMEM((per, cz), f32), dma((2,))],
        compiler_params=pltpu.CompilerParams(vmem_limit_bytes=4 << 20),
    )(*held)
    return moved, slip.T


def solution(mesh):
    n, nd = mesh.shape["strike"], mesh.shape["depth"]
    return jax.shard_map(
        functools.partial(per_device, n, nd),
        mesh=mesh,
        in_specs=(
            P(None, "strike", "depth", None),
            P(None, "strike", "depth", None),
            P("strike", "depth", None),
            P(),
            P(None, "depth", "strike"),
        ),
        out_specs=(P(None, "strike", "depth", None), P("depth", "strike")),
        check_vma=False,
    )
```

```python
import functools

import jax
import jax.numpy as jnp
from jax import lax
from jax.experimental import pallas as pl
from jax.experimental.pallas import tpu as pltpu
from jax.sharding import PartitionSpec as P

NEWTON = 8
BUOY = (1.0, 0.8, 0.6, 1.25)
C_ONE = 9.0 / 8.0
C_TWO = -1.0 / 24.0
MESH = pl.DeviceIdType.MESH


def law(coef, psi, normal_stress):
    half_q = 0.5 * jnp.exp(psi / coef)
    scale = normal_stress * coef
    return half_q, scale, scale * half_q


def friction(tau_total, half_q, scale, stiff):
    rate = 0.35 * tau_total / (1.0 + stiff)
    for _ in range(NEWTON - 1):
        arg_val = rate * half_q
        square = 1.0 + arg_val * arg_val
        inverse = lax.rsqrt(square)
        gain = 0.35 / (1.0 + stiff * inverse)
        magnitude = scale * jnp.log(jnp.abs(arg_val) + square * inverse)
        resid = tau_total - rate - jnp.where(arg_val < 0, -magnitude, magnitude)
        rate = rate + resid * gain
    return rate


def kernel(
    dims, vel, st, mat, order, fp, out, sums, ownp, picks,
    po, col, sx, so, vb, mb, bb, pb, zout, zin, packs, recv, halo, rates,
    lsem, psend, precv, hsend, hrecv, xsend, xrecv, zsend, zrecv, next_in, far_in, depth_in,
):
    n, nd, cx, cz, ny, fc, wide = dims
    row = ny // 2
    per = fc // n
    first_tile = n // 4
    tiles = fc // cx
    me = lax.axis_index("strike")
    dep = lax.axis_index("depth")
    has_left, has_right = me > 0, me < n - 1
    has_below, has_above = dep > 0, dep < nd - 1
    is_tile = jnp.logical_and(me >= first_tile, me < first_tile + tiles)
    near = jnp.logical_and(me >= first_tile - 1, me < first_tile + tiles)

    def tile_at(j):
        return first_tile <= j < first_tile + tiles

    def near_at(j):
        return first_tile - 1 <= j < first_tile + tiles

    last = first_tile + tiles
    is_last = me == last

    def pairs(j):
        inside = jnp.logical_and(j >= first_tile, j < last)
        return jnp.logical_or(j == 0, jnp.logical_and(j % 2 == first_tile % 2, inside))

    paired = pairs(me)
    head = first_tile - 1
    lead = me == head
    beyond = me == last + 1
    is_end = me == last - 1

    def sends_to(j):
        return jnp.logical_and(me != j, jnp.logical_or(near, tile_at(j)))

    def halo_to(j):
        return jnp.logical_and(is_last, me != j)

    def reaches(j):
        return jnp.logical_or(sends_to(j), halo_to(j))

    def reached_by(j):
        return jnp.logical_and(me != j, jnp.logical_or(is_tile, near_at(j) or j == last))

    def partner(j):
        beside = jnp.logical_or(me == j - 1, me == j + 1)
        return jnp.logical_or(beside, jnp.logical_or(reaches(j), reached_by(j)))

    barrier = pltpu.get_barrier_semaphore()
    for j in range(n):

        back = jnp.logical_and(j == me - 1, pairs(j))

        ahead = jnp.logical_and(j > me, partner(j))
        if j == last + 1:
            ahead = jnp.logical_and(ahead, jnp.logical_not(lead))

        @pl.when(jnp.logical_or(ahead, back))
        def _():
            pl.semaphore_signal(barrier, inc=1, device_id=(j, dep), device_id_type=MESH)

    @pl.when(jnp.logical_and(me >= 2, pairs(me - 2)))
    def _():
        pl.semaphore_signal(barrier, inc=1, device_id=(me - 2, dep), device_id_type=MESH)

    @pl.when(has_above)
    def _():
        pl.semaphore_signal(barrier, inc=1, device_id=(me, dep + 1), device_id_type=MESH)

    step = cx // 4
    columns = [
        pltpu.make_async_copy(
            st.at[3 * f, pl.ds(k * step, step), :, pl.ds(row, 128)],
            col.at[f, pl.ds(k * step, step)],
            lsem.at[2],
        )
        for k in range(4)
        for f in range(2)
    ]
    small = [
        pltpu.make_async_copy(order, po, lsem.at[0]),
        pltpu.make_async_copy(fp, pb, lsem.at[1]),
    ]
    z_rows = (
        (4, cz - 2), (4, cz - 1), (5, cz - 2), (5, cz - 1), (2, cz - 1),
        (4, 0), (5, 0), (2, 0), (2, 1),
    )
    zloads = [
        pltpu.make_async_copy(st.at[f, :, r], zout.at[k], lsem.at[3])
        for k, (f, r) in enumerate(z_rows)
    ]
    loads = [
        pltpu.make_async_copy(st.at[0], sx.at[0, pl.ds(2, cx)], lsem.at[4]),
        pltpu.make_async_copy(
            st.at[pl.ds(3, 2)], sx.at[pl.ds(1, 2), pl.ds(2, cx)], lsem.at[4]
        ),
        pltpu.make_async_copy(st.at[pl.ds(1, 2)], so.at[pl.ds(0, 2)], lsem.at[4]),
        pltpu.make_async_copy(st.at[5], so.at[2], lsem.at[4]),
        pltpu.make_async_copy(mat, mb, lsem.at[5]),
        pltpu.make_async_copy(vel, vb, lsem.at[5]),
    ]
    for load in small + columns + zloads + loads:
        load.start()

    def arrived(ref, sem):
        pltpu.make_async_copy(ref, ref, sem).wait()

    def both_arrived(one, other, first_ref, other_ref, whole_ref, sem):
        @pl.when(jnp.logical_and(one, other))
        def _():
            arrived(whole_ref, sem)

        @pl.when(jnp.logical_and(one, jnp.logical_not(other)))
        def _():
            arrived(first_ref, sem)

        @pl.when(jnp.logical_and(other, jnp.logical_not(one)))
        def _():
            arrived(other_ref, sem)

    zlo, zhi = zin.at[pl.ds(0, 5)], zin.at[pl.ds(5, 4)]
    zero_row = jnp.zeros((2, cz, ny), jnp.float32)

    @pl.when(jnp.logical_not(has_left))
    def _():
        for f in range(3):
            sx[f, 0:2] = zero_row

    @pl.when(jnp.logical_not(has_right))
    def _():
        for f in range(3):
            sx[f, cx + 2 : cx + 4] = zero_row

    @pl.when(jnp.logical_not(has_below))
    def _():
        zin[0:5] = jnp.zeros((5, cx, ny), jnp.float32)

    @pl.when(jnp.logical_not(has_above))
    def _():
        zin[5:9] = jnp.zeros((4, cx, ny), jnp.float32)

    for j in range(n):
        if not near_at(j):

            @pl.when(jnp.logical_not(is_tile))
            def _():
                recv[j] = jnp.zeros(recv.shape[1:], jnp.float32)

    def x_copies(up, fields=(0, 1, 2)):
        copies = []
        for f in fields:
            plane = (0, 3, 4)[f]
            if up:
                rows = 2 if f == 0 else 1
                src, dst, to = cx - rows, 2 - rows, me + 1
            else:
                rows = 1 if f == 0 else 2
                src, dst, to = 0, cx + 2, me - 1
            copies.append(
                pltpu.make_async_remote_copy(
                    src_ref=st.at[plane, pl.ds(src, rows)],
                    dst_ref=sx.at[f, pl.ds(dst, rows)],
                    send_sem=xsend,
                    recv_sem=xrecv,
                    device_id=(to, dep),
                    device_id_type=MESH,
                )
            )
        return copies

    def z_copy(up):
        return pltpu.make_async_remote_copy(
            src_ref=zout.at[pl.ds(0, 5)] if up else zout.at[pl.ds(5, 4)],
            dst_ref=zlo if up else zhi,
            send_sem=zsend,
            recv_sem=zrecv,
            device_id=(me, dep + 1 if up else dep - 1),
            device_id_type=MESH,
        )

    def pack_copy(j):
        return pltpu.make_async_remote_copy(
            src_ref=packs.at[min(max(j - first_tile, 0), tiles - 1)],
            dst_ref=recv.at[me],
            send_sem=psend,
            recv_sem=precv,
            device_id=(j, dep),
            device_id_type=MESH,
        )

    def pack_next():
        for j in range(1, n):

            @pl.when(jnp.logical_and(j == me + 1, sends_to(j)))
            def _():
                pack_copy(j).start()

            @pl.when(jnp.logical_and(j == me + 1, halo_to(j)))
            def _():
                halo_copy(j).start()

    def halo_copy(j):
        return pltpu.make_async_remote_copy(
            src_ref=st.at[0, 0, :, pl.ds(row, 128)],
            dst_ref=halo,
            send_sem=hsend,
            recv_sem=hrecv,
            device_id=(j, dep),
            device_id_type=MESH,
        )

    ahead_of_me = jnp.int32(0)
    for j in range(n):
        ahead_of_me = ahead_of_me + jnp.logical_and(j < me, partner(j)).astype(jnp.int32)
    earlier = ahead_of_me + has_below.astype(jnp.int32) + 2 * paired.astype(jnp.int32)
    earlier = earlier - beyond.astype(jnp.int32)
    late = me > last

    fast = me % 2 == 1

    def enter():
        @pl.when(earlier > 0)
        def _():
            pl.semaphore_wait(barrier, earlier)

        @pl.when(is_end)
        def _():
            pl.semaphore_signal(
                far_in.at[1], inc=1, device_id=(head, dep), device_id_type=MESH
            )

        @pl.when(is_last)
        def _():
            for j in range(last):
                halo_copy(j).start()

        spoken_for = jnp.logical_and(me > 2, pairs(me - 2))
        for j in range(n):
            told = jnp.logical_and(j < me - 1, reached_by(j))
            if j == head:
                told = jnp.logical_and(told, jnp.logical_not(beyond))
            told = jnp.logical_and(told, jnp.logical_not(jnp.logical_and(spoken_for, j == me - 3)))

            @pl.when(told)
            def _():
                pl.semaphore_signal(
                    far_in.at[late.astype(jnp.int32)],
                    inc=1,
                    device_id=(j, dep),
                    device_id_type=MESH,
                )

        @pl.when(paired)
        def _():
            pl.semaphore_signal(next_in, inc=1, device_id=(me + 1, dep), device_id_type=MESH)

        @pl.when(jnp.logical_and(paired, me > 0))
        def _():
            pl.semaphore_signal(
                far_in.at[is_end.astype(jnp.int32)],
                inc=1,
                device_id=(me - 1, dep),
                device_id_type=MESH,
            )

        silent = jnp.logical_or(pairs(me - 1), jnp.logical_and(me >= 2, pairs(me - 2)))

        @pl.when(jnp.logical_and(has_left, jnp.logical_not(silent)))
        def _():
            pl.semaphore_signal(next_in, inc=1, device_id=(me - 1, dep), device_id_type=MESH)

        @pl.when(has_below)
        def _():
            pl.semaphore_signal(depth_in, inc=1, device_id=(me, dep - 1), device_id_type=MESH)

        @pl.when(jnp.logical_and(has_left, fast))
        def _():
            for copy in x_copies(False, (1,)):
                copy.start()

    with jax.named_scope("entry_fast"):
        pl.when(fast)(enter)

    lane = lax.broadcasted_iota(jnp.int32, (cz, wide), 1)
    lane_one = lax.broadcasted_iota(jnp.int32, (cz, 128), 1)
    my_tile = jnp.clip(me - first_tile, 0, tiles - 1)
    with jax.named_scope("params_wait"):
        for load in small:
            load.wait()
    with jax.named_scope("params"):
        blocks = [jnp.zeros((cz, wide), jnp.float32) for _ in range(tiles)]
        params = [pb[j].T for j in range(per)]
        ownp[...] = jnp.ones(ownp.shape, jnp.float32)
        for f in range(4):
            for j in range(per):
                column = po[me * per + j]
                value = params[j][:, f : f + 1]
                ownp[f, j : j + 1] = pb[j, f : f + 1]
                for t in range(tiles):
                    local = column - t * cx
                    held = jnp.logical_and(local >= 0, local < cx)
                    place = jnp.where(held, f * cx + local, -1)
                    blocks[t] = jnp.where(lane == place, value, blocks[t])
        for f, value in enumerate(law(ownp[0], ownp[1], ownp[2])):
            ownp[f] = value
        picks[...] = jnp.zeros(picks.shape, jnp.float32)
        for j in range(per):
            slot_lane = lane[0:1] == 4 * cx + po[me * per + j]
            picks[j : j + 1] = jnp.where(slot_lane, 1.0, 0.0)
        for t in range(tiles):
            packs[t] = blocks[t]
    with jax.named_scope("column_wait"):
        arrived(col, lsem.at[2])
    with jax.named_scope("pack"):

        @pl.when(near)
        def _():
            base = 4 * cx + (me - first_tile) * cx
            normal = jnp.zeros((cz, wide), jnp.float32)
            shear = jnp.zeros((cz, wide), jnp.float32)
            for i in range(cx):
                here = lane == base + i
                normal = jnp.where(here, col[0, i, :, 0:1], normal)
                shear = jnp.where(here, col[1, i, :, 0:1], shear)
            dxx = C_ONE * (normal - pltpu.roll(normal, 1, 1)) + C_TWO * (
                pltpu.roll(normal, wide - 1, 1) - pltpu.roll(normal, 2, 1)
            )
            share = shear + 0.5 * dxx
            inside = jnp.logical_and(lane >= 4 * cx, lane < 4 * cx + fc)
            share = jnp.where(inside, share, 0.0)
            for t in range(tiles):
                packs[t] = packs[t] + share
            recv[me] = packs[my_tile]

        @pl.when(is_last)
        def _():
            halo[...] = col[0, 0]

    with jax.named_scope("entry_slow"):
        pl.when(jnp.logical_not(fast))(enter)

    for j in range(n):

        @pl.when(jnp.logical_and(j < me, sends_to(j)))
        def _():
            pack_copy(j).start()

    @pl.when(paired)
    def _():
        pack_next()

    @pl.when(jnp.logical_and(has_left, fast))
    def _():
        for copy in x_copies(False, (0, 2)):
            copy.start()

    @pl.when(jnp.logical_and(has_left, jnp.logical_not(fast)))
    def _():
        for copy in x_copies(False):
            copy.start()

    @pl.when(paired)
    def _():
        for copy in x_copies(True):
            copy.start()

    with jax.named_scope("z_loads"):
        arrived(zout, lsem.at[3])

    @pl.when(has_below)
    def _():
        z_copy(False).start()

    def send_far(low, high, kind):
        group = [
            (j, jnp.logical_and(j > me + 1, reaches(j))) for j in range(low, high)
        ]
        count = sum(on.astype(jnp.int32) for _, on in group)

        @pl.when(count > 0)
        def _():
            pl.semaphore_wait(far_in.at[kind], count)

        for j, on in group:

            @pl.when(jnp.logical_and(on, sends_to(j)))
            def _():
                pack_copy(j).start()

            @pl.when(jnp.logical_and(on, halo_to(j)))
            def _():
                halo_copy(j).start()

    with jax.named_scope("wait_next"):

        @pl.when(jnp.logical_and(has_right, jnp.logical_not(paired)))
        def _():
            pl.semaphore_wait(next_in, 1)
            pack_next()
            for copy in x_copies(True):
                copy.start()

        @pl.when(has_above)
        def _():
            pl.semaphore_wait(depth_in, 1)
            z_copy(True).start()

    with jax.named_scope("lead_far"):
        @pl.when(lead)
        def _():
            send_far(2, last + 1, 0)
            send_far(last + 1, n, 1)

    with jax.named_scope("loads"):
        arrived(st, lsem.at[4])
        arrived(st.at[pl.ds(0, 4)], lsem.at[5])

    yi = lax.broadcasted_iota(jnp.int32, (cz, ny), 1)
    zi = lax.broadcasted_iota(jnp.int32, (cz, ny), 0)

    def y_at(field, offset):
        moved = pltpu.roll(field, (-offset) % ny, 1)
        keep = yi < ny - offset if offset > 0 else yi >= -offset
        return jnp.where(keep, moved, 0.0)

    def z_at(field):
        def at(offset):
            if offset == 0:
                return field
            moved = pltpu.roll(field, (-offset) % cz, 0)
            keep = zi < cz - offset if offset > 0 else zi >= -offset
            return jnp.where(keep, moved, 0.0)

        return at

    def minus(at):
        return C_ONE * (at(0) - at(-1)) + C_TWO * (at(1) - at(-2))

    def plus(at):
        return C_ONE * (at(1) - at(0)) + C_TWO * (at(2) - at(-1))

    def along_x(f, x):
        return lambda offset: sx[f, x + 2 + offset]

    def along_y(field):
        return lambda offset: field if offset == 0 else y_at(field, offset)

    def buoyancy(x):
        material = mb[x]
        b = jnp.full((cz, ny), 0.25 * BUOY[0], jnp.float32)
        for index in range(1, 4):
            b = jnp.where(material == index, 0.25 * BUOY[index], b)
        bb[x] = b
        return b

    def across(x):
        return minus(along_x(0, x)), plus(along_x(1, x)), plus(along_x(2, x))

    def local(x):
        sxz, szz, syz = sx[2, x + 2], so[1, x], so[2, x]
        return (
            minus(along_y(sx[1, x + 2])) + minus(z_at(sxz)),
            plus(along_y(so[0, x])) + minus(z_at(syz)),
            plus(along_y(syz)) + plus(z_at(szz)),
        )

    def inner(x, carry):
        b, along, rest = buoyancy(x), across(x), local(x)
        for c in range(3):
            out[c, x] = vb[c, x] + b * (along[c] + rest[c])
        return carry

    def outer(x):
        b, rest = buoyancy(x), local(x)
        for c in range(3):
            out[c, x] = vb[c, x] + b * rest[c]

    edges = (0, 1, cx - 2, cx - 1)
    with jax.named_scope("outer"):
        for x in edges:
            outer(x)

    middle = cx // 2
    with jax.named_scope("inner"):
        lax.fori_loop(2, middle, inner, 0)

    with jax.named_scope("wait_far"):
        pl.when(jnp.logical_not(lead))(lambda: send_far(2, last + 1, 0))
    with jax.named_scope("wait_far2"):
        pl.when(jnp.logical_not(lead))(lambda: send_far(last + 1, n, 1))

    with jax.named_scope("inner2"):
        lax.fori_loop(middle, cx - 2, inner, 0)
    def z_done(up, down, sem):
        both_arrived(up, down, zin.at[pl.ds(0, 5)], zin.at[pl.ds(0, 4)], zin, sem)

    with jax.named_scope("z_wait"):

        z_done(has_below, has_above, zrecv)

    first = lax.broadcasted_iota(jnp.int32, (8, ny), 0)

    def face(x, carry):
        def low(k):
            return zin[k, pl.ds(x, 1), :]

        def high(k):
            return zin[5 + k, pl.ds(x, 1), :]

        def put(at, one, two):
            return jnp.where(first == at, one, jnp.where(first == two[0], two[1], 0.0))

        b = bb[x, 0:8]
        out[0, x, 0:8] -= b * put(0, C_ONE * low(1) + C_TWO * low(0), (1, C_TWO * low(1)))
        out[1, x, 0:8] -= b * put(0, C_ONE * low(3) + C_TWO * low(2), (1, C_TWO * low(3)))
        out[2, x, 0:8] -= b * jnp.where(first == 0, C_TWO * low(4), 0.0)
        b = bb[x, cz - 8 : cz]
        out[0, x, cz - 8 : cz] += b * jnp.where(first == 7, C_TWO * high(0), 0.0)
        out[1, x, cz - 8 : cz] += b * jnp.where(first == 7, C_TWO * high(1), 0.0)
        out[2, x, cz - 8 : cz] += b * put(
            7, C_ONE * high(2) + C_TWO * high(3), (6, C_TWO * high(2))
        )
        return carry

    with jax.named_scope("face"):
        lax.fori_loop(0, cx, face, 0)

    def level(columns):
        for start in range(0, len(columns), 4):
            parts = []
            for i in columns[start : start + 4]:
                low = out[0, i, :, row - 128 : row]
                high = out[0, i, :, row : row + 128]
                above = 0.5 * (high + pltpu.roll(low, 1, 1))
                below = 0.5 * (pltpu.roll(high, 127, 1) + low)
                low = jnp.where(lane_one == 127, below, low)
                parts.append((i, low, jnp.where(lane_one == 0, above, high)))
            for i, low, high in parts:
                out[0, i, :, row - 128 : row] = low
                out[0, i, :, row : row + 128] = high

    with jax.named_scope("mean_inside"):

        @pl.when(is_tile)
        def _():
            level(range(2, cx - 2))

    outside = jnp.logical_or(me < head, me > last)

    def x_done(up, down, sem):
        line = sx.at[0]
        both_arrived(
            up, down, line.at[pl.ds(0, 4)], line.at[pl.ds(0, 5)], line.at[pl.ds(0, 9)], sem
        )

    def add_edges(on_fault=False):
        with jax.named_scope("x_wait"):

            x_done(has_left, has_right, xrecv)

        with jax.named_scope("edges"):
            for x in edges:
                along = across(x)
                for c in range(1, 3):
                    out[c, x] += bb[x] * along[c]
                value = out[0, x] + bb[x] * along[0]
                if not on_fault:
                    out[0, x] = value
                    continue
                low, high = value[:, row - 128 : row], value[:, row : row + 128]
                above = 0.5 * (high + pltpu.roll(low, 1, 1))
                below = 0.5 * (pltpu.roll(high, 127, 1) + low)
                s = rates[:, x : x + 1]
                low = jnp.where(lane_one == 127, below - s, low)
                high = jnp.where(lane_one == 0, above + s, high)
                out[0, x, :, row - 128 : row] = low
                out[0, x, :, row : row + 128] = high
                if row > 128:
                    out[0, x, :, : row - 128] = value[:, : row - 128]
                    out[0, x, :, row + 128 :] = value[:, row + 128 :]

    pl.when(outside)(add_edges)

    with jax.named_scope("pack_wait"):
        @pl.when(is_tile)
        def _():
            arrived(recv.at[pl.ds(0, n - 1)], precv)

        @pl.when(me == first_tile - 1)
        def _():
            arrived(recv.at[pl.ds(0, tiles)], precv)

        @pl.when(jnp.logical_not(near))
        def _():
            arrived(recv.at[pl.ds(0, tiles + 1)], precv)

        @pl.when(jnp.logical_not(is_last))
        def _():
            arrived(halo, hrecv)

    with jax.named_scope("friction"):
        total = recv[first_tile - 1]
        for j in range(n):
            if j != first_tile - 1:
                total = total + recv[j]
        edge = 0.5 * C_TWO * halo[:, 0:1]
        total = total + jnp.where(lane == 4 * cx + fc - 1, edge, 0.0)

        sums[...] = total

        @pl.when(is_tile)
        def _():
            fields = [total[:, :128]]
            for f in range(1, 4):
                fields.append(pltpu.roll(total, wide - f * cx, 1)[:, :128])
            used = lane_one < cx
            fields = [jnp.where(used, field, 1.0) for field in fields]
            tau = fields[3]
            for t in range(tiles):
                moved = pltpu.roll(total, wide - (4 + t) * cx, 1)[:, :128]
                tau = tau + jnp.where(jnp.logical_and(used, my_tile == t), moved, 0.0)
            rates[...] = 0.5 * friction(tau, *law(*fields[:3]))

    def fix(columns):
        for start in range(0, len(columns), 4):
            parts = []
            for i in columns[start : start + 4]:
                s = rates[:, i : i + 1]
                low = out[0, i, :, row - 128 : row]
                high = out[0, i, :, row : row + 128]
                low = low - jnp.where(lane_one == 127, s, 0.0)
                high = high + jnp.where(lane_one == 0, s, 0.0)
                parts.append((i, low, high))
            for i, low, high in parts:
                out[0, i, :, row - 128 : row] = low
                out[0, i, :, row : row + 128] = high

    with jax.named_scope("fix"):

        @pl.when(is_tile)
        def _():
            fix(range(2, cx - 2))

    pl.when(jnp.logical_or(lead, is_last))(add_edges)
    pl.when(is_tile)(functools.partial(add_edges, True))

    with jax.named_scope("sends_done"):
        @pl.when(near)
        def _():
            arrived(recv.at[pl.ds(0, n - 1)], psend)

        @pl.when(jnp.logical_not(near))
        def _():
            arrived(recv.at[pl.ds(0, tiles)], psend)

        @pl.when(is_last)
        def _():
            arrived(recv.at[pl.ds(0, n - 1), :, pl.ds(0, 128)], hsend)

        z_done(has_above, has_below, zsend)
        x_done(has_right, has_left, xsend)


def write_out(held, sums, params, picks, out, slip_out, slip, sem):
    velocity = pltpu.make_async_copy(held, out, sem.at[0])
    velocity.start()
    tau = params[3] + lax.dot_general(
        picks[...],
        sums[...],
        (((1,), (1,)), ((), ())),
        precision=lax.Precision.HIGHEST,
        preferred_element_type=jnp.float32,
    )
    rate = friction(tau, params[0], params[1], params[2])
    slip[...] = rate[: slip.shape[0]]
    rates = pltpu.make_async_copy(slip, slip_out, sem.at[1])
    rates.start()
    velocity.wait()
    rates.wait()


def per_device(n, nd, velocity, stress, material, patch_order, fault_params):
    _, cx, cz, ny = stress.shape
    fc = patch_order.shape[0]
    per = fc // n
    wide = -(-(4 * cx + fc + 2) // 128) * 128
    dims = (n, nd, cx, cz, ny, fc, wide)
    tiles = fc // cx
    f32 = jnp.float32
    anywhere = pl.BlockSpec(memory_space=pltpu.HBM)
    dma = pltpu.SemaphoreType.DMA
    params = jnp.transpose(fault_params, (2, 0, 1))
    big = (velocity, stress, material, patch_order, params)
    held = pl.pallas_call(
        functools.partial(kernel, dims),
        out_shape=(
            jax.ShapeDtypeStruct(velocity.shape, f32),
            jax.ShapeDtypeStruct((cz, wide), f32),
            jax.ShapeDtypeStruct((4, -(-per // 8) * 8, cz), f32),
            jax.ShapeDtypeStruct((-(-per // 8) * 8, wide), f32),
        ),
        in_specs=[anywhere] * 5,
        out_specs=(pl.BlockSpec(memory_space=pltpu.VMEM),) * 4,
        scratch_shapes=[
            pltpu.SMEM((fc,), jnp.int32),
            pltpu.VMEM((2, cx, cz, 128), f32),
            pltpu.VMEM((3, cx + 4, cz, ny), f32),
            pltpu.VMEM((3, cx, cz, ny), f32),
            pltpu.VMEM((3, cx, cz, ny), f32),
            pltpu.VMEM((cx, cz, ny), jnp.int32),
            pltpu.VMEM((cx, cz, ny), f32),
            pltpu.VMEM((per, 4, cz), f32),
            pltpu.VMEM((9, cx, ny), f32),
            pltpu.VMEM((9, cx, ny), f32),
            pltpu.VMEM((tiles, cz, wide), f32),
            pltpu.VMEM((n, cz, wide), f32),
            pltpu.VMEM((cz, 128), f32),
            pltpu.VMEM((cz, 128), f32),
            dma((6,)),
            dma,
            dma,
            dma,
            dma,
            dma,
            dma,
            dma,
            dma,
            pltpu.SemaphoreType.REGULAR,
            pltpu.SemaphoreType.REGULAR((2,)),
            pltpu.SemaphoreType.REGULAR,
        ],
        compiler_params=pltpu.CompilerParams(collective_id=0, has_side_effects=True, vmem_limit_bytes=12 << 20),
    )(*[pltpu.with_memory_space_constraint(v, pltpu.HBM) for v in big])
    resident = pl.BlockSpec(memory_space=pltpu.VMEM)
    moved, slip = pl.pallas_call(
        write_out,
        out_shape=(
            jax.ShapeDtypeStruct(velocity.shape, f32),
            jax.ShapeDtypeStruct((per, cz), f32),
        ),
        in_specs=[resident] * 4,
        out_specs=(anywhere, anywhere),
        scratch_shapes=[pltpu.VMEM((per, cz), f32), dma((2,))],
        compiler_params=pltpu.CompilerParams(vmem_limit_bytes=4 << 20),
    )(*held)
    return moved, slip.T


def solution(mesh):
    n, nd = mesh.shape["strike"], mesh.shape["depth"]
    return jax.shard_map(
        functools.partial(per_device, n, nd),
        mesh=mesh,
        in_specs=(
            P(None, "strike", "depth", None),
            P(None, "strike", "depth", None),
            P("strike", "depth", None),
            P(),
            P(None, "depth", "strike"),
        ),
        out_specs=(P(None, "strike", "depth", None), P("depth", "strike")),
        check_vma=False,
    )
```

```python
import functools

import jax
import jax.numpy as jnp
from jax import lax
from jax.experimental import pallas as pl
from jax.experimental.pallas import tpu as pltpu
from jax.sharding import PartitionSpec as P

NEWTON = 8
BUOY = (1.0, 0.8, 0.6, 1.25)
C_ONE = 9.0 / 8.0
C_TWO = -1.0 / 24.0
MESH = pl.DeviceIdType.MESH


def law(coef, psi, normal_stress):
    half_q = 0.5 * jnp.exp(psi / coef)
    scale = normal_stress * coef
    return half_q, scale, scale * half_q


def friction(tau_total, half_q, scale, stiff):
    rate = 0.35 * tau_total / (1.0 + stiff)
    for _ in range(NEWTON - 1):
        arg_val = rate * half_q
        square = 1.0 + arg_val * arg_val
        inverse = lax.rsqrt(square)
        gain = 0.35 / (1.0 + stiff * inverse)
        magnitude = scale * jnp.log(jnp.abs(arg_val) + square * inverse)
        resid = tau_total - rate - jnp.where(arg_val < 0, -magnitude, magnitude)
        rate = rate + resid * gain
    return rate


def kernel(
    dims, vel, st, mat, order, fp, out, sums, ownp, picks,
    po, col, sx, so, vb, mb, bb, pb, zout, zin, packs, recv, halo, rates,
    lsem, psend, precv, hsend, hrecv, xsend, xrecv, zsend, zrecv, next_in, far_in, depth_in,
):
    n, nd, cx, cz, ny, fc, wide = dims
    row = ny // 2
    per = fc // n
    first_tile = n // 4
    tiles = fc // cx
    me = lax.axis_index("strike")
    dep = lax.axis_index("depth")
    has_left, has_right = me > 0, me < n - 1
    has_below, has_above = dep > 0, dep < nd - 1
    is_tile = jnp.logical_and(me >= first_tile, me < first_tile + tiles)
    near = jnp.logical_and(me >= first_tile - 1, me < first_tile + tiles)

    def tile_at(j):
        return first_tile <= j < first_tile + tiles

    def near_at(j):
        return first_tile - 1 <= j < first_tile + tiles

    last = first_tile + tiles
    is_last = me == last

    def pairs(j):
        inside = jnp.logical_and(j >= first_tile, j < last)
        return jnp.logical_or(j == 0, jnp.logical_and(j % 2 == first_tile % 2, inside))

    paired = pairs(me)
    head = first_tile - 1
    lead = me == head
    beyond = me == last + 1
    is_end = me == last - 1

    def sends_to(j):
        return jnp.logical_and(me != j, jnp.logical_or(near, tile_at(j)))

    def halo_to(j):
        return jnp.logical_and(is_last, me != j)

    def reaches(j):
        return jnp.logical_or(sends_to(j), halo_to(j))

    def reached_by(j):
        return jnp.logical_and(me != j, jnp.logical_or(is_tile, near_at(j) or j == last))

    def partner(j):
        beside = jnp.logical_or(me == j - 1, me == j + 1)
        return jnp.logical_or(beside, jnp.logical_or(reaches(j), reached_by(j)))

    barrier = pltpu.get_barrier_semaphore()
    for j in range(n):

        back = jnp.logical_and(j == me - 1, pairs(j))

        ahead = jnp.logical_and(j > me, partner(j))
        if j == last + 1:
            ahead = jnp.logical_and(ahead, jnp.logical_not(lead))

        @pl.when(jnp.logical_or(ahead, back))
        def _():
            pl.semaphore_signal(barrier, inc=1, device_id=(j, dep), device_id_type=MESH)

    @pl.when(jnp.logical_and(me >= 2, pairs(me - 2)))
    def _():
        pl.semaphore_signal(barrier, inc=1, device_id=(me - 2, dep), device_id_type=MESH)

    @pl.when(has_above)
    def _():
        pl.semaphore_signal(barrier, inc=1, device_id=(me, dep + 1), device_id_type=MESH)

    step = cx // 4
    columns = [
        pltpu.make_async_copy(
            st.at[3 * f, pl.ds(k * step, step), :, pl.ds(row, 128)],
            col.at[f, pl.ds(k * step, step)],
            lsem.at[2],
        )
        for k in range(4)
        for f in range(2)
    ]
    small = [
        pltpu.make_async_copy(order, po, lsem.at[0]),
        pltpu.make_async_copy(fp, pb, lsem.at[1]),
    ]
    z_rows = (
        (4, cz - 2), (4, cz - 1), (5, cz - 2), (5, cz - 1), (2, cz - 1),
        (4, 0), (5, 0), (2, 0), (2, 1),
    )
    zloads = [
        pltpu.make_async_copy(st.at[f, :, r], zout.at[k], lsem.at[3])
        for k, (f, r) in enumerate(z_rows)
    ]
    loads = [
        pltpu.make_async_copy(st.at[0], sx.at[0, pl.ds(2, cx)], lsem.at[4]),
        pltpu.make_async_copy(
            st.at[pl.ds(3, 2)], sx.at[pl.ds(1, 2), pl.ds(2, cx)], lsem.at[4]
        ),
        pltpu.make_async_copy(st.at[pl.ds(1, 2)], so.at[pl.ds(0, 2)], lsem.at[4]),
        pltpu.make_async_copy(st.at[5], so.at[2], lsem.at[4]),
        pltpu.make_async_copy(mat, mb, lsem.at[5]),
        pltpu.make_async_copy(vel, vb, lsem.at[5]),
    ]
    for load in small + columns + zloads + loads:
        load.start()

    def arrived(ref, sem):
        pltpu.make_async_copy(ref, ref, sem).wait()

    def both_arrived(one, other, first_ref, other_ref, whole_ref, sem):
        @pl.when(jnp.logical_and(one, other))
        def _():
            arrived(whole_ref, sem)

        @pl.when(jnp.logical_and(one, jnp.logical_not(other)))
        def _():
            arrived(first_ref, sem)

        @pl.when(jnp.logical_and(other, jnp.logical_not(one)))
        def _():
            arrived(other_ref, sem)

    zlo, zhi = zin.at[pl.ds(0, 5)], zin.at[pl.ds(5, 4)]
    zero_row = jnp.zeros((2, cz, ny), jnp.float32)

    @pl.when(jnp.logical_not(has_left))
    def _():
        for f in range(3):
            sx[f, 0:2] = zero_row

    @pl.when(jnp.logical_not(has_right))
    def _():
        for f in range(3):
            sx[f, cx + 2 : cx + 4] = zero_row

    @pl.when(jnp.logical_not(has_below))
    def _():
        zin[0:5] = jnp.zeros((5, cx, ny), jnp.float32)

    @pl.when(jnp.logical_not(has_above))
    def _():
        zin[5:9] = jnp.zeros((4, cx, ny), jnp.float32)

    for j in range(n):
        if not near_at(j):

            @pl.when(jnp.logical_not(is_tile))
            def _():
                recv[j] = jnp.zeros(recv.shape[1:], jnp.float32)

    def x_copies(up, fields=(0, 1, 2)):
        copies = []
        for f in fields:
            plane = (0, 3, 4)[f]
            if up:
                rows = 2 if f == 0 else 1
                src, dst, to = cx - rows, 2 - rows, me + 1
            else:
                rows = 1 if f == 0 else 2
                src, dst, to = 0, cx + 2, me - 1
            copies.append(
                pltpu.make_async_remote_copy(
                    src_ref=st.at[plane, pl.ds(src, rows)],
                    dst_ref=sx.at[f, pl.ds(dst, rows)],
                    send_sem=xsend,
                    recv_sem=xrecv,
                    device_id=(to, dep),
                    device_id_type=MESH,
                )
            )
        return copies

    def z_copy(up):
        return pltpu.make_async_remote_copy(
            src_ref=zout.at[pl.ds(0, 5)] if up else zout.at[pl.ds(5, 4)],
            dst_ref=zlo if up else zhi,
            send_sem=zsend,
            recv_sem=zrecv,
            device_id=(me, dep + 1 if up else dep - 1),
            device_id_type=MESH,
        )

    def pack_copy(j):
        return pltpu.make_async_remote_copy(
            src_ref=packs.at[min(max(j - first_tile, 0), tiles - 1)],
            dst_ref=recv.at[me],
            send_sem=psend,
            recv_sem=precv,
            device_id=(j, dep),
            device_id_type=MESH,
        )

    def pack_next():
        for j in range(1, n):

            @pl.when(jnp.logical_and(j == me + 1, sends_to(j)))
            def _():
                pack_copy(j).start()

            @pl.when(jnp.logical_and(j == me + 1, halo_to(j)))
            def _():
                halo_copy(j).start()

    def halo_copy(j):
        return pltpu.make_async_remote_copy(
            src_ref=st.at[0, 0, :, pl.ds(row, 128)],
            dst_ref=halo,
            send_sem=hsend,
            recv_sem=hrecv,
            device_id=(j, dep),
            device_id_type=MESH,
        )

    ahead_of_me = jnp.int32(0)
    for j in range(n):
        ahead_of_me = ahead_of_me + jnp.logical_and(j < me, partner(j)).astype(jnp.int32)
    earlier = ahead_of_me + has_below.astype(jnp.int32) + 2 * paired.astype(jnp.int32)
    earlier = earlier - beyond.astype(jnp.int32)
    late = me > last

    fast = me % 2 == 1

    def enter():
        @pl.when(earlier > 0)
        def _():
            pl.semaphore_wait(barrier, earlier)

        @pl.when(is_end)
        def _():
            pl.semaphore_signal(
                far_in.at[1], inc=1, device_id=(head, dep), device_id_type=MESH
            )

        @pl.when(is_last)
        def _():
            for j in range(last):
                halo_copy(j).start()

        spoken_for = jnp.logical_and(me > 2, pairs(me - 2))
        for j in range(n):
            told = jnp.logical_and(j < me - 1, reached_by(j))
            if j == head:
                told = jnp.logical_and(told, jnp.logical_not(beyond))
            told = jnp.logical_and(told, jnp.logical_not(jnp.logical_and(spoken_for, j == me - 3)))

            @pl.when(told)
            def _():
                pl.semaphore_signal(
                    far_in.at[late.astype(jnp.int32)],
                    inc=1,
                    device_id=(j, dep),
                    device_id_type=MESH,
                )

        @pl.when(paired)
        def _():
            pl.semaphore_signal(next_in, inc=1, device_id=(me + 1, dep), device_id_type=MESH)

        @pl.when(jnp.logical_and(paired, me > 0))
        def _():
            pl.semaphore_signal(
                far_in.at[is_end.astype(jnp.int32)],
                inc=1,
                device_id=(me - 1, dep),
                device_id_type=MESH,
            )

        silent = jnp.logical_or(pairs(me - 1), jnp.logical_and(me >= 2, pairs(me - 2)))

        @pl.when(jnp.logical_and(has_left, jnp.logical_not(silent)))
        def _():
            pl.semaphore_signal(next_in, inc=1, device_id=(me - 1, dep), device_id_type=MESH)

        @pl.when(has_below)
        def _():
            pl.semaphore_signal(depth_in, inc=1, device_id=(me, dep - 1), device_id_type=MESH)

        @pl.when(jnp.logical_and(has_left, fast))
        def _():
            for copy in x_copies(False, (1,)):
                copy.start()

    with jax.named_scope("entry_fast"):
        pl.when(fast)(enter)

    lane = lax.broadcasted_iota(jnp.int32, (cz, wide), 1)
    lane_one = lax.broadcasted_iota(jnp.int32, (cz, 128), 1)
    my_tile = jnp.clip(me - first_tile, 0, tiles - 1)
    with jax.named_scope("params_wait"):
        for load in small:
            load.wait()
    with jax.named_scope("params"):
        blocks = [jnp.zeros((cz, wide), jnp.float32) for _ in range(tiles)]
        params = [pb[j].T for j in range(per)]
        ownp[...] = jnp.ones(ownp.shape, jnp.float32)
        for f in range(4):
            for j in range(per):
                column = po[me * per + j]
                value = params[j][:, f : f + 1]
                ownp[f, j : j + 1] = pb[j, f : f + 1]
                for t in range(tiles):
                    local = column - t * cx
                    held = jnp.logical_and(local >= 0, local < cx)
                    place = jnp.where(held, f * cx + local, -1)
                    blocks[t] = jnp.where(lane == place, value, blocks[t])
        for f, value in enumerate(law(ownp[0], ownp[1], ownp[2])):
            ownp[f] = value
        picks[...] = jnp.zeros(picks.shape, jnp.float32)
        for j in range(per):
            slot_lane = lane[0:1] == 4 * cx + po[me * per + j]
            picks[j : j + 1] = jnp.where(slot_lane, 1.0, 0.0)
        for t in range(tiles):
            packs[t] = blocks[t]
    with jax.named_scope("column_wait"):
        arrived(col, lsem.at[2])
    with jax.named_scope("pack"):

        @pl.when(near)
        def _():
            base = 4 * cx + (me - first_tile) * cx
            normal = jnp.zeros((cz, wide), jnp.float32)
            shear = jnp.zeros((cz, wide), jnp.float32)
            for i in range(cx):
                here = lane == base + i
                normal = jnp.where(here, col[0, i, :, 0:1], normal)
                shear = jnp.where(here, col[1, i, :, 0:1], shear)
            dxx = C_ONE * (normal - pltpu.roll(normal, 1, 1)) + C_TWO * (
                pltpu.roll(normal, wide - 1, 1) - pltpu.roll(normal, 2, 1)
            )
            share = shear + 0.5 * dxx
            inside = jnp.logical_and(lane >= 4 * cx, lane < 4 * cx + fc)
            share = jnp.where(inside, share, 0.0)
            for t in range(tiles):
                packs[t] = packs[t] + share
            recv[me] = packs[my_tile]

        @pl.when(is_last)
        def _():
            halo[...] = col[0, 0]

    with jax.named_scope("entry_slow"):
        pl.when(jnp.logical_not(fast))(enter)

    for j in range(n):

        @pl.when(jnp.logical_and(j < me, sends_to(j)))
        def _():
            pack_copy(j).start()

    @pl.when(paired)
    def _():
        pack_next()

    @pl.when(jnp.logical_and(has_left, fast))
    def _():
        for copy in x_copies(False, (0, 2)):
            copy.start()

    @pl.when(jnp.logical_and(has_left, jnp.logical_not(fast)))
    def _():
        for copy in x_copies(False):
            copy.start()

    @pl.when(paired)
    def _():
        for copy in x_copies(True):
            copy.start()

    with jax.named_scope("z_loads"):
        arrived(zout, lsem.at[3])

    @pl.when(has_below)
    def _():
        z_copy(False).start()

    def send_far(low, high, kind):
        group = [
            (j, jnp.logical_and(j > me + 1, reaches(j))) for j in range(low, high)
        ]
        count = sum(on.astype(jnp.int32) for _, on in group)

        @pl.when(count > 0)
        def _():
            pl.semaphore_wait(far_in.at[kind], count)

        for j, on in group:

            @pl.when(jnp.logical_and(on, sends_to(j)))
            def _():
                pack_copy(j).start()

            @pl.when(jnp.logical_and(on, halo_to(j)))
            def _():
                halo_copy(j).start()

    with jax.named_scope("wait_next"):

        @pl.when(jnp.logical_and(has_right, jnp.logical_not(paired)))
        def _():
            pl.semaphore_wait(next_in, 1)
            pack_next()
            for copy in x_copies(True):
                copy.start()

        @pl.when(has_above)
        def _():
            pl.semaphore_wait(depth_in, 1)
            z_copy(True).start()

    with jax.named_scope("lead_far"):
        @pl.when(lead)
        def _():
            send_far(2, last + 1, 0)
            send_far(last + 1, n, 1)

    with jax.named_scope("loads"):
        arrived(st, lsem.at[4])
        arrived(st.at[pl.ds(0, 4)], lsem.at[5])

    yi = lax.broadcasted_iota(jnp.int32, (cz, ny), 1)
    zi = lax.broadcasted_iota(jnp.int32, (cz, ny), 0)

    def y_at(field, offset):
        moved = pltpu.roll(field, (-offset) % ny, 1)
        keep = yi < ny - offset if offset > 0 else yi >= -offset
        return jnp.where(keep, moved, 0.0)

    def z_at(field):
        def at(offset):
            if offset == 0:
                return field
            moved = pltpu.roll(field, (-offset) % cz, 0)
            keep = zi < cz - offset if offset > 0 else zi >= -offset
            return jnp.where(keep, moved, 0.0)

        return at

    def minus(at):
        return C_ONE * (at(0) - at(-1)) + C_TWO * (at(1) - at(-2))

    def plus(at):
        return C_ONE * (at(1) - at(0)) + C_TWO * (at(2) - at(-1))

    def along_x(f, x):
        return lambda offset: sx[f, x + 2 + offset]

    def along_y(field):
        return lambda offset: field if offset == 0 else y_at(field, offset)

    def buoyancy(x):
        material = mb[x]
        b = jnp.full((cz, ny), 0.25 * BUOY[0], jnp.float32)
        for index in range(1, 4):
            b = jnp.where(material == index, 0.25 * BUOY[index], b)
        bb[x] = b
        return b

    def across(x):
        return minus(along_x(0, x)), plus(along_x(1, x)), plus(along_x(2, x))

    def local(x):
        sxz, szz, syz = sx[2, x + 2], so[1, x], so[2, x]
        return (
            minus(along_y(sx[1, x + 2])) + minus(z_at(sxz)),
            plus(along_y(so[0, x])) + minus(z_at(syz)),
            plus(along_y(syz)) + plus(z_at(szz)),
        )

    def inner(x, carry):
        b, along, rest = buoyancy(x), across(x), local(x)
        for c in range(3):
            out[c, x] = vb[c, x] + b * (along[c] + rest[c])
        return carry

    def outer(x):
        b, rest = buoyancy(x), local(x)
        for c in range(3):
            out[c, x] = vb[c, x] + b * rest[c]

    edges = (0, 1, cx - 2, cx - 1)
    with jax.named_scope("outer"):
        for x in edges:
            outer(x)

    middle = cx // 2
    with jax.named_scope("inner"):
        lax.fori_loop(2, middle, inner, 0)

    with jax.named_scope("wait_far"):
        pl.when(jnp.logical_not(lead))(lambda: send_far(2, last + 1, 0))
    with jax.named_scope("wait_far2"):
        pl.when(jnp.logical_not(lead))(lambda: send_far(last + 1, n, 1))

    with jax.named_scope("inner2"):
        lax.fori_loop(middle, cx - 2, inner, 0)
    def z_done(up, down, sem):
        both_arrived(up, down, zin.at[pl.ds(0, 5)], zin.at[pl.ds(0, 4)], zin, sem)

    with jax.named_scope("z_wait"):

        z_done(has_below, has_above, zrecv)

    first = lax.broadcasted_iota(jnp.int32, (8, ny), 0)

    def face(x, carry):
        def low(k):
            return zin[k, pl.ds(x, 1), :]

        def high(k):
            return zin[5 + k, pl.ds(x, 1), :]

        def put(at, one, two):
            return jnp.where(first == at, one, jnp.where(first == two[0], two[1], 0.0))

        b = bb[x, 0:8]
        out[0, x, 0:8] -= b * put(0, C_ONE * low(1) + C_TWO * low(0), (1, C_TWO * low(1)))
        out[1, x, 0:8] -= b * put(0, C_ONE * low(3) + C_TWO * low(2), (1, C_TWO * low(3)))
        out[2, x, 0:8] -= b * jnp.where(first == 0, C_TWO * low(4), 0.0)
        b = bb[x, cz - 8 : cz]
        out[0, x, cz - 8 : cz] += b * jnp.where(first == 7, C_TWO * high(0), 0.0)
        out[1, x, cz - 8 : cz] += b * jnp.where(first == 7, C_TWO * high(1), 0.0)
        out[2, x, cz - 8 : cz] += b * put(
            7, C_ONE * high(2) + C_TWO * high(3), (6, C_TWO * high(2))
        )
        return carry

    with jax.named_scope("face"):
        lax.fori_loop(0, cx, face, 0)

    def level(columns):
        for start in range(0, len(columns), 4):
            parts = []
            for i in columns[start : start + 4]:
                low = out[0, i, :, row - 128 : row]
                high = out[0, i, :, row : row + 128]
                above = 0.5 * (high + pltpu.roll(low, 1, 1))
                below = 0.5 * (pltpu.roll(high, 127, 1) + low)
                low = jnp.where(lane_one == 127, below, low)
                parts.append((i, low, jnp.where(lane_one == 0, above, high)))
            for i, low, high in parts:
                out[0, i, :, row - 128 : row] = low
                out[0, i, :, row : row + 128] = high

    with jax.named_scope("mean_inside"):

        @pl.when(is_tile)
        def _():
            level(range(2, cx - 2))

    outside = jnp.logical_or(me < head, me > last)

    def x_done(up, down, sem):
        line = sx.at[0]
        both_arrived(
            up, down, line.at[pl.ds(0, 4)], line.at[pl.ds(0, 5)], line.at[pl.ds(0, 9)], sem
        )

    def add_edges(on_fault=False):
        with jax.named_scope("x_wait"):

            x_done(has_left, has_right, xrecv)

        with jax.named_scope("edges"):
            for x in edges:
                along = across(x)
                for c in range(1, 3):
                    out[c, x] += bb[x] * along[c]
                value = out[0, x] + bb[x] * along[0]
                if not on_fault:
                    out[0, x] = value
                    continue
                low, high = value[:, row - 128 : row], value[:, row : row + 128]
                above = 0.5 * (high + pltpu.roll(low, 1, 1))
                below = 0.5 * (pltpu.roll(high, 127, 1) + low)
                s = rates[:, x : x + 1]
                low = jnp.where(lane_one == 127, below - s, low)
                high = jnp.where(lane_one == 0, above + s, high)
                out[0, x, :, row - 128 : row] = low
                out[0, x, :, row : row + 128] = high
                if row > 128:
                    out[0, x, :, : row - 128] = value[:, : row - 128]
                    out[0, x, :, row + 128 :] = value[:, row + 128 :]

    pl.when(outside)(add_edges)

    with jax.named_scope("pack_wait"):
        @pl.when(is_tile)
        def _():
            arrived(recv.at[pl.ds(0, n - 1)], precv)

        @pl.when(me == first_tile - 1)
        def _():
            arrived(recv.at[pl.ds(0, tiles)], precv)

        @pl.when(jnp.logical_not(near))
        def _():
            arrived(recv.at[pl.ds(0, tiles + 1)], precv)

        @pl.when(jnp.logical_not(is_last))
        def _():
            arrived(halo, hrecv)

    with jax.named_scope("friction"):
        total = recv[first_tile - 1]
        for j in range(n):
            if j != first_tile - 1:
                total = total + recv[j]
        edge = 0.5 * C_TWO * halo[:, 0:1]
        total = total + jnp.where(lane == 4 * cx + fc - 1, edge, 0.0)

        sums[...] = total

        @pl.when(is_tile)
        def _():
            fields = [total[:, :128]]
            for f in range(1, 4):
                fields.append(pltpu.roll(total, wide - f * cx, 1)[:, :128])
            used = lane_one < cx
            fields = [jnp.where(used, field, 1.0) for field in fields]
            tau = fields[3]
            for t in range(tiles):
                moved = pltpu.roll(total, wide - (4 + t) * cx, 1)[:, :128]
                tau = tau + jnp.where(jnp.logical_and(used, my_tile == t), moved, 0.0)
            rates[...] = 0.5 * friction(tau, *law(*fields[:3]))

    def fix(columns):
        for start in range(0, len(columns), 4):
            parts = []
            for i in columns[start : start + 4]:
                s = rates[:, i : i + 1]
                low = out[0, i, :, row - 128 : row]
                high = out[0, i, :, row : row + 128]
                low = low - jnp.where(lane_one == 127, s, 0.0)
                high = high + jnp.where(lane_one == 0, s, 0.0)
                parts.append((i, low, high))
            for i, low, high in parts:
                out[0, i, :, row - 128 : row] = low
                out[0, i, :, row : row + 128] = high

    with jax.named_scope("fix"):

        @pl.when(is_tile)
        def _():
            fix(range(2, cx - 2))

    pl.when(jnp.logical_or(lead, is_last))(add_edges)
    pl.when(is_tile)(functools.partial(add_edges, True))

    with jax.named_scope("sends_done"):
        @pl.when(near)
        def _():
            arrived(recv.at[pl.ds(0, n - 1)], psend)

        @pl.when(jnp.logical_not(near))
        def _():
            arrived(recv.at[pl.ds(0, tiles)], psend)

        @pl.when(is_last)
        def _():
            arrived(recv.at[pl.ds(0, n - 1), :, pl.ds(0, 128)], hsend)

        z_done(has_above, has_below, zsend)
        x_done(has_right, has_left, xsend)


def write_out(held, sums, params, picks, out, slip_out, slip, sem):
    rows = held.shape[1] // 1
    for c in range(3):
        for x in range(0, held.shape[1], rows):
            part = held.at[c, pl.ds(x, rows)], out.at[c, pl.ds(x, rows)]
            pltpu.make_async_copy(*part, sem.at[0]).start()
    tau = params[3] + lax.dot_general(
        picks[...],
        sums[...],
        (((1,), (1,)), ((), ())),
        precision=lax.Precision.HIGHEST,
        preferred_element_type=jnp.float32,
    )
    rate = friction(tau, params[0], params[1], params[2])
    slip[...] = rate[: slip.shape[0]]
    rates = pltpu.make_async_copy(slip, slip_out, sem.at[1])
    rates.start()
    pltpu.make_async_copy(held, out, sem.at[0]).wait()
    rates.wait()


def per_device(n, nd, velocity, stress, material, patch_order, fault_params):
    _, cx, cz, ny = stress.shape
    fc = patch_order.shape[0]
    per = fc // n
    wide = -(-(4 * cx + fc + 2) // 128) * 128
    dims = (n, nd, cx, cz, ny, fc, wide)
    tiles = fc // cx
    f32 = jnp.float32
    anywhere = pl.BlockSpec(memory_space=pltpu.HBM)
    dma = pltpu.SemaphoreType.DMA
    params = jnp.transpose(fault_params, (2, 0, 1))
    big = (velocity, stress, material, patch_order, params)
    held = pl.pallas_call(
        functools.partial(kernel, dims),
        out_shape=(
            jax.ShapeDtypeStruct(velocity.shape, f32),
            jax.ShapeDtypeStruct((cz, wide), f32),
            jax.ShapeDtypeStruct((4, -(-per // 8) * 8, cz), f32),
            jax.ShapeDtypeStruct((-(-per // 8) * 8, wide), f32),
        ),
        in_specs=[anywhere] * 5,
        out_specs=(pl.BlockSpec(memory_space=pltpu.VMEM),) * 4,
        scratch_shapes=[
            pltpu.SMEM((fc,), jnp.int32),
            pltpu.VMEM((2, cx, cz, 128), f32),
            pltpu.VMEM((3, cx + 4, cz, ny), f32),
            pltpu.VMEM((3, cx, cz, ny), f32),
            pltpu.VMEM((3, cx, cz, ny), f32),
            pltpu.VMEM((cx, cz, ny), jnp.int32),
            pltpu.VMEM((cx, cz, ny), f32),
            pltpu.VMEM((per, 4, cz), f32),
            pltpu.VMEM((9, cx, ny), f32),
            pltpu.VMEM((9, cx, ny), f32),
            pltpu.VMEM((tiles, cz, wide), f32),
            pltpu.VMEM((n, cz, wide), f32),
            pltpu.VMEM((cz, 128), f32),
            pltpu.VMEM((cz, 128), f32),
            dma((6,)),
            dma,
            dma,
            dma,
            dma,
            dma,
            dma,
            dma,
            dma,
            pltpu.SemaphoreType.REGULAR,
            pltpu.SemaphoreType.REGULAR((2,)),
            pltpu.SemaphoreType.REGULAR,
        ],
        compiler_params=pltpu.CompilerParams(collective_id=0, has_side_effects=True, vmem_limit_bytes=12 << 20),
    )(*[pltpu.with_memory_space_constraint(v, pltpu.HBM) for v in big])
    resident = pl.BlockSpec(memory_space=pltpu.VMEM)
    moved, slip = pl.pallas_call(
        write_out,
        out_shape=(
            jax.ShapeDtypeStruct(velocity.shape, f32),
            jax.ShapeDtypeStruct((per, cz), f32),
        ),
        in_specs=[resident] * 4,
        out_specs=(anywhere, anywhere),
        scratch_shapes=[pltpu.VMEM((per, cz), f32), dma((2,))],
        compiler_params=pltpu.CompilerParams(vmem_limit_bytes=4 << 20),
    )(*held)
    return moved, slip.T


def solution(mesh):
    n, nd = mesh.shape["strike"], mesh.shape["depth"]
    return jax.shard_map(
        functools.partial(per_device, n, nd),
        mesh=mesh,
        in_specs=(
            P(None, "strike", "depth", None),
            P(None, "strike", "depth", None),
            P("strike", "depth", None),
            P(),
            P(None, "depth", "strike"),
        ),
        out_specs=(P(None, "strike", "depth", None), P("depth", "strike")),
        check_vma=False,
    )
```
